32 devices in a mesh: groups: 2 (over x), tensor: 16 (over z, y, core).
Axes of the slice: x: 2, y: 2, z: 4, core: 2. Of those that a mesh axis runs over, the one named last changes fastest.
Arguments:
- residual_in: bfloat16 [1024, 6144], P('groups', 'tensor'), parts along dimension 0
- norm_gain: bfloat16 [6144], P('tensor'), may hold values from 0.099609375 to 1.8984375
- final_gain: bfloat16 [6144], P('tensor'), may hold values from 0.099609375 to 1.8984375
- expert_ids: int32 [1024, 2], P('groups'), parts along dimension 0, may hold values from 0 to 3, all different within a row; in each aligned block of 512 rows (0 to 511, 512 to 1023, ...) at most 384 rows name the same one
- gate_values: float32 [1024, 2], P('groups'), parts along dimension 0, may hold values from 0.2 to 1
- w_gate: bfloat16 [6144, 32768], P(None, 'tensor'), may hold values from -0.078125 to 0.078125
- w_up: bfloat16 [6144, 32768], P(None, 'tensor'), may hold values from -0.078125 to 0.078125
- w_down: bfloat16 [32768, 6144], P('tensor')
- lm_head: bfloat16 [6144, 32768], P(None, 'tensor')
- target_ids: int32 [1024], P('groups'), parts along dimension 0, may hold values from 0 to 32767
- lengths: int32 [16], P('groups'), parts along dimension 0, may hold values from 1 to 64
Outputs:
- masked_logprob: float32 [1024], P(('groups', 'tensor')), parts along dimension 0
The draws below stay inside these ranges and needn't reach their ends.
There are 2 independent parts, one for each index of `groups`. The reference program is written for one: setup_inputs(seed, part) draws one part's arguments, and reference() takes and returns one part's arrays. A program takes and returns all parts, laid end to end along the dimension named above; an argument that names none is the same for every part. Nothing has to cross between parts.
Inputs may be any that keep to these rules, and one draw needn't show every extreme that they name: `expert_ids`: no expert is named by more than 384 tokens of a frontier batch, a bound that some block reaches.
All inputs are finite; a program needn't handle non-finite values.
Results may differ from the reference program's by a relative error of at most 0.0055.
Values may be sent and summed in bfloat16 or wider, within the bound.
No kernel may reach another device: no remote copies, remote signals or barrier semaphores. Data moves between devices by JAX's collectives and lax.ppermute only.
A program may use at most 192 MiB of HBM per device.

```python
import math
import jax
import jax.numpy as jnp
import numpy as np
from jax import lax

D = 6144
EXPERTS = 4
EXP_FF = 8192
VOCAB = 32768
TOP = 2
SEQ = 64
TOKENS = 512
CANDS = 8
CAP = 384


def draw_residual_in(key, part):
    column = jnp.arange(D, dtype=jnp.float32)
    rising = 1.0 + 2.0 * column / D
    values = jax.random.normal(key, (TOKENS, D), jnp.float32) * rising[None, :] * 0.3
    return values.astype(jnp.bfloat16)


def draw_w_down(key, part):
    heavy_count = max(4, D // 384)
    heavy_scale = (D / heavy_count) ** 0.5
    order = jax.random.permutation(jax.random.fold_in(key, 3), D)
    marks = jnp.zeros((D,), jnp.int32).at[order[:heavy_count]].set(1)
    light = jnp.exp(jax.random.uniform(jax.random.fold_in(key, 4), (D,), jnp.float32, -0.7, 0.4))
    total_rows = EXPERTS * EXP_FF
    column_scale = jnp.where(marks == 1, heavy_scale, light)
    base = jax.random.normal(key, (total_rows, D), jnp.float32)
    values = base * column_scale[None, :] * EXP_FF ** (-0.5)
    return values.astype(jnp.bfloat16)


def draw_lm_head(key, part):
    position = jnp.arange(VOCAB, dtype=jnp.float32) / VOCAB
    rough = jnp.exp(jax.random.uniform(jax.random.fold_in(key, 7), (1, VOCAB), jnp.float32, -0.35, 0.35))
    profile = 3.0 * jnp.exp(-2.302585 * position)
    base = jax.random.normal(key, (D, VOCAB), jnp.float32) * D ** (-0.5) * profile[None, :] * rough
    return base.astype(jnp.bfloat16)


def with_ends(array, stream_key, smallest, top_value):
    longest = array.shape.index(max(array.shape))
    spots = []
    for shift in (0, 1):
        where = [jax.random.randint(jax.random.fold_in(stream_key, axis), (), 0, length) for axis, length in enumerate(array.shape)]
        where[longest] = (where[longest] + shift) % array.shape[longest]
        spots.append(tuple(where))
    return array.at[spots[0]].set(smallest).at[spots[1]].set(top_value)


def block_levels(stream_key, dims, shards, low, top_value):
    level, own = 1.0, jax.random.fold_in(stream_key, 6)
    for axis_at, shards_of in shards:
        heights = jnp.exp(jax.random.uniform(jax.random.fold_in(own, axis_at), (shards_of,), jnp.float32, low / len(shards), top_value / len(shards)))
        level = level * jnp.repeat(heights, dims[axis_at] // shards_of).reshape([-1 if axis == axis_at else 1 for axis in range(len(dims))])
    return level


def rank_bounds(number_of, lean):
    loads = [(1 << 20) // math.isqrt(grade ** lean) + 1 for grade in range(1, number_of + 1)]
    deviation = 1 + sum(loads) // (1 << 30)
    return np.cumsum(np.array([max(1, weight // deviation) for weight in loads]))


def skewed_ids(rng, shape, number_of, slope):
    table = rank_bounds(number_of, slope)
    ticket = jax.random.randint(jax.random.fold_in(rng, 1), shape, 0, int(table[number_of - 1]))
    grade = jnp.searchsorted(jnp.asarray(table, jnp.int32), ticket, side="right")
    return jax.random.permutation(jax.random.fold_in(rng, 2), number_of)[grade].astype(jnp.int32)


def routed_block(stream_key, own, number, rows, amount, top, limit, skew):
    sequence = jax.random.permutation(stream_key, amount)
    crowded, usual = portions_of(amount, rows * top, limit, skew, True), portions_of(amount, rows * top, limit, skew, False)
    places = jnp.arange(amount)

    def named(sizes, offset_by):
        used = int((sizes > 0).sum())
        fixed = max(1, used // 4)
        shifted = fixed + (places - fixed + offset_by * (used - fixed)) % max(1, amount - fixed)
        return jnp.zeros((amount,), jnp.int32).at[sequence[jnp.where(places < fixed, places, shifted)]].set(jnp.asarray(sizes, jnp.int32))

    sizes = jnp.where(number % 4 == 0, named(crowded, number // 4), named(usual, number - number // 4 - 1))
    mixed = jax.random.permutation(jax.random.fold_in(own, 3), amount)
    donor, receiver = mixed[0:amount // 2 * 2:2], mixed[1:amount // 2 * 2:2]
    room = jnp.minimum(sizes[donor] - 1, limit - sizes[receiver]) // 2
    room = jnp.where((donor == sequence[0]) | (receiver == sequence[0]) | (sizes[receiver] == 0), 0, jnp.maximum(room, 0))
    shifted = jax.random.randint(jax.random.fold_in(own, 4), (amount // 2,), 0, 1 << 20) % (room + 1)
    sizes = sizes.at[donor].add(-shifted).at[receiver].add(shifted)
    items = jnp.searchsorted(jnp.cumsum(sizes), jnp.arange(rows * top), side="right").astype(jnp.int32)
    listing = items.reshape(top, rows).T
    listing = listing[jax.random.permutation(jax.random.fold_in(own, 1), rows)]
    offset_by = jax.random.randint(jax.random.fold_in(own, 2), (rows, 1), 0, top)
    return jnp.take_along_axis(listing, (jnp.arange(top)[None, :] + offset_by) % top, axis=1)


def portions_of(count, total, most, lean, full):
    loads = [(1 << 20) // math.isqrt(standing ** lean) + 1 for standing in range(1, count + 1)]
    largest = most if full else min(most, max(-(-total // count), total * loads[0] // sum(loads)))
    least = 1 if total - largest >= count - 1 else 0
    counts, spare = [largest] + [least] * (count - 1), total - largest - least * (count - 1)
    while spare > 0:
        movable = [i for i in range(1, count) if counts[i] < largest] or [i for i in range(1, count) if counts[i] < most]
        mass, budget = sum([loads[i] for i in movable]), spare
        for i in movable:
            extra = min(most - counts[i], max(1, budget * loads[i] // mass), spare)
            counts[i] = counts[i] + extra
            spare = spare - extra
    return np.array(counts)


def normal_values(stream_key, shape, scale, most, split=(), kind=jnp.bfloat16):
    level = block_levels(stream_key, shape, split, -0.22, 0.18) if split else 1.0
    entries = jax.random.normal(stream_key, shape, jnp.float32) * scale * level
    return jnp.minimum(jnp.maximum(entries, -most), most).astype(kind)


def setup_inputs(seed: int = 0, part: int = 0) -> dict:
    key_of = jax.random.split(jax.random.key(seed), 12)
    part_splits = jax.random.split(jax.random.fold_in(key_of[11], part), 12)
    residual_in = draw_residual_in(jax.random.fold_in(jax.random.fold_in(key_of[11], part), 71), part)
    norm_gain = jnp.clip(1.0 + 0.18 * jax.random.normal(key_of[1], (D,), jnp.float32), 0.099609375, 1.8984375).astype(jnp.bfloat16)
    final_gain = jnp.clip(1.0 + 0.18 * jax.random.normal(key_of[2], (D,), jnp.float32), 0.099609375, 1.8984375).astype(jnp.bfloat16)
    expert_ids_keys = jax.random.split(jax.random.fold_in(part_splits[3], 1), TOKENS // TOKENS)
    expert_ids_turns = jax.random.permutation(jax.random.fold_in(part_splits[3], 3), TOKENS // TOKENS)
    expert_ids = jax.vmap(lambda own, number: routed_block(jax.random.fold_in(part_splits[3], 2), own, number, TOKENS, EXPERTS, TOP, CAP, 2))(expert_ids_keys, expert_ids_turns).reshape((TOKENS, TOP))
    gate_values = jnp.clip(jax.random.uniform(part_splits[4], (TOKENS, TOP), jnp.float32, 0.2, 1.0), 0.2, 1.0)
    w_gate = normal_values(key_of[5], (D, EXPERTS * EXP_FF), D ** -0.5, 0.078125, ((1, 16),))
    w_up = normal_values(key_of[6], (D, EXPERTS * EXP_FF), D ** -0.5, 0.078125, ((1, 16),))
    w_down = draw_w_down(jax.random.fold_in(key_of[11], 71), part)
    lm_head = draw_lm_head(jax.random.fold_in(key_of[11], 71), part)
    target_ids = with_ends(skewed_ids(part_splits[9], (TOKENS,), VOCAB, 2), jax.random.fold_in(part_splits[9], 3), 0, VOCAB - 1).astype(jnp.int32)
    lengths = with_ends(jax.random.randint(part_splits[10], (CANDS,), 1, SEQ + 1), jax.random.fold_in(part_splits[10], 1), 1, SEQ).astype(jnp.int32)
    return {"residual_in": residual_in, "norm_gain": norm_gain, "final_gain": final_gain, "expert_ids": expert_ids, "gate_values": gate_values, "w_gate": w_gate, "w_up": w_up, "w_down": w_down, "lm_head": lm_head, "target_ids": target_ids, "lengths": lengths}


epsilon = 1e-05

def slots_of(expert_ids):
    flat_ids = expert_ids.reshape(-1)
    one_hot = (flat_ids[:, None] == jnp.arange(EXPERTS, dtype=jnp.int32)[None, :]).astype(jnp.int32)
    earlier = jnp.cumsum(one_hot, axis=0) - one_hot
    return lax.optimization_barrier(jnp.sum(earlier * one_hot, axis=1)).astype(jnp.int32).reshape(expert_ids.shape)

def rms_norm(values, gain_vec):
    mean_square = lax.optimization_barrier(jnp.mean(values * values, axis=1, keepdims=True))
    return (values / jnp.sqrt(mean_square + epsilon) * gain_vec.astype(jnp.float32)).astype(jnp.bfloat16)

def reference(residual_in, norm_gain, final_gain, expert_ids, gate_values, w_gate, w_up, w_down, lm_head, target_ids, lengths):
    stream = residual_in.astype(jnp.float32)
    normed = rms_norm(stream, norm_gain)
    slot_index = slots_of(expert_ids)
    buffer = jnp.zeros((EXPERTS, CAP, D), jnp.bfloat16)
    buffer = buffer.at[expert_ids, slot_index].set(jnp.broadcast_to(normed[:, None, :], (TOKENS, TOP, D)))
    outputs = []
    for expert in range(EXPERTS):
        columns = slice(expert * EXP_FF, (expert + 1) * EXP_FF)
        gate_out = jnp.dot(buffer[expert], w_gate[:, columns], preferred_element_type=jnp.float32)
        up_out = jnp.dot(buffer[expert], w_up[:, columns], preferred_element_type=jnp.float32)
        hidden = (jax.nn.silu(gate_out) * up_out).astype(jnp.bfloat16)
        outputs.append(jnp.dot(hidden, w_down[columns, :], preferred_element_type=jnp.float32))
    expert_table = jnp.stack(outputs)
    picked_rows = expert_table[expert_ids, slot_index]
    moe_out = lax.optimization_barrier(jnp.sum(gate_values[:, :, None] * picked_rows, axis=1))
    mixture = stream + moe_out
    normed_out = rms_norm(mixture, final_gain)
    logits = jnp.dot(normed_out, lm_head, preferred_element_type=jnp.float32)
    row_max = lax.optimization_barrier(jnp.max(logits, axis=1))
    row_total = lax.optimization_barrier(jnp.sum(jnp.exp(logits - row_max[:, None]), axis=1))
    picked = jnp.take_along_axis(logits, target_ids[:, None].astype(jnp.int32), axis=1)[:, 0]
    logprob = picked - row_max - jnp.log(row_total)
    position = jnp.arange(TOKENS, dtype=jnp.int32)
    in_length = position % SEQ < lengths[position // SEQ]
    return jnp.where(in_length, logprob, jnp.zeros_like(logprob)).astype(jnp.float32)
```

```python
import jax
import jax.numpy as jnp
from jax import lax
from jax.sharding import PartitionSpec as P

D = 6144
EXPERTS = 4
EXP_FF = 8192
TOP = 2
SEQ = 64
CAP = 384


epsilon = 1e-05


def combined_all(array, axis, combine):
    everything = jax.tree.map(lambda part: lax.all_gather(part, axis), array)
    leading = jax.tree.map(lambda part: part[0], everything)

    def hop(k, so_far):
        return combine(so_far, jax.tree.map(lambda part: part[k], everything))

    return lax.fori_loop(1, lax.axis_size(axis), hop, leading)


def slots_of(expert_ids):
    flat_ids = expert_ids.reshape(-1)
    pairs = jnp.arange(flat_ids.shape[0], dtype=jnp.int32)
    before = (pairs[None, :] < pairs[:, None]) & (flat_ids[None, :] == flat_ids[:, None])
    return jnp.sum(before.astype(jnp.int32), axis=1).reshape(expert_ids.shape)


def slot_tokens(expert_ids, slot_index):
    slot_code = (expert_ids * CAP + slot_index).reshape(-1)
    owner = jnp.arange(slot_code.shape[0], dtype=jnp.int32) // TOP
    wanted = jnp.arange(EXPERTS * CAP, dtype=jnp.int32)
    matches = slot_code[None, :] == wanted[:, None]
    return jnp.sum(jnp.where(matches, owner[None, :] + 1, 0), axis=1) - 1


def normalize(values, squares_total, gain_vec):
    return (
        values / jnp.sqrt(squares_total[:, None] / D + epsilon) * gain_vec.astype(jnp.float32)
    ).astype(jnp.bfloat16)


def body(
    residual_in,
    norm_gain,
    final_gain,
    expert_ids,
    gate_values,
    w_gate,
    w_up,
    w_down,
    lm_head,
    target_ids,
    lengths,
):
    tokens, feature_cols = residual_in.shape
    hidden_dev = w_gate.shape[1]
    per_expert = EXP_FF // hidden_dev
    expert_now = lax.axis_index("tensor") // per_expert
    stream = residual_in.astype(jnp.float32)
    in_total = lax.psum(jnp.sum(stream * stream, axis=1), "tensor")
    normed = normalize(stream, in_total, norm_gain)
    slot_index = slots_of(expert_ids)
    token_of = slot_tokens(expert_ids, slot_index)
    zero_bf = jnp.zeros((), jnp.bfloat16)
    own_slots = lax.dynamic_slice_in_dim(token_of, expert_now * CAP, CAP)
    occupied = own_slots >= 0
    safe_index = jnp.maximum(own_slots, 0)
    slot_rows = jnp.where(
        occupied[:, None], lax.all_gather(normed, "tensor", axis=1, tiled=True)[safe_index], zero_bf
    )
    gate_out = jnp.dot(slot_rows, w_gate, preferred_element_type=jnp.float32)
    up_out = jnp.dot(slot_rows, w_up, preferred_element_type=jnp.float32)
    hidden = (jax.nn.silu(gate_out) * up_out).astype(jnp.bfloat16)
    partial_value = jnp.dot(hidden, w_down, preferred_element_type=jnp.float32)
    weight_own = jnp.where(expert_ids == expert_now, gate_values, jnp.zeros_like(gate_values))
    weighted = (
        weight_own[:, 0:1] * partial_value[slot_index[:, 0]]
        + weight_own[:, 1:2] * partial_value[slot_index[:, 1]]
    )
    moe_cols = lax.psum_scatter(weighted, "tensor", scatter_dimension=1, tiled=True)
    mixture = stream + moe_cols
    out_total = lax.psum(jnp.sum(mixture * mixture, axis=1), "tensor")
    normed_out = normalize(mixture, out_total, final_gain)
    vocab_dev = lm_head.shape[1]
    logits = jnp.dot(
        lax.all_gather(normed_out, "tensor", axis=1, tiled=True),
        lm_head,
        preferred_element_type=jnp.float32,
    )
    row_max = jnp.max(logits, axis=1)
    row_total = jnp.sum(jnp.exp(logits - row_max[:, None]), axis=1)
    local_ids = target_ids - lax.axis_index("tensor") * vocab_dev
    vocab_cols = jnp.arange(vocab_dev, dtype=jnp.int32)
    picked = jnp.sum(jnp.where(vocab_cols[None, :] == local_ids[:, None], logits, 0.0), axis=1)

    def joined(earlier, later):
        merged_max = jnp.maximum(earlier[0], later[0])
        merged_total = earlier[1] * jnp.exp(earlier[0] - merged_max) + later[1] * jnp.exp(
            later[0] - merged_max
        )
        return (merged_max, merged_total, earlier[2] + later[2])

    merged_max, merged_total, target_logit = combined_all(
        (row_max, row_total, picked), "tensor", joined
    )
    logprob = target_logit - merged_max - jnp.log(merged_total)
    rows_dev = tokens // lax.axis_size("tensor")
    first_row = lax.axis_index("tensor") * rows_dev
    own_rows = lax.dynamic_slice_in_dim(logprob, first_row, rows_dev)
    position = first_row + jnp.arange(rows_dev, dtype=jnp.int32)
    in_length = position % SEQ < lengths[position // SEQ]
    return jnp.where(in_length, own_rows, jnp.zeros_like(own_rows)).astype(jnp.float32)


def solution(mesh):
    return jax.shard_map(
        body,
        mesh=mesh,
        in_specs=(
            P("groups", "tensor"),
            P("tensor"),
            P("tensor"),
            P("groups", None),
            P("groups", None),
            P(None, "tensor"),
            P(None, "tensor"),
            P("tensor", None),
            P(None, "tensor"),
            P("groups"),
            P("groups"),
        ),
        out_specs=P(("groups", "tensor")),
        check_vma=False,
    )
```

```python
import functools
import jax
import jax.numpy as jnp
from jax import lax
from jax.experimental import pallas as pl
from jax.experimental.pallas import tpu as pltpu
from jax.sharding import PartitionSpec as P

D = 6144
EXPERTS = 4
EXP_FF = 8192
TOP = 2
SEQ = 64
CAP = 384


epsilon = 1e-05


def combined_all(array, axis, combine):
    everything = jax.tree.map(lambda part: lax.all_gather(part, axis), array)
    leading = jax.tree.map(lambda part: part[0], everything)

    def hop(k, so_far):
        return combine(so_far, jax.tree.map(lambda part: part[k], everything))

    return lax.fori_loop(1, lax.axis_size(axis), hop, leading)


def slots_of(expert_ids):
    flat_ids = expert_ids.reshape(-1)
    pairs = jnp.arange(flat_ids.shape[0], dtype=jnp.int32)
    before = (pairs[None, :] < pairs[:, None]) & (flat_ids[None, :] == flat_ids[:, None])
    return jnp.sum(before.astype(jnp.int32), axis=1).reshape(expert_ids.shape)


def slot_tokens(expert_ids, slot_index):
    slot_code = (expert_ids * CAP + slot_index).reshape(-1)
    owner = jnp.arange(slot_code.shape[0], dtype=jnp.int32) // TOP
    wanted = jnp.arange(EXPERTS * CAP, dtype=jnp.int32)
    matches = slot_code[None, :] == wanted[:, None]
    return jnp.sum(jnp.where(matches, owner[None, :] + 1, 0), axis=1) - 1


def normalize(values, squares_total, gain_vec):
    return (
        values / jnp.sqrt(squares_total[:, None] / D + epsilon) * gain_vec.astype(jnp.float32)
    ).astype(jnp.bfloat16)


def plain_body(
    residual_in,
    norm_gain,
    final_gain,
    expert_ids,
    gate_values,
    w_gate,
    w_up,
    w_down,
    lm_head,
    target_ids,
    lengths,
):
    tokens, feature_cols = residual_in.shape
    hidden_dev = w_gate.shape[1]
    per_expert = EXP_FF // hidden_dev
    expert_now = lax.axis_index("tensor") // per_expert
    stream = residual_in.astype(jnp.float32)
    in_total = lax.psum(jnp.sum(stream * stream, axis=1), "tensor")
    normed = normalize(stream, in_total, norm_gain)
    slot_index = slots_of(expert_ids)
    token_of = slot_tokens(expert_ids, slot_index)
    zero_bf = jnp.zeros((), jnp.bfloat16)
    own_slots = lax.dynamic_slice_in_dim(token_of, expert_now * CAP, CAP)
    occupied = own_slots >= 0
    safe_index = jnp.maximum(own_slots, 0)
    slot_rows = jnp.where(
        occupied[:, None], lax.all_gather(normed, "tensor", axis=1, tiled=True)[safe_index], zero_bf
    )
    gate_out = jnp.dot(slot_rows, w_gate, preferred_element_type=jnp.float32)
    up_out = jnp.dot(slot_rows, w_up, preferred_element_type=jnp.float32)
    hidden = (jax.nn.silu(gate_out) * up_out).astype(jnp.bfloat16)
    partial_value = jnp.dot(hidden, w_down, preferred_element_type=jnp.float32)
    weight_own = jnp.where(expert_ids == expert_now, gate_values, jnp.zeros_like(gate_values))
    weighted = (
        weight_own[:, 0:1] * partial_value[slot_index[:, 0]]
        + weight_own[:, 1:2] * partial_value[slot_index[:, 1]]
    )
    moe_cols = lax.psum_scatter(weighted, "tensor", scatter_dimension=1, tiled=True)
    mixture = stream + moe_cols
    out_total = lax.psum(jnp.sum(mixture * mixture, axis=1), "tensor")
    normed_out = normalize(mixture, out_total, final_gain)
    vocab_dev = lm_head.shape[1]
    logits = jnp.dot(
        lax.all_gather(normed_out, "tensor", axis=1, tiled=True),
        lm_head,
        preferred_element_type=jnp.float32,
    )
    row_max = jnp.max(logits, axis=1)
    row_total = jnp.sum(jnp.exp(logits - row_max[:, None]), axis=1)
    local_ids = target_ids - lax.axis_index("tensor") * vocab_dev
    vocab_cols = jnp.arange(vocab_dev, dtype=jnp.int32)
    picked = jnp.sum(jnp.where(vocab_cols[None, :] == local_ids[:, None], logits, 0.0), axis=1)

    def joined(earlier, later):
        merged_max = jnp.maximum(earlier[0], later[0])
        merged_total = earlier[1] * jnp.exp(earlier[0] - merged_max) + later[1] * jnp.exp(
            later[0] - merged_max
        )
        return (merged_max, merged_total, earlier[2] + later[2])

    merged_max, merged_total, target_logit = combined_all(
        (row_max, row_total, picked), "tensor", joined
    )
    logprob = target_logit - merged_max - jnp.log(merged_total)
    rows_dev = tokens // lax.axis_size("tensor")
    first_row = lax.axis_index("tensor") * rows_dev
    own_rows = lax.dynamic_slice_in_dim(logprob, first_row, rows_dev)
    position = first_row + jnp.arange(rows_dev, dtype=jnp.int32)
    in_length = position % SEQ < lengths[position // SEQ]
    return jnp.where(in_length, own_rows, jnp.zeros_like(own_rows)).astype(jnp.float32)

VMEM_BYTES = 56 * 1024 * 1024
ORDER = (0, 1, 3, 2)


def send(array, pairs):
    return lax.ppermute(array, "tensor", pairs)


def core_pairs():
    return [(i, i ^ 1) for i in range(16)]


def row_pairs():
    return [(i, i ^ 2) for i in range(16)]


def plane_pairs(k):
    return [(i, ((i >> 2) + k) % 4 * 4 + (i & 3)) for i in range(16)]


def summed_all(array):
    array = array + send(array, core_pairs())
    array = array + send(array, row_pairs())
    others = [send(array, plane_pairs(k)) for k in (1, 2, 3)]
    return array + others[0] + (others[1] + others[2])


def one_hot(column, count):
    return column[None, :] == jnp.arange(count, dtype=jnp.int32)[:, None]


def params(steps):
    return pltpu.CompilerParams(
        dimension_semantics=("arbitrary",) * steps, vmem_limit_bytes=VMEM_BYTES
    )


def cost(rows, inner, cols, other_bytes):
    return pl.CostEstimate(
        flops=2 * rows * inner * cols,
        transcendentals=0,
        bytes_accessed=2 * inner * cols + other_bytes,
    )


def dispatch_kernel(slot_ref, x_ref, gain_ref, s0, s1, s2, s3, xc_ref):
    x = x_ref[...]
    scaled = (x.astype(jnp.float32) * gain_ref[...].astype(jnp.float32)).astype(jnp.bfloat16)
    tokens = x.shape[0]
    for k, out in enumerate((s0, s1, s2, s3)):
        rows = out.shape[0]
        spots = lax.broadcasted_iota(jnp.int32, (rows, tokens), 0)
        chosen = jnp.where(slot_ref[k : k + 1, :] == spots, 1.0, 0.0).astype(jnp.bfloat16)
        out[...] = jnp.dot(chosen, scaled, preferred_element_type=jnp.float32).astype(jnp.bfloat16)
    rows = xc_ref.shape[0]
    spots = lax.broadcasted_iota(jnp.int32, (rows, tokens), 0)
    chosen = jnp.where(slot_ref[4:5, :] == spots, 1.0, 0.0).astype(jnp.bfloat16)
    xc_ref[...] = jnp.dot(chosen, x, preferred_element_type=jnp.float32).astype(jnp.bfloat16)


def dispatch(slot_rows, x, gain, slots, live_rows):
    cols = x.shape[1]
    block = jax.ShapeDtypeStruct((slots, cols), jnp.bfloat16)
    return pl.pallas_call(
        dispatch_kernel,
        out_shape=[block] * 4 + [jax.ShapeDtypeStruct((live_rows, cols), jnp.bfloat16)],
        compiler_params=pltpu.CompilerParams(vmem_limit_bytes=VMEM_BYTES),
    )(slot_rows, x, gain)


def place(where_ref, blocks, wide_ref):
    cols = blocks[0].shape[1]
    for b, block in enumerate(blocks):
        at = pl.multiple_of(where_ref[1 + b] * cols, 128)
        wide_ref[:, pl.ds(at, cols)] = block[...]


def hidden_kernel(first, last, where_ref, *refs):
    blocks, (wg, wu), refs = refs[:4], refs[4:6], refs[6:]
    if not first:
        g_in, u_in, refs = refs[0], refs[1], refs[2:]
    if last:
        inv, h_out, wide = refs
    else:
        g_out, u_out, wide = refs

    @pl.when(pl.program_id(0) == 0)
    def _():
        place(where_ref, blocks, wide)

    g = jnp.dot(wide[...], wg[...], preferred_element_type=jnp.float32)
    u = jnp.dot(wide[...], wu[...], preferred_element_type=jnp.float32)
    if not first:
        g = g + g_in[...]
        u = u + u_in[...]
    if last:
        g = g * inv[...]
        u = u * inv[...]
        h_out[...] = (g / (1.0 + jnp.exp(-g)) * u).astype(jnp.bfloat16)
    else:
        g_out[...] = g
        u_out[...] = u


def hidden_part(where, blocks, w_gate, w_up, sums, inv):
    rows, cols = blocks[0].shape
    width = w_gate.shape[1]
    tile = 512
    first, last = sums is None, inv is not None
    whole = pl.BlockSpec((rows, cols), lambda n, w: (0, 0))
    weight = pl.BlockSpec((4 * cols, tile), lambda n, w: (w[0], n))
    out_tile = pl.BlockSpec((rows, tile), lambda n, w: (0, n))
    ins, specs = [where, *blocks, w_gate, w_up], [whole] * 4 + [weight] * 2
    aliases = {}
    if not first:
        ins += list(sums)
        specs += [out_tile] * 2
        if not last:
            aliases = {7: 0, 8: 1}
    if last:
        ins.append(inv)
        specs.append(pl.BlockSpec((rows, 1), lambda n, w: (0, 0)))
        outs, out_specs = jax.ShapeDtypeStruct((rows, width), jnp.bfloat16), out_tile
    else:
        outs = [jax.ShapeDtypeStruct((rows, width), jnp.float32)] * 2
        out_specs = [out_tile] * 2
    return pl.pallas_call(
        functools.partial(hidden_kernel, first, last),
        out_shape=outs,
        grid_spec=pltpu.PrefetchScalarGridSpec(
            num_scalar_prefetch=1,
            grid=(width // tile,),
            in_specs=specs,
            out_specs=out_specs,
            scratch_shapes=[pltpu.VMEM((rows, 4 * cols), jnp.bfloat16)],
        ),
        input_output_aliases=aliases,
        compiler_params=params(1),
        cost_estimate=cost(rows, 4 * cols, 2 * width, 16 * rows * width),
    )(*ins)


def down_kernel(where_ref, h_ref, w_ref, gate_ref, o_own, o_row, o_core, o_far, total):
    @pl.when(pl.program_id(0) == 0)
    def _():
        total[...] = jnp.zeros_like(total)

    total[...] += jnp.dot(h_ref[...], w_ref[...], preferred_element_type=jnp.float32)

    @pl.when(pl.program_id(0) == pl.num_programs(0) - 1)
    def _():
        cols = o_own.shape[1]
        for b, out in enumerate((o_own, o_row, o_core, o_far)):
            at = pl.multiple_of(where_ref[1 + b] * cols, 128)
            out[...] = (total[:, pl.ds(at, cols)] * gate_ref[...]).astype(out.dtype)


def down_part(where, hidden, w_down, gate_slot, cols):
    rows, inner = hidden.shape
    depth = 512
    block = pl.BlockSpec((rows, cols), lambda j, w: (0, 0))
    kinds = (jnp.float32, jnp.float32, jnp.bfloat16, jnp.bfloat16)
    return pl.pallas_call(
        down_kernel,
        out_shape=[jax.ShapeDtypeStruct((rows, cols), kind) for kind in kinds],
        grid_spec=pltpu.PrefetchScalarGridSpec(
            num_scalar_prefetch=1,
            grid=(inner // depth,),
            in_specs=[
                pl.BlockSpec((rows, depth), lambda j, w: (0, j)),
                pl.BlockSpec((depth, 4 * cols), lambda j, w: (j, w[0])),
                pl.BlockSpec((rows, 1), lambda j, w: (0, 0)),
            ],
            out_specs=[block] * 4,
            scratch_shapes=[pltpu.VMEM((rows, 4 * cols), jnp.float32)],
        ),
        compiler_params=params(1),
        cost_estimate=cost(rows, inner, 4 * cols, 24 * rows * cols),
    )(where, hidden, w_down, gate_slot)


def mix_kernel(slot_ref, x_ref, gain_ref, e0, e1, e2, e3, out_ref, squares_ref):
    rows = x_ref.shape[0]
    mixture = x_ref[...].astype(jnp.float32)
    moe = jnp.zeros_like(mixture)
    for j, part in enumerate((e0, e1, e2, e3)):
        slots = part.shape[0]
        spots = lax.broadcasted_iota(jnp.int32, (rows, slots), 1)
        chosen = jnp.where(slot_ref[:, j : j + 1] == spots, 1.0, 0.0).astype(jnp.bfloat16)
        moe = moe + jnp.dot(chosen, part[...], preferred_element_type=jnp.float32)
    mixture = mixture + moe
    out_ref[...] = (mixture * gain_ref[...].astype(jnp.float32)).astype(jnp.bfloat16)
    squares_ref[...] = jnp.sum(mixture * mixture, axis=1, keepdims=True)


def mix(slot_cols, x, gain, parts):
    rows, cols = x.shape
    return pl.pallas_call(
        mix_kernel,
        out_shape=[
            jax.ShapeDtypeStruct((rows, cols), jnp.bfloat16),
            jax.ShapeDtypeStruct((rows, 1), jnp.float32),
        ],
        compiler_params=pltpu.CompilerParams(vmem_limit_bytes=VMEM_BYTES),
    )(slot_cols, x, gain, *parts)


def vocab_kernel(first, last, where_ref, *refs):
    blocks, w_ref, refs = refs[:4], refs[4], refs[5:]
    if not first:
        sum_in, refs = refs[0], refs[1:]
    if last:
        inv, local_ids, out, wide, top, total, picked = refs
    else:
        out, wide = refs
    n = pl.program_id(0)

    @pl.when(n == 0)
    def _():
        place(where_ref, blocks, wide)

    value = jnp.dot(wide[...], w_ref[...], preferred_element_type=jnp.float32)
    if not first:
        value = value + sum_in[...]
    if not last:
        out[...] = value
        return
    logits = value * inv[...]
    rows, tile = logits.shape
    column = n * tile + lax.broadcasted_iota(jnp.int32, (rows, tile), 1)
    tile_pick = jnp.sum(jnp.where(column == local_ids[...], logits, 0.0), axis=1, keepdims=True)
    tile_top = jnp.max(logits, axis=1, keepdims=True)

    @pl.when(n == 0)
    def _():
        top[...] = tile_top
        total[...] = jnp.sum(jnp.exp(logits - tile_top), axis=1, keepdims=True)
        picked[...] = tile_pick

    @pl.when(n > 0)
    def _():
        new_top = jnp.maximum(top[...], tile_top)
        total[...] = total[...] * jnp.exp(top[...] - new_top) + jnp.sum(
            jnp.exp(logits - new_top), axis=1, keepdims=True
        )
        top[...] = new_top
        picked[...] = picked[...] + tile_pick

    @pl.when(n == pl.num_programs(0) - 1)
    def _():
        lane = lax.broadcasted_iota(jnp.int32, out.shape, 1)
        out[...] = jnp.where(lane == 0, top[...], jnp.where(lane == 1, total[...], picked[...]))


def vocab_part(where, blocks, lm_head, sums, inv, local_ids):
    rows, cols = blocks[0].shape
    width = lm_head.shape[1]
    tile = 512
    first, last = sums is None, inv is not None
    whole = pl.BlockSpec((rows, cols), lambda n, w: (0, 0))
    out_tile = pl.BlockSpec((rows, tile), lambda n, w: (0, n))
    ins = [where, *blocks, lm_head]
    specs = [whole] * 4 + [pl.BlockSpec((4 * cols, tile), lambda n, w: (w[0], n))]
    aliases = {}
    if not first:
        ins.append(sums)
        specs.append(out_tile)
        if not last:
            aliases = {6: 0}
    scratch = [pltpu.VMEM((rows, 4 * cols), jnp.bfloat16)]
    if last:
        ins += [inv, local_ids]
        specs += [pl.BlockSpec((rows, 1), lambda n, w: (0, 0))] * 2
        outs = jax.ShapeDtypeStruct((rows, 128), jnp.float32)
        out_specs = pl.BlockSpec((rows, 128), lambda n, w: (0, 0))
        scratch += [pltpu.VMEM((rows, 1), jnp.float32)] * 3
    else:
        outs, out_specs = jax.ShapeDtypeStruct((rows, width), jnp.float32), out_tile
    return pl.pallas_call(
        functools.partial(vocab_kernel, first, last),
        out_shape=outs,
        grid_spec=pltpu.PrefetchScalarGridSpec(
            num_scalar_prefetch=1,
            grid=(width // tile,),
            in_specs=specs,
            out_specs=out_specs,
            scratch_shapes=scratch,
        ),
        input_output_aliases=aliases,
        compiler_params=params(1),
        cost_estimate=cost(rows, 4 * cols, width, 8 * rows * width),
    )(*ins)


def spread(by_offset):
    arrived = {0: by_offset[0]}
    arrived[1] = send(by_offset[1], plane_pairs(1))
    arrived[3] = send(by_offset[3], plane_pairs(3))
    later, _, _ = lax.optimization_barrier((by_offset[2], arrived[1], arrived[3]))
    arrived[2] = send(later, plane_pairs(2))
    chunks = {}
    for k in ORDER:
        own = arrived[k]
        row = send(own, row_pairs())
        chunks[k] = (own, row, send(own, core_pairs()), send(row, core_pairs()))
    return chunks


def fast_body(
    residual_in,
    norm_gain,
    final_gain,
    expert_ids,
    gate_values,
    w_gate,
    w_up,
    w_down,
    lm_head,
    target_ids,
    lengths,
    live_rows,
    slots,
):
    tokens, cols = residual_in.shape
    me = lax.axis_index("tensor")
    plane, row, core = me // 4, me // 2 % 2, me % 2
    offsets = [row * 2 + core, (1 - row) * 2 + core, row * 2 + 1 - core, (1 - row) * 2 + 1 - core]
    where = {k: jnp.stack([(plane + k) % 4, *offsets]).astype(jnp.int32) for k in range(4)}

    place_in = jnp.arange(tokens, dtype=jnp.int32)
    cands = lengths.shape[0]
    cand = jnp.arange(cands, dtype=jnp.int32)
    starts = jnp.sum(jnp.where(cand[None, :] < cand[:, None], lengths[None, :], 0), axis=1)
    step = jnp.arange(SEQ, dtype=jnp.int32)
    live = (step[None, :] < lengths[:, None]).reshape(-1)
    packed = jnp.where(live, (starts[:, None] + step[None, :]).reshape(-1), -1)

    expert_at = (plane + jnp.arange(EXPERTS, dtype=jnp.int32)) % EXPERTS
    hit = (expert_ids[:, :, None] == expert_at[None, None, :]) & live[:, None, None]
    used = jnp.any(hit, axis=1)
    gate = jnp.sum(jnp.where(hit, gate_values[:, :, None], 0.0), axis=1)
    earlier = (place_in[None, :] < place_in[:, None]).astype(jnp.bfloat16)
    rank = jnp.dot(earlier, used.astype(jnp.bfloat16), preferred_element_type=jnp.float32)
    slot = jnp.where(used, rank.astype(jnp.int32), -1)

    slot_rows = jnp.concatenate(
        [slot.T, packed[None, :], jnp.zeros((3, tokens), jnp.int32)], axis=0
    )
    *picked_rows, x_live = dispatch(slot_rows, residual_in, norm_gain[None, :], slots, live_rows)
    chunks = spread(picked_rows)

    stream = residual_in.astype(jnp.float32)
    in_total = summed_all(jnp.sum(stream * stream, axis=1))
    in_scale = 1.0 / jnp.sqrt(in_total / D + epsilon)
    own_slot = one_hot(slot[:, 0], slots)
    inv_slot = jnp.sum(jnp.where(own_slot, in_scale[None, :], 0.0), axis=1, keepdims=True)
    gate_slot = jnp.sum(jnp.where(own_slot, gate[:, 0][None, :], 0.0), axis=1, keepdims=True)
    live_at = one_hot(packed, live_rows)
    slot_live = (
        jnp.sum(jnp.where(live_at[:, :, None], slot[None, :, :] + 1, 0), axis=1) - 1
    )
    slot_live = jnp.stack([slot_live[:, (4 - k) % 4] for k in range(4)], axis=1)
    target_live = jnp.sum(jnp.where(live_at, target_ids[None, :], 0), axis=1, keepdims=True)

    sums = None
    for k in ORDER:
        last = k == ORDER[-1]
        sums = hidden_part(
            where[(4 - k) % 4], chunks[k], w_gate, w_up, sums, inv_slot if last else None
        )
    hidden = sums

    parts = {}
    for k in (2, 1, 3, 0):
        own, across, near, far = down_part(where[k], hidden, w_down, gate_slot, cols)
        near = send(near, core_pairs())
        far = send(far, core_pairs())
        across = send((across + far.astype(jnp.float32)).astype(jnp.bfloat16), row_pairs())
        own = own + near.astype(jnp.float32) + across.astype(jnp.float32)
        own = own.astype(jnp.bfloat16)
        parts[k] = send(own, plane_pairs(k)) if k else own

    scaled, squares = mix(slot_live, x_live, final_gain[None, :], [parts[k] for k in range(4)])
    chunks = spread([scaled] * 4)
    out_total = summed_all(squares.reshape(-1))
    out_scale = (1.0 / jnp.sqrt(out_total / D + epsilon))[:, None]
    local_ids = target_live - me * lm_head.shape[1]
    sums = None
    for k in ORDER:
        last = k == ORDER[-1]
        sums = vocab_part(
            where[(4 - k) % 4], chunks[k], lm_head, sums, out_scale if last else None, local_ids
        )
    stats = sums[:, :3].T

    def joined(a, b):
        top = jnp.maximum(a[0], b[0])
        return jnp.stack(
            [top, a[1] * jnp.exp(a[0] - top) + b[1] * jnp.exp(b[0] - top), a[2] + b[2]]
        )

    stats = joined(stats, send(stats, core_pairs()))
    stats = joined(stats, send(stats, row_pairs()))
    others = [send(stats, plane_pairs(k)) for k in (1, 2, 3)]
    stats = joined(joined(stats, others[0]), joined(others[1], others[2]))
    logprob = stats[2] - stats[0] - jnp.log(stats[1])
    rows_dev = tokens // lax.axis_size("tensor")
    own_packed = lax.dynamic_slice_in_dim(packed, me * rows_dev, rows_dev)
    mine = own_packed[:, None] == jnp.arange(live_rows, dtype=jnp.int32)[None, :]
    return jnp.sum(jnp.where(mine, logprob[None, :], 0.0), axis=1)


def body(*args):
    if lax.axis_size("tensor") != 16:
        return plain_body(*args)
    tokens = args[0].shape[0]
    return fast_body(*args, live_rows=tokens, slots=CAP)


def solution(mesh):
    return jax.shard_map(
        body,
        mesh=mesh,
        in_specs=(
            P("groups", "tensor"),
            P("tensor"),
            P("tensor"),
            P("groups", None),
            P("groups", None),
            P(None, "tensor"),
            P(None, "tensor"),
            P("tensor", None),
            P(None, "tensor"),
            P("groups"),
            P("groups"),
        ),
        out_specs=P(("groups", "tensor")),
        check_vma=False,
    )
```

```python
import functools
import jax
import jax.numpy as jnp
from jax import lax
from jax.experimental import pallas as pl
from jax.experimental.pallas import tpu as pltpu
from jax.sharding import PartitionSpec as P

D = 6144
EXPERTS = 4
EXP_FF = 8192
TOP = 2
SEQ = 64
CAP = 384


epsilon = 1e-05


def combined_all(array, axis, combine):
    everything = jax.tree.map(lambda part: lax.all_gather(part, axis), array)
    leading = jax.tree.map(lambda part: part[0], everything)

    def hop(k, so_far):
        return combine(so_far, jax.tree.map(lambda part: part[k], everything))

    return lax.fori_loop(1, lax.axis_size(axis), hop, leading)


def slots_of(expert_ids):
    flat_ids = expert_ids.reshape(-1)
    pairs = jnp.arange(flat_ids.shape[0], dtype=jnp.int32)
    before = (pairs[None, :] < pairs[:, None]) & (flat_ids[None, :] == flat_ids[:, None])
    return jnp.sum(before.astype(jnp.int32), axis=1).reshape(expert_ids.shape)


def slot_tokens(expert_ids, slot_index):
    slot_code = (expert_ids * CAP + slot_index).reshape(-1)
    owner = jnp.arange(slot_code.shape[0], dtype=jnp.int32) // TOP
    wanted = jnp.arange(EXPERTS * CAP, dtype=jnp.int32)
    matches = slot_code[None, :] == wanted[:, None]
    return jnp.sum(jnp.where(matches, owner[None, :] + 1, 0), axis=1) - 1


def normalize(values, squares_total, gain_vec):
    return (
        values / jnp.sqrt(squares_total[:, None] / D + epsilon) * gain_vec.astype(jnp.float32)
    ).astype(jnp.bfloat16)


def plain_body(
    residual_in,
    norm_gain,
    final_gain,
    expert_ids,
    gate_values,
    w_gate,
    w_up,
    w_down,
    lm_head,
    target_ids,
    lengths,
):
    tokens, feature_cols = residual_in.shape
    hidden_dev = w_gate.shape[1]
    per_expert = EXP_FF // hidden_dev
    expert_now = lax.axis_index("tensor") // per_expert
    stream = residual_in.astype(jnp.float32)
    in_total = lax.psum(jnp.sum(stream * stream, axis=1), "tensor")
    normed = normalize(stream, in_total, norm_gain)
    slot_index = slots_of(expert_ids)
    token_of = slot_tokens(expert_ids, slot_index)
    zero_bf = jnp.zeros((), jnp.bfloat16)
    own_slots = lax.dynamic_slice_in_dim(token_of, expert_now * CAP, CAP)
    occupied = own_slots >= 0
    safe_index = jnp.maximum(own_slots, 0)
    slot_rows = jnp.where(
        occupied[:, None], lax.all_gather(normed, "tensor", axis=1, tiled=True)[safe_index], zero_bf
    )
    gate_out = jnp.dot(slot_rows, w_gate, preferred_element_type=jnp.float32)
    up_out = jnp.dot(slot_rows, w_up, preferred_element_type=jnp.float32)
    hidden = (jax.nn.silu(gate_out) * up_out).astype(jnp.bfloat16)
    partial_value = jnp.dot(hidden, w_down, preferred_element_type=jnp.float32)
    weight_own = jnp.where(expert_ids == expert_now, gate_values, jnp.zeros_like(gate_values))
    weighted = (
        weight_own[:, 0:1] * partial_value[slot_index[:, 0]]
        + weight_own[:, 1:2] * partial_value[slot_index[:, 1]]
    )
    moe_cols = lax.psum_scatter(weighted, "tensor", scatter_dimension=1, tiled=True)
    mixture = stream + moe_cols
    out_total = lax.psum(jnp.sum(mixture * mixture, axis=1), "tensor")
    normed_out = normalize(mixture, out_total, final_gain)
    vocab_dev = lm_head.shape[1]
    logits = jnp.dot(
        lax.all_gather(normed_out, "tensor", axis=1, tiled=True),
        lm_head,
        preferred_element_type=jnp.float32,
    )
    row_max = jnp.max(logits, axis=1)
    row_total = jnp.sum(jnp.exp(logits - row_max[:, None]), axis=1)
    local_ids = target_ids - lax.axis_index("tensor") * vocab_dev
    vocab_cols = jnp.arange(vocab_dev, dtype=jnp.int32)
    picked = jnp.sum(jnp.where(vocab_cols[None, :] == local_ids[:, None], logits, 0.0), axis=1)

    def joined(earlier, later):
        merged_max = jnp.maximum(earlier[0], later[0])
        merged_total = earlier[1] * jnp.exp(earlier[0] - merged_max) + later[1] * jnp.exp(
            later[0] - merged_max
        )
        return (merged_max, merged_total, earlier[2] + later[2])

    merged_max, merged_total, target_logit = combined_all(
        (row_max, row_total, picked), "tensor", joined
    )
    logprob = target_logit - merged_max - jnp.log(merged_total)
    rows_dev = tokens // lax.axis_size("tensor")
    first_row = lax.axis_index("tensor") * rows_dev
    own_rows = lax.dynamic_slice_in_dim(logprob, first_row, rows_dev)
    position = first_row + jnp.arange(rows_dev, dtype=jnp.int32)
    in_length = position % SEQ < lengths[position // SEQ]
    return jnp.where(in_length, own_rows, jnp.zeros_like(own_rows)).astype(jnp.float32)

VMEM_BYTES = 56 * 1024 * 1024
GROUPS = ((0,), (1, 3), (2,))
TIERS = ((256, 192), (288, 224), (320, 256), (384, 288))


def send(array, pairs):
    return lax.ppermute(array, "tensor", pairs)


def core_pairs():
    return [(i, i ^ 1) for i in range(16)]


def row_pairs():
    return [(i, i ^ 2) for i in range(16)]


def plane_pairs(k):
    return [(i, ((i >> 2) + k) % 4 * 4 + (i & 3)) for i in range(16)]


def after(value, *others):
    return lax.optimization_barrier((value, *others))[0]


def summed_all(array):
    array = array + send(array, core_pairs())
    array = array + send(array, row_pairs())
    others = [send(array, plane_pairs(k)) for k in (1, 2, 3)]
    return array + others[0] + (others[1] + others[2])


def one_hot(column, count):
    return column[None, :] == jnp.arange(count, dtype=jnp.int32)[:, None]


def params(steps):
    return pltpu.CompilerParams(
        dimension_semantics=("arbitrary",) * steps, vmem_limit_bytes=VMEM_BYTES
    )


def cost(rows, inner, cols, other_bytes):
    return pl.CostEstimate(
        flops=2 * rows * inner * cols,
        transcendentals=0,
        bytes_accessed=2 * inner * cols + other_bytes,
    )


def dispatch_kernel(slot_ref, x_ref, gain_ref, s0, s1, s2, s3, xc_ref):
    x = x_ref[...]
    scaled = (x.astype(jnp.float32) * gain_ref[...].astype(jnp.float32)).astype(jnp.bfloat16)
    tokens = x.shape[0]
    for k, out in enumerate((s0, s1, s2, s3)):
        rows = out.shape[0]
        spots = lax.broadcasted_iota(jnp.int32, (rows, tokens), 0)
        chosen = jnp.where(slot_ref[k : k + 1, :] == spots, 1.0, 0.0).astype(jnp.bfloat16)
        out[...] = jnp.dot(chosen, scaled, preferred_element_type=jnp.float32).astype(jnp.bfloat16)
    rows = xc_ref.shape[0]
    spots = lax.broadcasted_iota(jnp.int32, (rows, tokens), 0)
    chosen = jnp.where(slot_ref[4:5, :] == spots, 1.0, 0.0).astype(jnp.bfloat16)
    xc_ref[...] = jnp.dot(chosen, x, preferred_element_type=jnp.float32).astype(jnp.bfloat16)


def dispatch(slot_rows, x, gain, slots, live_rows):
    cols = x.shape[1]
    block = jax.ShapeDtypeStruct((slots, cols), jnp.bfloat16)
    return pl.pallas_call(
        dispatch_kernel,
        out_shape=[block] * 4 + [jax.ShapeDtypeStruct((live_rows, cols), jnp.bfloat16)],
        compiler_params=pltpu.CompilerParams(vmem_limit_bytes=VMEM_BYTES),
    )(slot_rows, x, gain)


def place(where_ref, chunk, blocks, wide_ref):
    rows, cols = wide_ref.shape[0], blocks[0].shape[1]
    for g in range(chunk):
        for b, block in enumerate(blocks):
            at = pl.multiple_of(g * 4 * cols + where_ref[b] * cols, 128)
            wide_ref[:, pl.ds(at, cols)] = block[g * rows : (g + 1) * rows, :]


def product(wide, weights):
    depth = weights[0].shape[0]
    value = None
    for g, w in enumerate(weights):
        part = jnp.dot(
            wide[:, g * depth : (g + 1) * depth], w[...], preferred_element_type=jnp.float32
        )
        value = part if value is None else value + part
    return value


def hidden_kernel(chunk, first, last, where_ref, *refs):
    blocks, wg, wu, refs = refs[:4], refs[4 : 4 + chunk], refs[4 + chunk : 4 + 2 * chunk], refs[4 + 2 * chunk :]
    if not first:
        g_in, u_in, refs = refs[0], refs[1], refs[2:]
    if last:
        inv, h_out, wide = refs
    else:
        g_out, u_out, wide = refs

    @pl.when(pl.program_id(0) == 0)
    def _():
        place(where_ref, chunk, blocks, wide)

    g = product(wide, wg)
    u = product(wide, wu)
    if not first:
        g = g + g_in[...]
        u = u + u_in[...]
    if last:
        g = g * inv[...]
        u = u * inv[...]
        h_out[...] = (g / (1.0 + jnp.exp(-g)) * u).astype(jnp.bfloat16)
    else:
        g_out[...] = g
        u_out[...] = u


def weight_specs(chunk, depth, tile):
    return [
        pl.BlockSpec((depth, tile), functools.partial(lambda g, n, w: (w[4 + g], n), g))
        for g in range(chunk)
    ]


def hidden_part(where, blocks, slots, w_gate, w_up, sums, inv):
    cols = blocks[0].shape[1]
    chunk = blocks[0].shape[0] // slots
    width = w_gate.shape[1]
    tile = 512
    first, last = sums is None, inv is not None
    whole = pl.BlockSpec((chunk * slots, cols), lambda n, w: (0, 0))
    out_tile = pl.BlockSpec((slots, tile), lambda n, w: (0, n))
    ins = [where, *blocks] + [w_gate] * chunk + [w_up] * chunk
    specs = [whole] * 4 + weight_specs(chunk, 4 * cols, tile) * 2
    aliases = {}
    if not first:
        if not last:
            aliases = {len(ins): 0, len(ins) + 1: 1}
        ins += list(sums)
        specs += [out_tile] * 2
    if last:
        ins.append(inv)
        specs.append(pl.BlockSpec((slots, 1), lambda n, w: (0, 0)))
        outs, out_specs = jax.ShapeDtypeStruct((slots, width), jnp.bfloat16), out_tile
    else:
        outs = [jax.ShapeDtypeStruct((slots, width), jnp.float32)] * 2
        out_specs = [out_tile] * 2
    return pl.pallas_call(
        functools.partial(hidden_kernel, chunk, first, last),
        out_shape=outs,
        grid_spec=pltpu.PrefetchScalarGridSpec(
            num_scalar_prefetch=1,
            grid=(width // tile,),
            in_specs=specs,
            out_specs=out_specs,
            scratch_shapes=[pltpu.VMEM((slots, chunk * 4 * cols), jnp.bfloat16)],
        ),
        input_output_aliases=aliases,
        compiler_params=params(1),
        cost_estimate=cost(slots, chunk * 4 * cols, 2 * width, 16 * slots * width),
    )(*ins)


def down_kernel(where_ref, h_ref, w_ref, gate_ref, o_own, o_row, o_core, total):
    @pl.when(pl.program_id(0) == 0)
    def _():
        total[...] = jnp.zeros_like(total)

    total[...] += jnp.dot(h_ref[...], w_ref[...], preferred_element_type=jnp.float32)

    @pl.when(pl.program_id(0) == pl.num_programs(0) - 1)
    def _():
        rows, cols = o_own.shape
        for b in range(4):
            at = pl.multiple_of(where_ref[b] * cols, 128)
            value = total[:, pl.ds(at, cols)] * gate_ref[...]
            if b < 2:
                (o_own, o_row)[b][...] = value
            else:
                o_core[(b - 2) * rows : (b - 1) * rows, :] = value.astype(jnp.bfloat16)


def down_part(where, hidden, w_down, gate_slot, cols):
    rows, inner = hidden.shape
    depth = 1024
    block = pl.BlockSpec((rows, cols), lambda j, w: (0, 0))
    return pl.pallas_call(
        down_kernel,
        out_shape=[
            jax.ShapeDtypeStruct((rows, cols), jnp.float32),
            jax.ShapeDtypeStruct((rows, cols), jnp.float32),
            jax.ShapeDtypeStruct((2 * rows, cols), jnp.bfloat16),
        ],
        grid_spec=pltpu.PrefetchScalarGridSpec(
            num_scalar_prefetch=1,
            grid=(inner // depth,),
            in_specs=[
                pl.BlockSpec((rows, depth), lambda j, w: (0, j)),
                pl.BlockSpec((depth, 4 * cols), lambda j, w: (j, w[4])),
                pl.BlockSpec((rows, 1), lambda j, w: (0, 0)),
            ],
            out_specs=[block] * 2 + [pl.BlockSpec((2 * rows, cols), lambda j, w: (0, 0))],
            scratch_shapes=[pltpu.VMEM((rows, 4 * cols), jnp.float32)],
        ),
        compiler_params=params(1),
        cost_estimate=cost(rows, inner, 4 * cols, 24 * rows * cols),
    )(where, hidden, w_down, gate_slot)


def mix_kernel(slot_ref, x_ref, gain_ref, e0, e1, e2, e3, out_ref, squares_ref):
    rows = x_ref.shape[0]
    mixture = x_ref[...].astype(jnp.float32)
    moe = jnp.zeros_like(mixture)
    for j, part in enumerate((e0, e1, e2, e3)):
        slots = part.shape[0]
        spots = lax.broadcasted_iota(jnp.int32, (rows, slots), 1)
        chosen = jnp.where(slot_ref[:, j : j + 1] == spots, 1.0, 0.0).astype(jnp.bfloat16)
        moe = moe + jnp.dot(chosen, part[...], preferred_element_type=jnp.float32)
    mixture = mixture + moe
    out_ref[...] = (mixture * gain_ref[...].astype(jnp.float32)).astype(jnp.bfloat16)
    squares_ref[...] = jnp.sum(mixture * mixture, axis=1, keepdims=True)


def mix(slot_cols, x, gain, parts):
    rows, cols = x.shape
    return pl.pallas_call(
        mix_kernel,
        out_shape=[
            jax.ShapeDtypeStruct((rows, cols), jnp.bfloat16),
            jax.ShapeDtypeStruct((rows, 1), jnp.float32),
        ],
        compiler_params=pltpu.CompilerParams(vmem_limit_bytes=VMEM_BYTES),
    )(slot_cols, x, gain, *parts)


def vocab_kernel(chunk, first, last, where_ref, *refs):
    blocks, weights, refs = refs[:4], refs[4 : 4 + chunk], refs[4 + chunk :]
    if not first:
        sum_in, refs = refs[0], refs[1:]
    if last:
        inv, local_ids, out, wide, top, total, picked = refs
    else:
        out, wide = refs
    n = pl.program_id(0)

    @pl.when(n == 0)
    def _():
        place(where_ref, chunk, blocks, wide)

    value = product(wide, weights)
    if not first:
        value = value + sum_in[...]
    if not last:
        out[...] = value
        return
    logits = value * inv[...]
    rows, tile = logits.shape
    column = n * tile + lax.broadcasted_iota(jnp.int32, (rows, tile), 1)
    tile_pick = jnp.sum(jnp.where(column == local_ids[...], logits, 0.0), axis=1, keepdims=True)
    tile_top = jnp.max(logits, axis=1, keepdims=True)

    @pl.when(n == 0)
    def _():
        top[...] = tile_top
        total[...] = jnp.sum(jnp.exp(logits - tile_top), axis=1, keepdims=True)
        picked[...] = tile_pick

    @pl.when(n > 0)
    def _():
        new_top = jnp.maximum(top[...], tile_top)
        total[...] = total[...] * jnp.exp(top[...] - new_top) + jnp.sum(
            jnp.exp(logits - new_top), axis=1, keepdims=True
        )
        top[...] = new_top
        picked[...] = picked[...] + tile_pick

    @pl.when(n == pl.num_programs(0) - 1)
    def _():
        lane = lax.broadcasted_iota(jnp.int32, out.shape, 1)
        out[...] = jnp.where(lane == 0, top[...], jnp.where(lane == 1, total[...], picked[...]))


def vocab_part(where, blocks, rows, lm_head, sums, inv, local_ids):
    cols = blocks[0].shape[1]
    chunk = blocks[0].shape[0] // rows
    width = lm_head.shape[1]
    tile = 512
    first, last = sums is None, inv is not None
    whole = pl.BlockSpec((chunk * rows, cols), lambda n, w: (0, 0))
    out_tile = pl.BlockSpec((rows, tile), lambda n, w: (0, n))
    ins = [where, *blocks] + [lm_head] * chunk
    specs = [whole] * 4 + weight_specs(chunk, 4 * cols, tile)
    aliases = {}
    if not first:
        if not last:
            aliases = {len(ins): 0}
        ins.append(sums)
        specs.append(out_tile)
    scratch = [pltpu.VMEM((rows, chunk * 4 * cols), jnp.bfloat16)]
    if last:
        ins += [inv, local_ids]
        specs += [pl.BlockSpec((rows, 1), lambda n, w: (0, 0))] * 2
        outs = jax.ShapeDtypeStruct((rows, 128), jnp.float32)
        out_specs = pl.BlockSpec((rows, 128), lambda n, w: (0, 0))
        scratch += [pltpu.VMEM((rows, 1), jnp.float32)] * 3
    else:
        outs, out_specs = jax.ShapeDtypeStruct((rows, width), jnp.float32), out_tile
    return pl.pallas_call(
        functools.partial(vocab_kernel, chunk, first, last),
        out_shape=outs,
        grid_spec=pltpu.PrefetchScalarGridSpec(
            num_scalar_prefetch=1,
            grid=(width // tile,),
            in_specs=specs,
            out_specs=out_specs,
            scratch_shapes=scratch,
        ),
        input_output_aliases=aliases,
        compiler_params=params(1),
        cost_estimate=cost(rows, chunk * 4 * cols, width, 8 * rows * width),
    )(*ins)


def shared(own, row):
    return (own, row, send(own, core_pairs()), send(row, core_pairs()))


def spread_and_sum(by_offset, part):
    a1 = send(by_offset[1], plane_pairs(1))
    a3 = send(by_offset[3], plane_pairs(3))
    row0 = send(by_offset[0], row_pairs())
    a2 = send(after(by_offset[2], a1, a3), plane_pairs(2))
    near = jnp.concatenate([a1, a3], axis=0)
    row13 = send(near, row_pairs())
    sums = part(0, shared(by_offset[0], row0), None)
    a2 = after(a2, sums)
    row2 = send(a2, row_pairs())
    sums = part(1, shared(near, row13), sums)
    row2 = after(row2, sums)
    return part(2, shared(a2, row2), sums)


def live_part(
    residual_in,
    norm_gain,
    final_gain,
    w_gate,
    w_up,
    w_down,
    lm_head,
    target_ids,
    packed,
    slot,
    gate,
    in_squares,
    live_rows,
    slots,
):
    tokens, cols = residual_in.shape
    me = lax.axis_index("tensor")
    plane, row, core = me // 4, me // 2 % 2, me % 2
    at = [row * 2 + core, (1 - row) * 2 + core, row * 2 + 1 - core, (1 - row) * 2 + 1 - core]
    planes = [(plane + k) % 4 for k in range(4)]
    group_at = [
        jnp.stack(at + [planes[(4 - k) % 4] for k in group]).astype(jnp.int32) for group in GROUPS
    ]
    down_at = [jnp.stack(at + [planes[k]]).astype(jnp.int32) for k in range(4)]

    slot_rows = jnp.concatenate(
        [slot.T, packed[None, :], jnp.zeros((3, tokens), jnp.int32)], axis=0
    )
    *picked_rows, x_live = dispatch(slot_rows, residual_in, norm_gain[None, :], slots, live_rows)

    in_total = summed_all(in_squares)
    in_scale = 1.0 / jnp.sqrt(in_total / D + epsilon)
    own_slot = one_hot(slot[:, 0], slots)
    inv_slot = jnp.sum(jnp.where(own_slot, in_scale[None, :], 0.0), axis=1, keepdims=True)
    gate_slot = jnp.sum(jnp.where(own_slot, gate[:, 0][None, :], 0.0), axis=1, keepdims=True)
    live_at = one_hot(packed, live_rows)
    slot_live = (
        jnp.sum(jnp.where(live_at[:, :, None], slot[None, :, :] + 1, 0), axis=1) - 1
    )
    slot_live = jnp.stack([slot_live[:, (4 - k) % 4] for k in range(4)], axis=1)
    target_live = jnp.sum(jnp.where(live_at, target_ids[None, :], 0), axis=1, keepdims=True)

    hidden = spread_and_sum(
        picked_rows,
        lambda g, blocks, sums: hidden_part(
            group_at[g], blocks, slots, w_gate, w_up, sums, inv_slot if g == 2 else None
        ),
    )

    parts, heard, crossed, own = {}, {}, {}, {}
    waits = ()
    for turn, k in enumerate((2, 1, 3, 0)):
        kept, across, near = down_part(down_at[k], after(hidden, *waits), w_down, gate_slot, cols)
        heard[turn] = send(near, core_pairs())
        far = heard[turn][slots:].astype(jnp.float32)
        crossed[turn] = send((across + far).astype(jnp.bfloat16), row_pairs())
        total = (
            kept + heard[turn][:slots].astype(jnp.float32) + crossed[turn].astype(jnp.float32)
        ).astype(jnp.bfloat16)
        parts[k] = send(total, plane_pairs(k)) if k else total
        waits = (kept,)
        if turn >= 1:
            waits += (heard[turn - 1],)
        if turn >= 2:
            waits += (crossed[turn - 2],)

    scaled, squares = mix(slot_live, x_live, final_gain[None, :], [parts[k] for k in range(4)])
    out_total = summed_all(squares.reshape(-1))
    out_scale = (1.0 / jnp.sqrt(out_total / D + epsilon))[:, None]
    local_ids = target_live - me * lm_head.shape[1]
    stats = spread_and_sum(
        [scaled] * 4,
        lambda g, blocks, sums: vocab_part(
            group_at[g], blocks, live_rows, lm_head, sums, out_scale if g == 2 else None, local_ids
        ),
    )
    spot = packed[:, None] == jnp.arange(live_rows, dtype=jnp.int32)[None, :]
    return jnp.stack(
        [jnp.sum(jnp.where(spot, stats[:, j][None, :], 0.0), axis=1) for j in range(3)]
    )


def fast_body(
    residual_in,
    norm_gain,
    final_gain,
    expert_ids,
    gate_values,
    w_gate,
    w_up,
    w_down,
    lm_head,
    target_ids,
    lengths,
):
    tokens = residual_in.shape[0]
    devices = lax.axis_size("tensor")
    me = lax.axis_index("tensor")
    plane = me // 4
    cands = lengths.shape[0]
    cand = jnp.arange(cands, dtype=jnp.int32)
    starts = jnp.sum(jnp.where(cand[None, :] < cand[:, None], lengths[None, :], 0), axis=1)
    step = jnp.arange(SEQ, dtype=jnp.int32)
    live = (step[None, :] < lengths[:, None]).reshape(-1)
    packed = jnp.where(live, (starts[:, None] + step[None, :]).reshape(-1), -1)

    expert_at = (plane + jnp.arange(EXPERTS, dtype=jnp.int32)) % EXPERTS
    hit = (expert_ids[:, :, None] == expert_at[None, None, :]) & live[:, None, None]
    used = jnp.any(hit, axis=1)
    fullest = jnp.max(jnp.sum(used.astype(jnp.int32), axis=0))
    alive = jnp.sum(lengths)
    need = jnp.zeros((), jnp.float32)
    for rows, slots in TIERS:
        need = need + jnp.where((alive > rows) | (fullest > slots), 1.0, 0.0)
    pairs = [(g, g ^ 1) for g in range(2)]
    need = jnp.maximum(need, lax.ppermute(need, "groups", pairs))

    gate = jnp.sum(jnp.where(hit, gate_values[:, :, None], 0.0), axis=1)
    place_in = jnp.arange(tokens, dtype=jnp.int32)
    earlier = (place_in[None, :] < place_in[:, None]).astype(jnp.bfloat16)
    rank = jnp.dot(earlier, used.astype(jnp.bfloat16), preferred_element_type=jnp.float32)
    slot = jnp.where(used, rank.astype(jnp.int32), -1)
    stream = residual_in.astype(jnp.float32)
    in_squares = jnp.sum(stream * stream, axis=1)

    stats = lax.switch(
        need.astype(jnp.int32),
        [
            functools.partial(live_part, live_rows=rows, slots=slots)
            for rows, slots in TIERS + ((tokens, CAP),)
        ],
        residual_in,
        norm_gain,
        final_gain,
        w_gate,
        w_up,
        w_down,
        lm_head,
        target_ids,
        packed,
        slot,
        gate,
        in_squares,
    )
    rows_dev = tokens // devices
    stats = stats.reshape(3, devices, rows_dev).transpose(1, 0, 2)
    stats = lax.all_to_all(stats, "tensor", 0, 0, tiled=True)
    top = jnp.max(stats[:, 0], axis=0)
    total = jnp.sum(stats[:, 1] * jnp.exp(stats[:, 0] - top[None, :]), axis=0)
    logprob = jnp.sum(stats[:, 2], axis=0) - top - jnp.log(total)
    own_live = lax.dynamic_slice_in_dim(packed, me * rows_dev, rows_dev) >= 0
    return jnp.where(own_live, logprob, 0.0)


def body(*args):
    if lax.axis_size("tensor") == 16 and lax.axis_size("groups") == 2:
        return fast_body(*args)
    return plain_body(*args)


def solution(mesh):
    return jax.shard_map(
        body,
        mesh=mesh,
        in_specs=(
            P("groups", "tensor"),
            P("tensor"),
            P("tensor"),
            P("groups", None),
            P("groups", None),
            P(None, "tensor"),
            P(None, "tensor"),
            P("tensor", None),
            P(None, "tensor"),
            P("groups"),
            P("groups"),
        ),
        out_specs=P(("groups", "tensor")),
        check_vma=False,
    )
```

```python
import functools
import jax
import jax.numpy as jnp
from jax import lax
from jax.experimental import pallas as pl
from jax.experimental.pallas import tpu as pltpu
from jax.sharding import PartitionSpec as P

D = 6144
EXPERTS = 4
EXP_FF = 8192
TOP = 2
SEQ = 64
CAP = 384


epsilon = 1e-05


def combined_all(array, axis, combine):
    everything = jax.tree.map(lambda part: lax.all_gather(part, axis), array)
    leading = jax.tree.map(lambda part: part[0], everything)

    def hop(k, so_far):
        return combine(so_far, jax.tree.map(lambda part: part[k], everything))

    return lax.fori_loop(1, lax.axis_size(axis), hop, leading)


def slots_of(expert_ids):
    flat_ids = expert_ids.reshape(-1)
    pairs = jnp.arange(flat_ids.shape[0], dtype=jnp.int32)
    before = (pairs[None, :] < pairs[:, None]) & (flat_ids[None, :] == flat_ids[:, None])
    return jnp.sum(before.astype(jnp.int32), axis=1).reshape(expert_ids.shape)


def slot_tokens(expert_ids, slot_index):
    slot_code = (expert_ids * CAP + slot_index).reshape(-1)
    owner = jnp.arange(slot_code.shape[0], dtype=jnp.int32) // TOP
    wanted = jnp.arange(EXPERTS * CAP, dtype=jnp.int32)
    matches = slot_code[None, :] == wanted[:, None]
    return jnp.sum(jnp.where(matches, owner[None, :] + 1, 0), axis=1) - 1


def normalize(values, squares_total, gain_vec):
    return (
        values / jnp.sqrt(squares_total[:, None] / D + epsilon) * gain_vec.astype(jnp.float32)
    ).astype(jnp.bfloat16)


def plain_body(
    residual_in,
    norm_gain,
    final_gain,
    expert_ids,
    gate_values,
    w_gate,
    w_up,
    w_down,
    lm_head,
    target_ids,
    lengths,
):
    tokens, feature_cols = residual_in.shape
    hidden_dev = w_gate.shape[1]
    per_expert = EXP_FF // hidden_dev
    expert_now = lax.axis_index("tensor") // per_expert
    stream = residual_in.astype(jnp.float32)
    in_total = lax.psum(jnp.sum(stream * stream, axis=1), "tensor")
    normed = normalize(stream, in_total, norm_gain)
    slot_index = slots_of(expert_ids)
    token_of = slot_tokens(expert_ids, slot_index)
    zero_bf = jnp.zeros((), jnp.bfloat16)
    own_slots = lax.dynamic_slice_in_dim(token_of, expert_now * CAP, CAP)
    occupied = own_slots >= 0
    safe_index = jnp.maximum(own_slots, 0)
    slot_rows = jnp.where(
        occupied[:, None], lax.all_gather(normed, "tensor", axis=1, tiled=True)[safe_index], zero_bf
    )
    gate_out = jnp.dot(slot_rows, w_gate, preferred_element_type=jnp.float32)
    up_out = jnp.dot(slot_rows, w_up, preferred_element_type=jnp.float32)
    hidden = (jax.nn.silu(gate_out) * up_out).astype(jnp.bfloat16)
    partial_value = jnp.dot(hidden, w_down, preferred_element_type=jnp.float32)
    weight_own = jnp.where(expert_ids == expert_now, gate_values, jnp.zeros_like(gate_values))
    weighted = (
        weight_own[:, 0:1] * partial_value[slot_index[:, 0]]
        + weight_own[:, 1:2] * partial_value[slot_index[:, 1]]
    )
    moe_cols = lax.psum_scatter(weighted, "tensor", scatter_dimension=1, tiled=True)
    mixture = stream + moe_cols
    out_total = lax.psum(jnp.sum(mixture * mixture, axis=1), "tensor")
    normed_out = normalize(mixture, out_total, final_gain)
    vocab_dev = lm_head.shape[1]
    logits = jnp.dot(
        lax.all_gather(normed_out, "tensor", axis=1, tiled=True),
        lm_head,
        preferred_element_type=jnp.float32,
    )
    row_max = jnp.max(logits, axis=1)
    row_total = jnp.sum(jnp.exp(logits - row_max[:, None]), axis=1)
    local_ids = target_ids - lax.axis_index("tensor") * vocab_dev
    vocab_cols = jnp.arange(vocab_dev, dtype=jnp.int32)
    picked = jnp.sum(jnp.where(vocab_cols[None, :] == local_ids[:, None], logits, 0.0), axis=1)

    def joined(earlier, later):
        merged_max = jnp.maximum(earlier[0], later[0])
        merged_total = earlier[1] * jnp.exp(earlier[0] - merged_max) + later[1] * jnp.exp(
            later[0] - merged_max
        )
        return (merged_max, merged_total, earlier[2] + later[2])

    merged_max, merged_total, target_logit = combined_all(
        (row_max, row_total, picked), "tensor", joined
    )
    logprob = target_logit - merged_max - jnp.log(merged_total)
    rows_dev = tokens // lax.axis_size("tensor")
    first_row = lax.axis_index("tensor") * rows_dev
    own_rows = lax.dynamic_slice_in_dim(logprob, first_row, rows_dev)
    position = first_row + jnp.arange(rows_dev, dtype=jnp.int32)
    in_length = position % SEQ < lengths[position // SEQ]
    return jnp.where(in_length, own_rows, jnp.zeros_like(own_rows)).astype(jnp.float32)

VMEM_BYTES = 56 * 1024 * 1024
TIERS = ((256, 192), (288, 224), (320, 256), (384, 288))
CHUNKS = (0, 1, 3, 2)
BF = jnp.bfloat16
F32 = jnp.float32


def send(array, pairs):
    return lax.ppermute(array, "tensor", pairs)


def xor_pairs(mask):
    return [(i, i ^ mask) for i in range(16)]


def plane_pairs(k):
    return [(i, ((i >> 2) + k) % 4 * 4 + (i & 3)) for i in range(16)]


def after(value, *others):
    return lax.optimization_barrier((value, *others))[0]


def params(steps):
    return pltpu.CompilerParams(
        dimension_semantics=("arbitrary",) * steps, vmem_limit_bytes=VMEM_BYTES
    )


def cost(rows, inner, cols, other_bytes):
    return pl.CostEstimate(
        flops=2 * rows * inner * cols,
        transcendentals=0,
        bytes_accessed=2 * inner * cols + other_bytes,
    )


def route_kernel(where_ref, lengths_ref, ids_ref, gates_ref, slots_ref, gate_ref, need_ref, used_ref):
    tokens = ids_ref.shape[1]
    spot = lax.broadcasted_iota(jnp.int32, (1, tokens), 1)
    cand = lax.shift_right_logical(spot, SEQ.bit_length() - 1)
    size = jnp.zeros_like(spot)
    start = jnp.zeros_like(spot)
    alive = jnp.int32(0)
    for c in range(lengths_ref.shape[0]):
        size = jnp.where(cand == c, lengths_ref[c], size)
        start = jnp.where(cand == c, alive, start)
        alive = alive + lengths_ref[c]
    step = spot - cand * SEQ
    live = step < size
    used_ref[...] = jnp.zeros_like(used_ref)
    for k in range(EXPERTS):
        expert = lax.rem(where_ref[0] + k, EXPERTS)
        first = (ids_ref[0:1, :] == expert) & live
        second = (ids_ref[1:2, :] == expert) & live
        used_ref[k : k + 1, :] = jnp.where(first | second, 1.0, 0.0)
        if k == 0:
            gate_ref[...] = jnp.where(first, gates_ref[0:1, :], 0.0) + jnp.where(
                second, gates_ref[1:2, :], 0.0
            )
    used = used_ref[...]
    source = lax.broadcasted_iota(jnp.int32, (tokens, tokens), 0)
    target = lax.broadcasted_iota(jnp.int32, (tokens, tokens), 1)
    earlier = jnp.where(source < target, 1.0, 0.0).astype(BF)
    rank = jnp.dot(used.astype(BF), earlier, preferred_element_type=F32)
    slots_ref[...] = jnp.where(used > 0.0, rank.astype(jnp.int32), -1)
    slots_ref[4:5, :] = jnp.where(live, start + step, -1)
    fullest = jnp.max(jnp.sum(used, axis=1, keepdims=True))
    need = jnp.float32(0.0)
    for rows, slots in TIERS:
        over = (alive > rows) | (fullest > float(slots))
        need = need + jnp.where(over, 1.0, 0.0)
    need_ref[...] = jnp.full(need_ref.shape, need, F32)


def route(plane, lengths, ids, gates):
    tokens = ids.shape[1]
    smem = pl.BlockSpec(memory_space=pltpu.SMEM)
    vmem = pl.BlockSpec(memory_space=pltpu.VMEM)
    return pl.pallas_call(
        route_kernel,
        in_specs=[smem, smem, vmem, vmem],
        out_specs=[vmem] * 3,
        out_shape=[
            jax.ShapeDtypeStruct((8, tokens), jnp.int32),
            jax.ShapeDtypeStruct((1, tokens), F32),
            jax.ShapeDtypeStruct((8, 128), F32),
        ],
        scratch_shapes=[pltpu.VMEM((8, tokens), F32)],
        compiler_params=pltpu.CompilerParams(vmem_limit_bytes=VMEM_BYTES),
    )(plane.reshape(1), lengths, ids, gates)


def dispatch_kernel(slot_ref, x_ref, gain_ref, s0, s1, s2, s3, xc_ref):
    x = x_ref[...]
    scaled = (x.astype(F32) * gain_ref[...].astype(F32)).astype(BF)
    tokens = x.shape[0]
    for k, out in enumerate((s0, s1, s2, s3)):
        rows = out.shape[0]
        spots = lax.broadcasted_iota(jnp.int32, (rows, tokens), 0)
        chosen = jnp.where(slot_ref[k : k + 1, :] == spots, 1.0, 0.0).astype(BF)
        out[...] = jnp.dot(chosen, scaled, preferred_element_type=F32).astype(BF)
    rows = xc_ref.shape[0]
    spots = lax.broadcasted_iota(jnp.int32, (rows, tokens), 0)
    chosen = jnp.where(slot_ref[4:5, :] == spots, 1.0, 0.0).astype(BF)
    xc_ref[...] = jnp.dot(chosen, x, preferred_element_type=F32).astype(BF)


def dispatch(slot_rows, x, gain, slots, live_rows):
    cols = x.shape[1]
    block = jax.ShapeDtypeStruct((slots, cols), BF)
    return pl.pallas_call(
        dispatch_kernel,
        out_shape=[block] * 4 + [jax.ShapeDtypeStruct((live_rows, cols), BF)],
        compiler_params=pltpu.CompilerParams(vmem_limit_bytes=VMEM_BYTES),
    )(slot_rows, x, gain)


def place(where_ref, blocks, wide_ref):
    own0, a1, a3, row0, row13, core_a, a2, row2, core_b = blocks
    rows, cols = wide_ref.shape[0], own0.shape[1]

    def put(block, piece, quarter, chunk):
        at = (where_ref[4 + chunk] * 4 + where_ref[quarter]) * cols
        wide_ref[:, pl.ds(pl.multiple_of(at, 128), cols)] = block[piece * rows : (piece + 1) * rows, :]

    put(own0, 0, 0, 0)
    put(a1, 0, 0, 1)
    put(a3, 0, 0, 2)
    put(row0, 0, 1, 0)
    put(row13, 0, 1, 1)
    put(row13, 1, 1, 2)
    for piece, (quarter, chunk) in enumerate(((2, 0), (2, 1), (2, 2), (3, 0), (3, 1), (3, 2))):
        put(core_a, piece, quarter, chunk)
    put(a2, 0, 0, 3)
    put(row2, 0, 1, 3)
    put(core_b, 0, 2, 3)
    put(core_b, 1, 3, 3)


def whole_specs(blocks):
    return [pl.BlockSpec(block.shape, lambda n, w: (0, 0)) for block in blocks]


def hidden_kernel(where_ref, *refs):
    blocks, (wg, wu, inv, h_out, wide) = refs[:9], refs[9:]

    @pl.when(pl.program_id(0) == 0)
    def _():
        place(where_ref, blocks, wide)

    g = jnp.dot(wide[...], wg[...], preferred_element_type=F32) * inv[...]
    u = jnp.dot(wide[...], wu[...], preferred_element_type=F32) * inv[...]
    h_out[...] = (g / (1.0 + jnp.exp(-g)) * u).astype(BF)


def hidden_all(where, blocks, w_gate, w_up, inv):
    slots = blocks[0].shape[0]
    inner, width = w_gate.shape
    tile = 256
    weight = pl.BlockSpec((inner, tile), lambda n, w: (0, n))
    return pl.pallas_call(
        hidden_kernel,
        out_shape=jax.ShapeDtypeStruct((slots, width), BF),
        grid_spec=pltpu.PrefetchScalarGridSpec(
            num_scalar_prefetch=1,
            grid=(width // tile,),
            in_specs=whole_specs(blocks)
            + [weight, weight, pl.BlockSpec((slots, 1), lambda n, w: (0, 0))],
            out_specs=pl.BlockSpec((slots, tile), lambda n, w: (0, n)),
            scratch_shapes=[pltpu.VMEM((slots, inner), BF)],
        ),
        compiler_params=params(1),
        cost_estimate=cost(slots, inner, 2 * width, 4 * slots * inner),
    )(where, *blocks, w_gate, w_up, inv)


def down_kernel(where_ref, h_ref, w0, w1, gate_ref, o_own, o_row, o_core, total):
    rows = h_ref.shape[0]
    wide = w0.shape[1]

    @pl.when(pl.program_id(0) == 0)
    def _():
        total[...] = jnp.zeros_like(total)

    for g, w in enumerate((w0, w1)):
        total[:, g * wide : (g + 1) * wide] += jnp.dot(
            h_ref[...], w[...], preferred_element_type=F32
        )

    @pl.when(pl.program_id(0) == pl.num_programs(0) - 1)
    def _():
        cols = o_own.shape[1]
        for g in range(2):
            for b in range(4):
                at = pl.multiple_of(g * wide + where_ref[b] * cols, 128)
                value = total[:, pl.ds(at, cols)] * gate_ref[...]
                if b < 2:
                    (o_own, o_row)[b][g * rows : (g + 1) * rows, :] = value
                else:
                    first = ((b - 2) * 2 + g) * rows
                    o_core[first : first + rows, :] = value.astype(BF)


def down_half(where, hidden, w_down, gate_slot, cols):
    rows, inner = hidden.shape
    depth = 512
    sizes = ((2 * rows, F32), (2 * rows, F32), (4 * rows, BF))
    return pl.pallas_call(
        down_kernel,
        out_shape=[jax.ShapeDtypeStruct((count, cols), kind) for count, kind in sizes],
        grid_spec=pltpu.PrefetchScalarGridSpec(
            num_scalar_prefetch=1,
            grid=(inner // depth,),
            in_specs=[
                pl.BlockSpec((rows, depth), lambda j, w: (0, j)),
                pl.BlockSpec((depth, 4 * cols), lambda j, w: (j, w[4])),
                pl.BlockSpec((depth, 4 * cols), lambda j, w: (j, w[5])),
                pl.BlockSpec((rows, 1), lambda j, w: (0, 0)),
            ],
            out_specs=[pl.BlockSpec((count, cols), lambda j, w: (0, 0)) for count, _ in sizes],
            scratch_shapes=[pltpu.VMEM((rows, 8 * cols), F32)],
        ),
        compiler_params=params(1),
        cost_estimate=cost(rows, inner, 8 * cols, 48 * rows * cols),
    )(where, hidden, w_down, w_down, gate_slot)


def mix_kernel(slot_ref, x_ref, gain_ref, e0, e2, e1, e3, out_ref, squares_ref):
    rows = x_ref.shape[0]
    mixture = x_ref[...].astype(F32)
    moe = jnp.zeros_like(mixture)
    for j, part in enumerate((e0, e1, e2, e3)):
        slots = part.shape[0]
        spots = lax.broadcasted_iota(jnp.int32, (rows, slots), 1)
        chosen = jnp.where(slot_ref[:, j : j + 1] == spots, 1.0, 0.0).astype(BF)
        moe = moe + jnp.dot(chosen, part[...], preferred_element_type=F32)
    mixture = mixture + moe
    out_ref[...] = (mixture * gain_ref[...].astype(F32)).astype(BF)
    squares_ref[...] = jnp.sum(mixture * mixture, axis=1, keepdims=True)


def mix(slot_cols, x, gain, parts):
    rows, cols = x.shape
    return pl.pallas_call(
        mix_kernel,
        out_shape=[
            jax.ShapeDtypeStruct((rows, cols), BF),
            jax.ShapeDtypeStruct((rows, 1), F32),
        ],
        compiler_params=pltpu.CompilerParams(vmem_limit_bytes=VMEM_BYTES),
    )(slot_cols, x, gain, *parts)


def vocab_kernel(where_ref, *refs):
    blocks, (w_ref, inv, local_ids, out, wide, top, total, picked) = refs[:9], refs[9:]
    n = pl.program_id(0)

    @pl.when(n == 0)
    def _():
        place(where_ref, blocks, wide)

    logits = jnp.dot(wide[...], w_ref[...], preferred_element_type=F32) * inv[...]
    rows, tile = logits.shape
    column = n * tile + lax.broadcasted_iota(jnp.int32, (rows, tile), 1)
    tile_pick = jnp.sum(jnp.where(column == local_ids[...], logits, 0.0), axis=1, keepdims=True)
    tile_top = jnp.max(logits, axis=1, keepdims=True)

    @pl.when(n == 0)
    def _():
        top[...] = tile_top
        total[...] = jnp.sum(jnp.exp(logits - tile_top), axis=1, keepdims=True)
        picked[...] = tile_pick

    @pl.when(n > 0)
    def _():
        new_top = jnp.maximum(top[...], tile_top)
        total[...] = total[...] * jnp.exp(top[...] - new_top) + jnp.sum(
            jnp.exp(logits - new_top), axis=1, keepdims=True
        )
        top[...] = new_top
        picked[...] = picked[...] + tile_pick

    @pl.when(n == pl.num_programs(0) - 1)
    def _():
        lane = lax.broadcasted_iota(jnp.int32, out.shape, 1)
        out[...] = jnp.where(lane == 0, top[...], jnp.where(lane == 1, total[...], picked[...]))


def vocab_all(where, blocks, lm_head, inv, local_ids):
    rows = blocks[0].shape[0]
    inner, width = lm_head.shape
    tile = 512
    column = pl.BlockSpec((rows, 1), lambda n, w: (0, 0))
    return pl.pallas_call(
        vocab_kernel,
        out_shape=jax.ShapeDtypeStruct((rows, 128), F32),
        grid_spec=pltpu.PrefetchScalarGridSpec(
            num_scalar_prefetch=1,
            grid=(width // tile,),
            in_specs=whole_specs(blocks)
            + [pl.BlockSpec((inner, tile), lambda n, w: (0, n)), column, column],
            out_specs=pl.BlockSpec((rows, 128), lambda n, w: (0, 0)),
            scratch_shapes=[pltpu.VMEM((rows, inner), BF)] + [pltpu.VMEM((rows, 1), F32)] * 3,
        ),
        compiler_params=params(1),
        cost_estimate=cost(rows, inner, width, 4 * rows * inner),
    )(where, *blocks, lm_head, inv, local_ids)


def spread(by_offset, squares):
    own0 = by_offset[0]
    a1 = send(by_offset[1], plane_pairs(1))
    a3 = send(by_offset[3], plane_pairs(3))
    row0 = send(own0, xor_pairs(2))
    squares = squares + send(squares, xor_pairs(1))
    squares = squares + send(squares, xor_pairs(2))
    a2 = send(after(by_offset[2], a1, a3, squares), plane_pairs(2))
    row13 = send(jnp.concatenate([a1, a3], axis=0), xor_pairs(2))
    squares = squares + send(squares, xor_pairs(4))
    squares = squares + send(squares, xor_pairs(8))
    a2 = after(a2, squares)
    row2 = send(a2, xor_pairs(2))
    stack = jnp.concatenate([own0, a1, a3, row0, row13], axis=0)
    core_a = send(after(stack, a2), xor_pairs(1))
    core_b = send(jnp.concatenate([a2, row2], axis=0), xor_pairs(1))
    return (own0, a1, a3, row0, row13, core_a, a2, row2, core_b), squares


def live_part(
    x,
    norm_gain,
    final_gain,
    w_gate,
    w_up,
    w_down,
    lm_head,
    target_ids,
    slot_rows,
    gate_row,
    in_squares,
    where,
    down_a,
    down_b,
    first_id,
    live_rows,
    slots,
):
    cols = x.shape[1]
    *picked_rows, x_live = dispatch(slot_rows, x, norm_gain, slots, live_rows)
    blocks, in_total = spread(picked_rows, in_squares)

    in_scale = 1.0 / jnp.sqrt(in_total / D + epsilon)
    own_slot = slot_rows[0][None, :] == jnp.arange(slots, dtype=jnp.int32)[:, None]
    inv_slot = jnp.sum(jnp.where(own_slot, in_scale[None, :], 0.0), axis=1, keepdims=True)
    gate_slot = jnp.sum(jnp.where(own_slot, gate_row, 0.0), axis=1, keepdims=True)
    packed = slot_rows[4]
    live_at = packed[None, :] == jnp.arange(live_rows, dtype=jnp.int32)[:, None]
    slot_live = jnp.stack(
        [
            jnp.sum(jnp.where(live_at, slot_rows[(4 - k) % 4][None, :] + 1, 0), axis=1) - 1
            for k in range(4)
        ],
        axis=1,
    )
    local_ids = (
        jnp.sum(jnp.where(live_at, target_ids[None, :], 0), axis=1, keepdims=True) - first_id
    )

    hidden = hidden_all(where, blocks, w_gate, w_up, inv_slot)

    two = 2 * slots
    own_a, row_a, core_a = down_half(down_a, hidden, w_down, gate_slot, cols)
    heard_a = send(core_a, xor_pairs(1))
    across_a = (row_a + heard_a[two:].astype(F32)).astype(BF)
    own_b, row_b, core_b = down_half(down_b, after(hidden, across_a), w_down, gate_slot, cols)
    crossed_a = send(across_a, xor_pairs(2))
    heard_b = send(core_b, xor_pairs(1))
    total_a = (own_a + heard_a[:two].astype(F32) + crossed_a.astype(F32)).astype(BF)
    part2 = send(total_a[:slots], plane_pairs(2))
    part1 = send(total_a[slots:], plane_pairs(1))
    across_b = (row_b + heard_b[two:].astype(F32)).astype(BF)
    crossed_b = send(across_b, xor_pairs(2))
    total_b = (own_b + heard_b[:two].astype(F32) + crossed_b.astype(F32)).astype(BF)
    part3 = send(total_b[:slots], plane_pairs(3))
    parts = (total_b[slots:], part2, part1, part3)

    scaled, squares = mix(slot_live, x_live, final_gain, parts)
    blocks, out_total = spread([scaled] * 4, squares.reshape(-1))
    out_scale = (1.0 / jnp.sqrt(out_total / D + epsilon))[:, None]
    stats = vocab_all(where, blocks, lm_head, out_scale, local_ids)
    spot = packed[:, None] == jnp.arange(live_rows, dtype=jnp.int32)[None, :]
    return jnp.stack(
        [jnp.sum(jnp.where(spot, stats[:, j][None, :], 0.0), axis=1) for j in range(3)]
    )


def fast_body(
    residual_in,
    norm_gain,
    final_gain,
    expert_ids,
    gate_values,
    w_gate,
    w_up,
    w_down,
    lm_head,
    target_ids,
    lengths,
):
    tokens = residual_in.shape[0]
    devices = lax.axis_size("tensor")
    me = lax.axis_index("tensor").astype(jnp.int32)
    plane, row, core = me >> 2, (me >> 1) & 1, me & 1
    slot_rows, gate_row, need = route(plane, lengths, expert_ids.T, gate_values.T)
    need = jnp.maximum(need, lax.ppermute(need, "groups", [(0, 1), (1, 0)]))

    at = [row * 2 + core, (1 - row) * 2 + core, row * 2 + 1 - core, (1 - row) * 2 + 1 - core]
    planes = [(plane + k) & 3 for k in range(4)]
    where = jnp.stack(at + [planes[(4 - k) % 4] for k in CHUNKS])
    down_a = jnp.stack(at + [planes[2], planes[1]])
    down_b = jnp.stack(at + [planes[3], planes[0]])
    stream = residual_in.astype(F32)
    in_squares = jnp.sum(stream * stream, axis=1)

    stats = lax.switch(
        need[0, 0].astype(jnp.int32),
        [
            functools.partial(live_part, live_rows=rows, slots=slots)
            for rows, slots in TIERS + ((tokens, CAP),)
        ],
        residual_in,
        norm_gain[None, :],
        final_gain[None, :],
        w_gate,
        w_up,
        w_down,
        lm_head,
        target_ids,
        slot_rows,
        gate_row,
        in_squares,
        where,
        down_a,
        down_b,
        me * lm_head.shape[1],
    )
    rows_dev = tokens // devices
    stats = stats.reshape(3, devices, rows_dev).transpose(1, 0, 2)
    stats = lax.all_to_all(stats, "tensor", 0, 0, tiled=True)
    top = jnp.max(stats[:, 0], axis=0)
    total = jnp.sum(stats[:, 1] * jnp.exp(stats[:, 0] - top[None, :]), axis=0)
    logprob = jnp.sum(stats[:, 2], axis=0) - top - jnp.log(total)
    own_live = lax.dynamic_slice_in_dim(slot_rows[4], me * rows_dev, rows_dev) >= 0
    return jnp.where(own_live, logprob, 0.0)


def body(*args):
    if lax.axis_size("tensor") == 16 and lax.axis_size("groups") == 2:
        return fast_body(*args)
    return plain_body(*args)


def solution(mesh):
    return jax.shard_map(
        body,
        mesh=mesh,
        in_specs=(
            P("groups", "tensor"),
            P("tensor"),
            P("tensor"),
            P("groups", None),
            P("groups", None),
            P(None, "tensor"),
            P(None, "tensor"),
            P("tensor", None),
            P(None, "tensor"),
            P("groups"),
            P("groups"),
        ),
        out_specs=P(("groups", "tensor")),
        check_vma=False,
    )
```

```python
import functools
import jax
import jax.numpy as jnp
from jax import lax
from jax.experimental import pallas as pl
from jax.experimental.pallas import tpu as pltpu
from jax.sharding import PartitionSpec as P

D = 6144
EXPERTS = 4
EXP_FF = 8192
TOP = 2
SEQ = 64
CAP = 384


epsilon = 1e-05


def combined_all(array, axis, combine):
    everything = jax.tree.map(lambda part: lax.all_gather(part, axis), array)
    leading = jax.tree.map(lambda part: part[0], everything)

    def hop(k, so_far):
        return combine(so_far, jax.tree.map(lambda part: part[k], everything))

    return lax.fori_loop(1, lax.axis_size(axis), hop, leading)


def slots_of(expert_ids):
    flat_ids = expert_ids.reshape(-1)
    pairs = jnp.arange(flat_ids.shape[0], dtype=jnp.int32)
    before = (pairs[None, :] < pairs[:, None]) & (flat_ids[None, :] == flat_ids[:, None])
    return jnp.sum(before.astype(jnp.int32), axis=1).reshape(expert_ids.shape)


def slot_tokens(expert_ids, slot_index):
    slot_code = (expert_ids * CAP + slot_index).reshape(-1)
    owner = jnp.arange(slot_code.shape[0], dtype=jnp.int32) // TOP
    wanted = jnp.arange(EXPERTS * CAP, dtype=jnp.int32)
    matches = slot_code[None, :] == wanted[:, None]
    return jnp.sum(jnp.where(matches, owner[None, :] + 1, 0), axis=1) - 1


def normalize(values, squares_total, gain_vec):
    return (
        values / jnp.sqrt(squares_total[:, None] / D + epsilon) * gain_vec.astype(jnp.float32)
    ).astype(jnp.bfloat16)


def plain_body(
    residual_in,
    norm_gain,
    final_gain,
    expert_ids,
    gate_values,
    w_gate,
    w_up,
    w_down,
    lm_head,
    target_ids,
    lengths,
):
    tokens, feature_cols = residual_in.shape
    hidden_dev = w_gate.shape[1]
    per_expert = EXP_FF // hidden_dev
    expert_now = lax.axis_index("tensor") // per_expert
    stream = residual_in.astype(jnp.float32)
    in_total = lax.psum(jnp.sum(stream * stream, axis=1), "tensor")
    normed = normalize(stream, in_total, norm_gain)
    slot_index = slots_of(expert_ids)
    token_of = slot_tokens(expert_ids, slot_index)
    zero_bf = jnp.zeros((), jnp.bfloat16)
    own_slots = lax.dynamic_slice_in_dim(token_of, expert_now * CAP, CAP)
    occupied = own_slots >= 0
    safe_index = jnp.maximum(own_slots, 0)
    slot_rows = jnp.where(
        occupied[:, None], lax.all_gather(normed, "tensor", axis=1, tiled=True)[safe_index], zero_bf
    )
    gate_out = jnp.dot(slot_rows, w_gate, preferred_element_type=jnp.float32)
    up_out = jnp.dot(slot_rows, w_up, preferred_element_type=jnp.float32)
    hidden = (jax.nn.silu(gate_out) * up_out).astype(jnp.bfloat16)
    partial_value = jnp.dot(hidden, w_down, preferred_element_type=jnp.float32)
    weight_own = jnp.where(expert_ids == expert_now, gate_values, jnp.zeros_like(gate_values))
    weighted = (
        weight_own[:, 0:1] * partial_value[slot_index[:, 0]]
        + weight_own[:, 1:2] * partial_value[slot_index[:, 1]]
    )
    moe_cols = lax.psum_scatter(weighted, "tensor", scatter_dimension=1, tiled=True)
    mixture = stream + moe_cols
    out_total = lax.psum(jnp.sum(mixture * mixture, axis=1), "tensor")
    normed_out = normalize(mixture, out_total, final_gain)
    vocab_dev = lm_head.shape[1]
    logits = jnp.dot(
        lax.all_gather(normed_out, "tensor", axis=1, tiled=True),
        lm_head,
        preferred_element_type=jnp.float32,
    )
    row_max = jnp.max(logits, axis=1)
    row_total = jnp.sum(jnp.exp(logits - row_max[:, None]), axis=1)
    local_ids = target_ids - lax.axis_index("tensor") * vocab_dev
    vocab_cols = jnp.arange(vocab_dev, dtype=jnp.int32)
    picked = jnp.sum(jnp.where(vocab_cols[None, :] == local_ids[:, None], logits, 0.0), axis=1)

    def joined(earlier, later):
        merged_max = jnp.maximum(earlier[0], later[0])
        merged_total = earlier[1] * jnp.exp(earlier[0] - merged_max) + later[1] * jnp.exp(
            later[0] - merged_max
        )
        return (merged_max, merged_total, earlier[2] + later[2])

    merged_max, merged_total, target_logit = combined_all(
        (row_max, row_total, picked), "tensor", joined
    )
    logprob = target_logit - merged_max - jnp.log(merged_total)
    rows_dev = tokens // lax.axis_size("tensor")
    first_row = lax.axis_index("tensor") * rows_dev
    own_rows = lax.dynamic_slice_in_dim(logprob, first_row, rows_dev)
    position = first_row + jnp.arange(rows_dev, dtype=jnp.int32)
    in_length = position % SEQ < lengths[position // SEQ]
    return jnp.where(in_length, own_rows, jnp.zeros_like(own_rows)).astype(jnp.float32)

TIERS = ((256, 192), (288, 224), (320, 256), (384, 288))
CHUNKS = ((0,), (1, 3), (2,))
VMEM = pl.BlockSpec(memory_space=pltpu.VMEM)
BF = jnp.bfloat16
F32 = jnp.float32


def send(array, pairs):
    return lax.ppermute(array, "tensor", pairs)


def xor_pairs(mask):
    return [(i, i ^ mask) for i in range(16)]


def plane_pairs(k):
    return [(i, ((i >> 2) + k) % 4 * 4 + (i & 3)) for i in range(16)]


def after(value, *others):
    return lax.optimization_barrier((value, *others))[0]


def params(mebibytes):
    return pltpu.CompilerParams(vmem_limit_bytes=mebibytes * 1024 * 1024)


def cost(rows, inner, cols, other_bytes):
    return pl.CostEstimate(
        flops=2 * rows * inner * cols,
        transcendentals=0,
        bytes_accessed=2 * inner * cols + other_bytes,
    )


def route_kernel(where_ref, lengths_ref, ids_ref, gates_ref, slots_ref, gate_ref, need_ref, used_ref):
    tokens = ids_ref.shape[1]
    spot = lax.broadcasted_iota(jnp.int32, (1, tokens), 1)
    cand = lax.shift_right_logical(spot, SEQ.bit_length() - 1)
    size = jnp.zeros_like(spot)
    start = jnp.zeros_like(spot)
    alive = jnp.int32(0)
    for c in range(lengths_ref.shape[0]):
        size = jnp.where(cand == c, lengths_ref[c], size)
        start = jnp.where(cand == c, alive, start)
        alive = alive + lengths_ref[c]
    step = spot - cand * SEQ
    live = step < size
    used_ref[...] = jnp.zeros_like(used_ref)
    for k in range(EXPERTS):
        expert = lax.rem(where_ref[0] + k, EXPERTS)
        first = (ids_ref[0:1, :] == expert) & live
        second = (ids_ref[1:2, :] == expert) & live
        used_ref[k : k + 1, :] = jnp.where(first | second, 1.0, 0.0)
        if k == 0:
            gate_ref[...] = jnp.where(first, gates_ref[0:1, :], 0.0) + jnp.where(
                second, gates_ref[1:2, :], 0.0
            )
    used = used_ref[...]
    source = lax.broadcasted_iota(jnp.int32, (tokens, tokens), 0)
    target = lax.broadcasted_iota(jnp.int32, (tokens, tokens), 1)
    earlier = jnp.where(source < target, 1.0, 0.0).astype(BF)
    rank = jnp.dot(used.astype(BF), earlier, preferred_element_type=F32)
    slots_ref[...] = jnp.where(used > 0.0, rank.astype(jnp.int32), -1)
    slots_ref[4:5, :] = jnp.where(live, start + step, -1)
    fullest = jnp.max(jnp.sum(used, axis=1, keepdims=True))
    need = jnp.float32(0.0)
    for rows, slots in TIERS:
        over = (alive > rows) | (fullest > float(slots))
        need = need + jnp.where(over, 1.0, 0.0)
    need_ref[...] = jnp.full(need_ref.shape, need, F32)


def route(plane, lengths, ids, gates):
    tokens = ids.shape[1]
    smem = pl.BlockSpec(memory_space=pltpu.SMEM)
    vmem = pl.BlockSpec(memory_space=pltpu.VMEM)
    return pl.pallas_call(
        route_kernel,
        in_specs=[smem, smem, vmem, vmem],
        out_specs=[vmem] * 3,
        out_shape=[
            jax.ShapeDtypeStruct((8, tokens), jnp.int32),
            jax.ShapeDtypeStruct((1, tokens), F32),
            jax.ShapeDtypeStruct((8, 128), F32),
        ],
        scratch_shapes=[pltpu.VMEM((8, tokens), F32)],
        compiler_params=params(16),
    )(plane.reshape(1), lengths, ids, gates)


def dispatch_kernel(slot_ref, x_ref, gain_ref, s0, s1, s2, s3, xc_ref):
    x = x_ref[...]
    scaled = (x.astype(F32) * gain_ref[...].astype(F32)).astype(BF)
    tokens = x.shape[0]
    for k, out in enumerate((s0, s1, s2, s3)):
        rows = out.shape[0]
        spots = lax.broadcasted_iota(jnp.int32, (rows, tokens), 0)
        chosen = jnp.where(slot_ref[k : k + 1, :] == spots, 1.0, 0.0).astype(BF)
        out[...] = jnp.dot(chosen, scaled, preferred_element_type=F32).astype(BF)
    rows = xc_ref.shape[0]
    spots = lax.broadcasted_iota(jnp.int32, (rows, tokens), 0)
    chosen = jnp.where(slot_ref[4:5, :] == spots, 1.0, 0.0).astype(BF)
    xc_ref[...] = jnp.dot(chosen, x, preferred_element_type=F32).astype(BF)


def dispatch(slot_rows, x, gain, slots, live_rows):
    cols = x.shape[1]
    block = jax.ShapeDtypeStruct((slots, cols), BF)
    return pl.pallas_call(
        dispatch_kernel,
        out_shape=[block] * 4 + [jax.ShapeDtypeStruct((live_rows, cols), BF)],
        compiler_params=params(16),
    )(slot_rows, x, gain)


def place(where_ref, blocks, wide_ref):
    own, across, *core = blocks
    rows, cols = wide_ref.shape[0], own.shape[1]
    count = own.shape[0] // rows
    for g in range(count):
        pieces = ((own, g), (across, g), (core[0], g), (core[-1], g if len(core) == 2 else count + g))
        for quarter, (block, piece) in enumerate(pieces):
            at = pl.multiple_of((g * 4 + where_ref[quarter]) * cols, 128)
            wide_ref[:, pl.ds(at, cols)] = block[piece * rows : (piece + 1) * rows, :]


def whole_specs(arrays):
    return [pl.BlockSpec(array.shape, lambda n, w: (0, 0)) for array in arrays]


def product(wide, weights):
    depth = weights[0].shape[0]
    value = None
    for j, w in enumerate(weights):
        part = jnp.dot(
            wide[:, j * depth : (j + 1) * depth], w[...], preferred_element_type=F32
        )
        value = part if value is None else value + part
    return value


def weight_specs(count, depth, tile):
    return [
        pl.BlockSpec((depth, tile), functools.partial(lambda j, n, w: (w[4 + j], n), j))
        for j in range(count)
    ]


def hidden_kernel(given, count, first, last, where_ref, *refs):
    blocks, refs = refs[:given], refs[given:]
    wg, wu, refs = refs[:count], refs[count : 2 * count], refs[2 * count :]
    if not first:
        g_in, u_in, refs = refs[0], refs[1], refs[2:]
    if last:
        inv, h_out, wide = refs
    else:
        g_out, u_out, wide = refs
    n = pl.program_id(0)
    tile = wu[0].shape[1]

    @pl.when(n == 0)
    def _():
        place(where_ref, blocks, wide)

    g = product(wide, wg)
    u = product(wide, wu)
    at = pl.ds(pl.multiple_of(n * tile, 128), tile)
    if not first:
        g = g + g_in[:, at]
        u = u + u_in[:, at]
    if last:
        g = g * inv[...]
        u = u * inv[...]
        h_out[...] = (g / (1.0 + jnp.exp(-g)) * u).astype(BF)
    else:
        g_out[:, at] = g
        u_out[:, at] = u


def hidden_part(where, blocks, slots, w_gate, w_up, sums, inv):
    cols = blocks[0].shape[1]
    count = blocks[0].shape[0] // slots
    inner, width = w_up.shape
    tile, depth = 512, inner // 4
    first, last = sums is None, inv is not None
    ins = [where, *blocks] + [w_gate] * count + [w_up] * count
    specs = whole_specs(blocks) + weight_specs(count, depth, tile) * 2
    aliases = {}
    if not first:
        if not last:
            aliases = {len(ins): 0, len(ins) + 1: 1}
        ins += list(sums)
        specs += [VMEM] * 2
    if last:
        ins.append(inv)
        specs += whole_specs([inv])
        outs = jax.ShapeDtypeStruct((slots, width), BF)
        out_specs = pl.BlockSpec((slots, tile), lambda n, w: (0, n))
    else:
        outs, out_specs = [pltpu.VMEM((slots, width), F32)] * 2, [VMEM] * 2
    return pl.pallas_call(
        functools.partial(hidden_kernel, len(blocks), count, first, last),
        out_shape=outs,
        grid_spec=pltpu.PrefetchScalarGridSpec(
            num_scalar_prefetch=1,
            grid=(width // tile,),
            in_specs=specs,
            out_specs=out_specs,
            scratch_shapes=[pltpu.VMEM((slots, 4 * count * cols), BF)],
        ),
        input_output_aliases=aliases,
        compiler_params=params(30),
        cost_estimate=cost(slots, count * depth, 2 * width, 0),
    )(*ins)


def down_kernel(where_ref, h_ref, w_ref, gate_ref, *refs):
    *outs, total = refs
    rows = h_ref.shape[0]
    half = w_ref.shape[1]
    step = pl.program_id(0)
    value = jnp.dot(h_ref[...], w_ref[...], preferred_element_type=F32) * gate_ref[...]
    total[:, pl.ds(pl.multiple_of(lax.rem(step, 2) * half, 128), half)] = value
    for c in range(4):
        own, across, core = outs[3 * (c // 2) : 3 * (c // 2) + 3]
        g = c % 2

        @pl.when(step == 2 * c + 1)
        def _():
            cols = own.shape[1]
            for b in range(4):
                part = total[:, pl.ds(pl.multiple_of(where_ref[b] * cols, 128), cols)]
                if b < 2:
                    (own, across)[b][g * rows : (g + 1) * rows, :] = part
                else:
                    first = ((b - 2) * 2 + g) * rows
                    core[first : first + rows, :] = part.astype(BF)


def down_all(where, hidden, w_down, gate_slot, cols):
    rows, inner = hidden.shape
    sizes = ((2 * rows, F32), (2 * rows, F32), (4 * rows, BF)) * 2
    return pl.pallas_call(
        down_kernel,
        out_shape=[jax.ShapeDtypeStruct((count, cols), kind) for count, kind in sizes],
        grid_spec=pltpu.PrefetchScalarGridSpec(
            num_scalar_prefetch=1,
            grid=(8,),
            in_specs=[
                pl.BlockSpec((rows, inner), lambda j, w: (0, 0)),
                pl.BlockSpec((inner, 2 * cols), lambda j, w: (0, w[4 + j // 2] * 2 + j % 2)),
                pl.BlockSpec((rows, 1), lambda j, w: (0, 0)),
            ],
            out_specs=[pl.BlockSpec((count, cols), lambda j, w: (0, 0)) for count, _ in sizes],
            scratch_shapes=[pltpu.VMEM((rows, 4 * cols), F32)],
        ),
        compiler_params=params(40),
        cost_estimate=cost(rows, inner, 16 * cols, 64 * rows * cols),
    )(where, hidden, w_down, gate_slot)


def mix_kernel(slot_ref, x_ref, gain_ref, e0, e2, e1, e3, out_ref, squares_ref):
    rows = x_ref.shape[0]
    mixture = x_ref[...].astype(F32)
    moe = jnp.zeros_like(mixture)
    for j, part in enumerate((e0, e1, e2, e3)):
        slots = part.shape[0]
        spots = lax.broadcasted_iota(jnp.int32, (rows, slots), 1)
        chosen = jnp.where(slot_ref[:, j : j + 1] == spots, 1.0, 0.0).astype(BF)
        moe = moe + jnp.dot(chosen, part[...], preferred_element_type=F32)
    mixture = mixture + moe
    out_ref[...] = (mixture * gain_ref[...].astype(F32)).astype(BF)
    squares_ref[...] = jnp.sum(mixture * mixture, axis=1, keepdims=True)


def mix(slot_cols, x, gain, parts):
    rows, cols = x.shape
    return pl.pallas_call(
        mix_kernel,
        out_shape=[
            jax.ShapeDtypeStruct((rows, cols), BF),
            jax.ShapeDtypeStruct((rows, 1), F32),
        ],
        compiler_params=params(16),
    )(slot_cols, x, gain, *parts)


def vocab_kernel(given, count, first, last, tile, where_ref, *refs):
    blocks, refs = refs[:given], refs[given:]
    weights, refs = refs[:count], refs[count:]
    if not first:
        sum_in, refs = refs[0], refs[1:]
    if last:
        inv, local_ids, out, wide, top, total, picked = refs
    else:
        out, wide = refs
    n = pl.program_id(0)

    @pl.when(n == 0)
    def _():
        place(where_ref, blocks, wide)

    value = product(wide, weights)
    at = pl.ds(pl.multiple_of(n * tile, 128), tile)
    if not first:
        value = value + sum_in[:, at]
    if not last:
        out[:, at] = value
        return
    logits = value * inv[...]
    column = n * tile + lax.broadcasted_iota(jnp.int32, logits.shape, 1)
    tile_pick = jnp.sum(jnp.where(column == local_ids[...], logits, 0.0), axis=1, keepdims=True)
    tile_top = jnp.max(logits, axis=1, keepdims=True)

    @pl.when(n == 0)
    def _():
        top[...] = tile_top
        total[...] = jnp.sum(jnp.exp(logits - tile_top), axis=1, keepdims=True)
        picked[...] = tile_pick

    @pl.when(n > 0)
    def _():
        new_top = jnp.maximum(top[...], tile_top)
        total[...] = total[...] * jnp.exp(top[...] - new_top) + jnp.sum(
            jnp.exp(logits - new_top), axis=1, keepdims=True
        )
        top[...] = new_top
        picked[...] = picked[...] + tile_pick

    @pl.when(n == pl.num_programs(0) - 1)
    def _():
        lane = lax.broadcasted_iota(jnp.int32, out.shape, 1)
        out[...] = jnp.where(lane == 0, top[...], jnp.where(lane == 1, total[...], picked[...]))


def vocab_part(where, blocks, rows, lm_head, sums, inv, local_ids):
    cols = blocks[0].shape[1]
    count = blocks[0].shape[0] // rows
    inner, width = lm_head.shape
    tile = 512
    first, last = sums is None, inv is not None
    ins = [where, *blocks] + [lm_head] * count
    specs = whole_specs(blocks) + weight_specs(count, inner // 4, tile)
    aliases = {}
    if not first:
        if not last:
            aliases = {len(ins): 0}
        ins.append(sums)
        specs.append(VMEM)
    scratch = [pltpu.VMEM((rows, 4 * count * cols), BF)]
    if last:
        ins += [inv, local_ids]
        specs += whole_specs([inv, local_ids])
        outs = jax.ShapeDtypeStruct((rows, 128), F32)
        out_specs = pl.BlockSpec((rows, 128), lambda n, w: (0, 0))
        scratch += [pltpu.VMEM((rows, 1), F32)] * 3
    else:
        outs, out_specs = pltpu.VMEM((rows, width), F32), VMEM
    return pl.pallas_call(
        functools.partial(vocab_kernel, len(blocks), count, first, last, tile),
        out_shape=outs,
        grid_spec=pltpu.PrefetchScalarGridSpec(
            num_scalar_prefetch=1,
            grid=(width // tile,),
            in_specs=specs,
            out_specs=out_specs,
            scratch_shapes=scratch,
        ),
        input_output_aliases=aliases,
        compiler_params=params(32),
        cost_estimate=cost(rows, inner * count // 4, width, 0),
    )(*ins)


def spread(by_offset, squares, part):
    own0 = by_offset[0]
    a1 = send(by_offset[1], plane_pairs(1))
    a3 = send(by_offset[3], plane_pairs(3))
    row0 = send(own0, xor_pairs(2))
    core0 = send(own0, xor_pairs(1))
    diagonal0 = send(own0, xor_pairs(3))
    squares = squares + send(squares, xor_pairs(1))
    squares = squares + send(squares, xor_pairs(2))

    near = jnp.concatenate([a1, a3], axis=0)
    row0, core0, diagonal0, near, squares, far = lax.optimization_barrier(
        (row0, core0, diagonal0, near, squares, by_offset[2])
    )
    a2 = send(far, plane_pairs(2))
    row13 = send(near, xor_pairs(2))
    sums = part(0, (own0, row0, core0, diagonal0), None, None)

    a2, row13, squares, sums = lax.optimization_barrier((a2, row13, squares, sums))
    row2 = send(a2, xor_pairs(2))
    core13 = send(jnp.concatenate([near, row13], axis=0), xor_pairs(1))
    squares = squares + send(squares, xor_pairs(4))
    squares = squares + send(squares, xor_pairs(8))
    sums = part(1, (near, row13, core13), sums, None)

    row2, squares, sums = lax.optimization_barrier((row2, squares, sums))
    core2 = send(jnp.concatenate([a2, row2], axis=0), xor_pairs(1))
    return part(2, (a2, row2, core2), sums, squares)


def live_part(
    x,
    norm_gain,
    final_gain,
    w_gate,
    w_up,
    w_down,
    lm_head,
    target_ids,
    slot_rows,
    gate_row,
    in_squares,
    where,
    down_at,
    first_id,
    live_rows,
    slots,
):
    cols = x.shape[1]
    *picked_rows, x_live = dispatch(slot_rows, x, norm_gain, slots, live_rows)
    own_slot = slot_rows[0][None, :] == jnp.arange(slots, dtype=jnp.int32)[:, None]
    gate_slot = jnp.sum(jnp.where(own_slot, gate_row, 0.0), axis=1, keepdims=True)
    packed = slot_rows[4]
    live_at = packed[None, :] == jnp.arange(live_rows, dtype=jnp.int32)[:, None]
    slot_live = jnp.stack(
        [
            jnp.sum(jnp.where(live_at, slot_rows[(4 - k) % 4][None, :] + 1, 0), axis=1) - 1
            for k in range(4)
        ],
        axis=1,
    )
    local_ids = (
        jnp.sum(jnp.where(live_at, target_ids[None, :], 0), axis=1, keepdims=True) - first_id
    )

    def hidden_step(group, blocks, sums, squares):
        inv = None
        if squares is not None:
            scale = 1.0 / jnp.sqrt(squares / D + epsilon)
            inv = jnp.sum(jnp.where(own_slot, scale[None, :], 0.0), axis=1, keepdims=True)
        return hidden_part(where[group], blocks, slots, w_gate, w_up, sums, inv)

    hidden = spread(picked_rows, in_squares, hidden_step)

    two = 2 * slots
    own_a, row_a, core_a, own_b, row_b, core_b = down_all(
        down_at, hidden, w_down, gate_slot, cols
    )
    heard_a = send(core_a, xor_pairs(1))
    heard_b = send(core_b, xor_pairs(1))
    across_a = (row_a + heard_a[two:].astype(F32)).astype(BF)
    crossed_a = send(across_a, xor_pairs(2))
    total_a = (own_a + heard_a[:two].astype(F32) + crossed_a.astype(F32)).astype(BF)
    part2 = send(total_a[:slots], plane_pairs(2))
    part1 = send(total_a[slots:], plane_pairs(1))
    across_b = (row_b + heard_b[two:].astype(F32)).astype(BF)
    crossed_b = send(after(across_b, crossed_a), xor_pairs(2))
    total_b = (own_b + heard_b[:two].astype(F32) + crossed_b.astype(F32)).astype(BF)
    part3 = send(total_b[:slots], plane_pairs(3))
    parts = (total_b[slots:], part2, part1, part3)

    scaled, squares = mix(slot_live, x_live, final_gain, parts)

    def vocab_step(group, blocks, sums, squares):
        inv = None
        if squares is not None:
            inv = (1.0 / jnp.sqrt(squares / D + epsilon))[:, None]
        return vocab_part(where[group], blocks, live_rows, lm_head, sums, inv, local_ids)

    stats = spread([scaled] * 4, squares.reshape(-1), vocab_step)
    spot = packed[:, None] == jnp.arange(live_rows, dtype=jnp.int32)[None, :]
    return jnp.stack(
        [jnp.sum(jnp.where(spot, stats[:, j][None, :], 0.0), axis=1) for j in range(3)]
    )


def fast_body(
    residual_in,
    norm_gain,
    final_gain,
    expert_ids,
    gate_values,
    w_gate,
    w_up,
    w_down,
    lm_head,
    target_ids,
    lengths,
):
    tokens = residual_in.shape[0]
    devices = lax.axis_size("tensor")
    me = lax.axis_index("tensor").astype(jnp.int32)
    plane, row, core = me >> 2, (me >> 1) & 1, me & 1
    slot_rows, gate_row, need = route(plane, lengths, expert_ids.T, gate_values.T)
    need = jnp.maximum(need, lax.ppermute(need, "groups", [(0, 1), (1, 0)]))

    at = [row * 2 + core, (1 - row) * 2 + core, row * 2 + 1 - core, (1 - row) * 2 + 1 - core]
    planes = [(plane + k) & 3 for k in range(4)]
    where = [jnp.stack(at + [planes[(4 - k) % 4] for k in group]) for group in CHUNKS]
    down_at = jnp.stack(at + [planes[k] for k in (2, 1, 3, 0)])
    stream = residual_in.astype(F32)
    in_squares = jnp.sum(stream * stream, axis=1)

    stats = lax.switch(
        need[0, 0].astype(jnp.int32),
        [
            functools.partial(live_part, live_rows=rows, slots=slots)
            for rows, slots in TIERS + ((tokens, CAP),)
        ],
        residual_in,
        norm_gain[None, :],
        final_gain[None, :],
        w_gate,
        w_up,
        w_down,
        lm_head,
        target_ids,
        slot_rows,
        gate_row,
        in_squares,
        where,
        down_at,
        me * lm_head.shape[1],
    )
    rows_dev = tokens // devices
    stats = stats.reshape(3, devices, rows_dev).transpose(1, 0, 2)
    stats = lax.all_to_all(stats, "tensor", 0, 0, tiled=True)
    top = jnp.max(stats[:, 0], axis=0)
    total = jnp.sum(stats[:, 1] * jnp.exp(stats[:, 0] - top[None, :]), axis=0)
    logprob = jnp.sum(stats[:, 2], axis=0) - top - jnp.log(total)
    own_live = lax.dynamic_slice_in_dim(slot_rows[4], me * rows_dev, rows_dev) >= 0
    return jnp.where(own_live, logprob, 0.0)


def body(*args):
    if lax.axis_size("tensor") == 16 and lax.axis_size("groups") == 2:
        return fast_body(*args)
    return plain_body(*args)


def solution(mesh):
    return jax.shard_map(
        body,
        mesh=mesh,
        in_specs=(
            P("groups", "tensor"),
            P("tensor"),
            P("tensor"),
            P("groups", None),
            P("groups", None),
            P(None, "tensor"),
            P(None, "tensor"),
            P("tensor", None),
            P(None, "tensor"),
            P("groups"),
            P("groups"),
        ),
        out_specs=P(("groups", "tensor")),
        check_vma=False,
    )
```

```python
import functools
import jax
import jax.numpy as jnp
from jax import lax
from jax.experimental import pallas as pl
from jax.experimental.pallas import tpu as pltpu
from jax.sharding import PartitionSpec as P

D = 6144
EXPERTS = 4
EXP_FF = 8192
TOP = 2
SEQ = 64
CAP = 384


epsilon = 1e-05


def combined_all(array, axis, combine):
    everything = jax.tree.map(lambda part: lax.all_gather(part, axis), array)
    leading = jax.tree.map(lambda part: part[0], everything)

    def hop(k, so_far):
        return combine(so_far, jax.tree.map(lambda part: part[k], everything))

    return lax.fori_loop(1, lax.axis_size(axis), hop, leading)


def slots_of(expert_ids):
    flat_ids = expert_ids.reshape(-1)
    pairs = jnp.arange(flat_ids.shape[0], dtype=jnp.int32)
    before = (pairs[None, :] < pairs[:, None]) & (flat_ids[None, :] == flat_ids[:, None])
    return jnp.sum(before.astype(jnp.int32), axis=1).reshape(expert_ids.shape)


def slot_tokens(expert_ids, slot_index):
    slot_code = (expert_ids * CAP + slot_index).reshape(-1)
    owner = jnp.arange(slot_code.shape[0], dtype=jnp.int32) // TOP
    wanted = jnp.arange(EXPERTS * CAP, dtype=jnp.int32)
    matches = slot_code[None, :] == wanted[:, None]
    return jnp.sum(jnp.where(matches, owner[None, :] + 1, 0), axis=1) - 1


def normalize(values, squares_total, gain_vec):
    return (
        values / jnp.sqrt(squares_total[:, None] / D + epsilon) * gain_vec.astype(jnp.float32)
    ).astype(jnp.bfloat16)


def plain_body(
    residual_in,
    norm_gain,
    final_gain,
    expert_ids,
    gate_values,
    w_gate,
    w_up,
    w_down,
    lm_head,
    target_ids,
    lengths,
):
    tokens, feature_cols = residual_in.shape
    hidden_dev = w_gate.shape[1]
    per_expert = EXP_FF // hidden_dev
    expert_now = lax.axis_index("tensor") // per_expert
    stream = residual_in.astype(jnp.float32)
    in_total = lax.psum(jnp.sum(stream * stream, axis=1), "tensor")
    normed = normalize(stream, in_total, norm_gain)
    slot_index = slots_of(expert_ids)
    token_of = slot_tokens(expert_ids, slot_index)
    zero_bf = jnp.zeros((), jnp.bfloat16)
    own_slots = lax.dynamic_slice_in_dim(token_of, expert_now * CAP, CAP)
    occupied = own_slots >= 0
    safe_index = jnp.maximum(own_slots, 0)
    slot_rows = jnp.where(
        occupied[:, None], lax.all_gather(normed, "tensor", axis=1, tiled=True)[safe_index], zero_bf
    )
    gate_out = jnp.dot(slot_rows, w_gate, preferred_element_type=jnp.float32)
    up_out = jnp.dot(slot_rows, w_up, preferred_element_type=jnp.float32)
    hidden = (jax.nn.silu(gate_out) * up_out).astype(jnp.bfloat16)
    partial_value = jnp.dot(hidden, w_down, preferred_element_type=jnp.float32)
    weight_own = jnp.where(expert_ids == expert_now, gate_values, jnp.zeros_like(gate_values))
    weighted = (
        weight_own[:, 0:1] * partial_value[slot_index[:, 0]]
        + weight_own[:, 1:2] * partial_value[slot_index[:, 1]]
    )
    moe_cols = lax.psum_scatter(weighted, "tensor", scatter_dimension=1, tiled=True)
    mixture = stream + moe_cols
    out_total = lax.psum(jnp.sum(mixture * mixture, axis=1), "tensor")
    normed_out = normalize(mixture, out_total, final_gain)
    vocab_dev = lm_head.shape[1]
    logits = jnp.dot(
        lax.all_gather(normed_out, "tensor", axis=1, tiled=True),
        lm_head,
        preferred_element_type=jnp.float32,
    )
    row_max = jnp.max(logits, axis=1)
    row_total = jnp.sum(jnp.exp(logits - row_max[:, None]), axis=1)
    local_ids = target_ids - lax.axis_index("tensor") * vocab_dev
    vocab_cols = jnp.arange(vocab_dev, dtype=jnp.int32)
    picked = jnp.sum(jnp.where(vocab_cols[None, :] == local_ids[:, None], logits, 0.0), axis=1)

    def joined(earlier, later):
        merged_max = jnp.maximum(earlier[0], later[0])
        merged_total = earlier[1] * jnp.exp(earlier[0] - merged_max) + later[1] * jnp.exp(
            later[0] - merged_max
        )
        return (merged_max, merged_total, earlier[2] + later[2])

    merged_max, merged_total, target_logit = combined_all(
        (row_max, row_total, picked), "tensor", joined
    )
    logprob = target_logit - merged_max - jnp.log(merged_total)
    rows_dev = tokens // lax.axis_size("tensor")
    first_row = lax.axis_index("tensor") * rows_dev
    own_rows = lax.dynamic_slice_in_dim(logprob, first_row, rows_dev)
    position = first_row + jnp.arange(rows_dev, dtype=jnp.int32)
    in_length = position % SEQ < lengths[position // SEQ]
    return jnp.where(in_length, own_rows, jnp.zeros_like(own_rows)).astype(jnp.float32)

TIERS = ((288, 224), (352, 272))
CHUNKS = ((0,), (1, 3), (2,))
VMEM = pl.BlockSpec(memory_space=pltpu.VMEM)
BF = jnp.bfloat16
F32 = jnp.float32


def send(array, pairs):
    return lax.ppermute(array, "tensor", pairs)


def xor_pairs(mask):
    return [(i, i ^ mask) for i in range(16)]


def plane_pairs(k):
    return [(i, ((i >> 2) + k) % 4 * 4 + (i & 3)) for i in range(16)]


def after(value, *others):
    return lax.optimization_barrier((value, *others))[0]


def params(mebibytes):
    return pltpu.CompilerParams(vmem_limit_bytes=mebibytes * 1024 * 1024)


def load_kernel(w_ref, after_ref, out_ref, token_ref, sem):
    copy = pltpu.make_async_copy(w_ref, out_ref, sem)
    copy.start()
    copy.wait()
    token_ref[...] = jnp.zeros_like(token_ref)


def resident(weight, ready):
    weight = pltpu.with_memory_space_constraint(weight, pltpu.HBM)
    return pl.pallas_call(
        load_kernel,
        in_specs=[pl.BlockSpec(memory_space=pltpu.HBM), pl.BlockSpec(memory_space=pl.ANY)],
        out_specs=[VMEM, VMEM],
        out_shape=[
            pltpu.VMEM(weight.shape, weight.dtype),
            jax.ShapeDtypeStruct((8, 128), F32),
        ],
        scratch_shapes=[pltpu.SemaphoreType.DMA],
        compiler_params=params(1),
        cost_estimate=pl.CostEstimate(
            flops=0, transcendentals=0, bytes_accessed=4 * weight.size
        ),
    )(weight, ready)


def cost(rows, inner, cols, other_bytes):
    return pl.CostEstimate(
        flops=2 * rows * inner * cols,
        transcendentals=0,
        bytes_accessed=2 * inner * cols + other_bytes,
    )


def route_kernel(where_ref, lengths_ref, ids_ref, gates_ref, slots_ref, gate_ref, need_ref, used_ref):
    tokens = ids_ref.shape[1]
    spot = lax.broadcasted_iota(jnp.int32, (1, tokens), 1)
    cand = lax.shift_right_logical(spot, SEQ.bit_length() - 1)
    size = jnp.zeros_like(spot)
    start = jnp.zeros_like(spot)
    alive = jnp.int32(0)
    for c in range(lengths_ref.shape[0]):
        size = jnp.where(cand == c, lengths_ref[c], size)
        start = jnp.where(cand == c, alive, start)
        alive = alive + lengths_ref[c]
    step = spot - cand * SEQ
    live = step < size
    used_ref[...] = jnp.zeros_like(used_ref)
    for k in range(EXPERTS):
        expert = lax.rem(where_ref[0] + k, EXPERTS)
        first = (ids_ref[0:1, :] == expert) & live
        second = (ids_ref[1:2, :] == expert) & live
        used_ref[k : k + 1, :] = jnp.where(first | second, 1.0, 0.0)
        if k == 0:
            gate_ref[...] = jnp.where(first, gates_ref[0:1, :], 0.0) + jnp.where(
                second, gates_ref[1:2, :], 0.0
            )
    used = used_ref[...]
    source = lax.broadcasted_iota(jnp.int32, (tokens, tokens), 0)
    target = lax.broadcasted_iota(jnp.int32, (tokens, tokens), 1)
    earlier = jnp.where(source < target, 1.0, 0.0).astype(BF)
    rank = jnp.dot(used.astype(BF), earlier, preferred_element_type=F32)
    slots_ref[...] = jnp.where(used > 0.0, rank.astype(jnp.int32), -1)
    slots_ref[4:5, :] = jnp.where(live, start + step, -1)
    fullest = jnp.max(jnp.sum(used, axis=1, keepdims=True))
    need = jnp.float32(0.0)
    for rows, slots in TIERS:
        over = (alive > rows) | (fullest > float(slots))
        need = need + jnp.where(over, 1.0, 0.0)
    need_ref[...] = jnp.full(need_ref.shape, need, F32)


def route(plane, lengths, ids, gates):
    tokens = ids.shape[1]
    smem = pl.BlockSpec(memory_space=pltpu.SMEM)
    vmem = pl.BlockSpec(memory_space=pltpu.VMEM)
    return pl.pallas_call(
        route_kernel,
        in_specs=[smem, smem, vmem, vmem],
        out_specs=[vmem] * 3,
        out_shape=[
            jax.ShapeDtypeStruct((8, tokens), jnp.int32),
            jax.ShapeDtypeStruct((1, tokens), F32),
            jax.ShapeDtypeStruct((8, 128), F32),
        ],
        scratch_shapes=[pltpu.VMEM((8, tokens), F32)],
        compiler_params=params(16),
    )(plane.reshape(1), lengths, ids, gates)


def dispatch_kernel(slot_ref, x_ref, gain_ref, s0, s1, s2, s3, xc_ref):
    x = x_ref[...]
    scaled = (x.astype(F32) * gain_ref[...].astype(F32)).astype(BF)
    tokens = x.shape[0]
    for k, out in enumerate((s0, s1, s2, s3)):
        rows = out.shape[0]
        spots = lax.broadcasted_iota(jnp.int32, (rows, tokens), 0)
        chosen = jnp.where(slot_ref[k : k + 1, :] == spots, 1.0, 0.0).astype(BF)
        out[...] = jnp.dot(chosen, scaled, preferred_element_type=F32).astype(BF)
    rows = xc_ref.shape[0]
    spots = lax.broadcasted_iota(jnp.int32, (rows, tokens), 0)
    chosen = jnp.where(slot_ref[4:5, :] == spots, 1.0, 0.0).astype(BF)
    xc_ref[...] = jnp.dot(chosen, x, preferred_element_type=F32).astype(BF)


def dispatch(slot_rows, x, gain, slots, live_rows):
    cols = x.shape[1]
    block = jax.ShapeDtypeStruct((slots, cols), BF)
    return pl.pallas_call(
        dispatch_kernel,
        out_shape=[block] * 4 + [jax.ShapeDtypeStruct((live_rows, cols), BF)],
        compiler_params=params(16),
    )(slot_rows, x, gain)


def place(where_ref, blocks, wide_ref):
    own, across, *core = blocks
    rows, cols = wide_ref.shape[0], own.shape[1]
    count = own.shape[0] // rows
    for g in range(count):
        pieces = ((own, g), (across, g), (core[0], g), (core[-1], g if len(core) == 2 else count + g))
        for quarter, (block, piece) in enumerate(pieces):
            at = pl.multiple_of((g * 4 + where_ref[quarter]) * cols, 128)
            wide_ref[:, pl.ds(at, cols)] = block[piece * rows : (piece + 1) * rows, :]


def whole_specs(arrays):
    return [pl.BlockSpec(array.shape, lambda n, w: (0, 0)) for array in arrays]


def product(wide, weights):
    depth = weights[0].shape[0]
    value = None
    for j, w in enumerate(weights):
        part = jnp.dot(
            wide[:, j * depth : (j + 1) * depth], w[...], preferred_element_type=F32
        )
        value = part if value is None else value + part
    return value


def resident_product(where_ref, wide, weight, n, tile):
    depth = weight.shape[0] // 4
    value = None
    for j in range(wide.shape[1] // depth):
        first = pl.multiple_of(where_ref[4 + j] * depth, 128)
        part = jnp.dot(
            wide[:, j * depth : (j + 1) * depth],
            weight[pl.ds(first, depth), pl.ds(pl.multiple_of(n * tile, 128), tile)],
            preferred_element_type=F32,
        )
        value = part if value is None else value + part
    return value


def weight_specs(count, depth, tile):
    return [
        pl.BlockSpec((depth, tile), functools.partial(lambda j, n, w: (w[4 + j], n), j))
        for j in range(count)
    ]


def by_slot(slot_ref, values, slots):
    spots = lax.broadcasted_iota(jnp.int32, (slots, slot_ref.shape[1]), 0)
    chosen = jnp.where(slot_ref[0:1, :] == spots, values, 0.0)
    return jnp.sum(chosen, axis=1, keepdims=True)


def hidden_kernel(given, count, first, last, where_ref, *refs):
    blocks, refs = refs[:given], refs[given:]
    wg, wu, refs = refs[0], refs[1 : 1 + count], refs[1 + count :]
    if not first:
        g_in, u_in, refs = refs[0], refs[1], refs[2:]
    if last:
        slot_ref, squares_ref, h_out, wide, inv = refs
    else:
        g_out, u_out, wide = refs
    n = pl.program_id(0)
    tile = wu[0].shape[1]

    @pl.when(n == 0)
    def _():
        place(where_ref, blocks, wide)
        if last:
            scale = 1.0 / jnp.sqrt(squares_ref[...] / D + epsilon)
            inv[...] = by_slot(slot_ref, scale, inv.shape[0])

    g = resident_product(where_ref, wide, wg, n, tile)
    u = product(wide, wu)
    at = pl.ds(pl.multiple_of(n * tile, 128), tile)
    if not first:
        g = g + g_in[:, at]
        u = u + u_in[:, at]
    if last:
        g = g * inv[...]
        u = u * inv[...]
        h_out[...] = (g / (1.0 + jnp.exp(-g)) * u).astype(BF)
    else:
        g_out[:, at] = g
        u_out[:, at] = u


def hidden_part(where, blocks, slots, w_gate, w_up, sums, rows_of):
    cols = blocks[0].shape[1]
    count = blocks[0].shape[0] // slots
    inner, width = w_up.shape
    tile, depth = 256, inner // 4
    first, last = sums is None, rows_of is not None
    w_gate = pltpu.with_memory_space_constraint(w_gate, pltpu.VMEM)
    w_up = pltpu.with_memory_space_constraint(w_up, pltpu.HBM)
    ins = [where, *blocks, w_gate] + [w_up] * count
    specs = whole_specs(blocks) + [VMEM] + weight_specs(count, depth, tile)
    aliases = {}
    if not first:
        if not last:
            aliases = {len(ins): 0, len(ins) + 1: 1}
        ins += [pltpu.with_memory_space_constraint(part, pltpu.VMEM) for part in sums]
        specs += [VMEM] * 2
    if last:
        ins += rows_of
        specs += whole_specs(rows_of)
        outs = jax.ShapeDtypeStruct((slots, width), BF)
        out_specs = pl.BlockSpec((slots, tile), lambda n, w: (0, n))
    else:
        outs, out_specs = [pltpu.VMEM((slots, width), F32)] * 2, [VMEM] * 2
    return pl.pallas_call(
        functools.partial(hidden_kernel, len(blocks), count, first, last),
        out_shape=outs,
        grid_spec=pltpu.PrefetchScalarGridSpec(
            num_scalar_prefetch=1,
            grid=(width // tile,),
            in_specs=specs,
            out_specs=out_specs,
            scratch_shapes=[pltpu.VMEM((slots, 4 * count * cols), BF)]
            + [pltpu.VMEM((slots, 1), F32)] * last,
        ),
        input_output_aliases=aliases,
        compiler_params=params(30),
        cost_estimate=cost(slots, 8 if first else count * depth, 2 * width, 0),
    )(*ins)


def down_kernel(where_ref, h_ref, w_ref, slot_ref, row_ref, *refs):
    *outs, total, gate_ref = refs
    rows = h_ref.shape[0]
    half = w_ref.shape[1]
    step = pl.program_id(0)

    @pl.when(step == 0)
    def _():
        gate_ref[...] = by_slot(slot_ref, row_ref[...], rows)

    value = jnp.dot(h_ref[...], w_ref[...], preferred_element_type=F32) * gate_ref[...]
    total[:, pl.ds(pl.multiple_of(lax.rem(step, 2) * half, 128), half)] = value
    for c in range(4):
        own, across, core = outs[3 * (c // 2) : 3 * (c // 2) + 3]
        g = c % 2

        @pl.when(step == 2 * c + 1)
        def _():
            cols = own.shape[1]
            for b in range(4):
                part = total[:, pl.ds(pl.multiple_of(where_ref[b] * cols, 128), cols)]
                if b < 2:
                    (own, across)[b][g * rows : (g + 1) * rows, :] = part
                else:
                    first = ((b - 2) * 2 + g) * rows
                    core[first : first + rows, :] = part.astype(BF)


def down_all(where, hidden, w_down, slot_rows, gate_row, cols):
    rows, inner = hidden.shape
    sizes = ((2 * rows, F32), (2 * rows, F32), (4 * rows, BF)) * 2
    return pl.pallas_call(
        down_kernel,
        out_shape=[jax.ShapeDtypeStruct((count, cols), kind) for count, kind in sizes],
        grid_spec=pltpu.PrefetchScalarGridSpec(
            num_scalar_prefetch=1,
            grid=(8,),
            in_specs=[
                pl.BlockSpec((rows, inner), lambda j, w: (0, 0)),
                pl.BlockSpec((inner, 2 * cols), lambda j, w: (0, w[4 + j // 2] * 2 + j % 2)),
                *whole_specs([slot_rows, gate_row]),
            ],
            out_specs=[pl.BlockSpec((count, cols), lambda j, w: (0, 0)) for count, _ in sizes],
            scratch_shapes=[pltpu.VMEM((rows, 4 * cols), F32), pltpu.VMEM((rows, 1), F32)],
        ),
        compiler_params=params(40),
        cost_estimate=cost(rows, inner, 16 * cols, 64 * rows * cols),
    )(where, hidden, w_down, slot_rows, gate_row)


def mix_kernel(slot_ref, x_ref, gain_ref, e0, e2, e1, e3, out_ref, squares_ref):
    rows = x_ref.shape[0]
    mixture = x_ref[...].astype(F32)
    moe = jnp.zeros_like(mixture)
    for j, part in enumerate((e0, e1, e2, e3)):
        slots = part.shape[0]
        spots = lax.broadcasted_iota(jnp.int32, (rows, slots), 1)
        chosen = jnp.where(slot_ref[:, j : j + 1] == spots, 1.0, 0.0).astype(BF)
        moe = moe + jnp.dot(chosen, part[...], preferred_element_type=F32)
    mixture = mixture + moe
    out_ref[...] = (mixture * gain_ref[...].astype(F32)).astype(BF)
    squares_ref[...] = jnp.sum(mixture * mixture, axis=1, keepdims=True)


def mix(slot_cols, x, gain, parts):
    rows, cols = x.shape
    return pl.pallas_call(
        mix_kernel,
        out_shape=[
            jax.ShapeDtypeStruct((rows, cols), BF),
            jax.ShapeDtypeStruct((rows, 1), F32),
        ],
        compiler_params=params(16),
    )(slot_cols, x, gain, *parts)


def vocab_kernel(given, count, first, last, tile, where_ref, *refs):
    blocks, refs = refs[:given], refs[given:]
    weight, refs = refs[0], refs[1:]
    if not first:
        sum_in, refs = refs[0], refs[1:]
    if last:
        inv, local_ids, out, wide, top, total, picked = refs
    else:
        out, wide = refs
    n = pl.program_id(0)

    @pl.when(n == 0)
    def _():
        place(where_ref, blocks, wide)

    value = resident_product(where_ref, wide, weight, n, tile)
    at = pl.ds(pl.multiple_of(n * tile, 128), tile)
    if not first:
        value = value + sum_in[:, at]
    if not last:
        out[:, at] = value
        return
    logits = value * (1.0 / jnp.sqrt(inv[...] / D + epsilon))
    column = n * tile + lax.broadcasted_iota(jnp.int32, logits.shape, 1)
    tile_pick = jnp.sum(jnp.where(column == local_ids[...], logits, 0.0), axis=1, keepdims=True)
    tile_top = jnp.max(logits, axis=1, keepdims=True)

    @pl.when(n == 0)
    def _():
        top[...] = tile_top
        total[...] = jnp.sum(jnp.exp(logits - tile_top), axis=1, keepdims=True)
        picked[...] = tile_pick

    @pl.when(n > 0)
    def _():
        new_top = jnp.maximum(top[...], tile_top)
        total[...] = total[...] * jnp.exp(top[...] - new_top) + jnp.sum(
            jnp.exp(logits - new_top), axis=1, keepdims=True
        )
        top[...] = new_top
        picked[...] = picked[...] + tile_pick

    @pl.when(n == pl.num_programs(0) - 1)
    def _():
        lane = lax.broadcasted_iota(jnp.int32, out.shape, 1)
        out[...] = jnp.where(lane == 0, top[...], jnp.where(lane == 1, total[...], picked[...]))


def vocab_part(where, blocks, rows, lm_head, sums, inv, local_ids):
    cols = blocks[0].shape[1]
    count = blocks[0].shape[0] // rows
    inner, width = lm_head.shape
    tile = 512 if rows <= 352 else 256
    first, last = sums is None, inv is not None
    lm_head = pltpu.with_memory_space_constraint(lm_head, pltpu.VMEM)
    ins = [where, *blocks, lm_head]
    specs = whole_specs(blocks) + [VMEM]
    aliases = {}
    if not first:
        if not last:
            aliases = {len(ins): 0}
        ins.append(pltpu.with_memory_space_constraint(sums, pltpu.VMEM))
        specs.append(VMEM)
    scratch = [pltpu.VMEM((rows, 4 * count * cols), BF)]
    if last:
        ins += [inv, local_ids]
        specs += whole_specs([inv, local_ids])
        outs = jax.ShapeDtypeStruct((rows, 128), F32)
        out_specs = pl.BlockSpec((rows, 128), lambda n, w: (0, 0))
        scratch += [pltpu.VMEM((rows, 1), F32)] * 3
    else:
        outs, out_specs = pltpu.VMEM((rows, width), F32), VMEM
    return pl.pallas_call(
        functools.partial(vocab_kernel, len(blocks), count, first, last, tile),
        out_shape=outs,
        grid_spec=pltpu.PrefetchScalarGridSpec(
            num_scalar_prefetch=1,
            grid=(width // tile,),
            in_specs=specs,
            out_specs=out_specs,
            scratch_shapes=scratch,
        ),
        input_output_aliases=aliases,
        compiler_params=params(32),
        cost_estimate=cost(rows, 8 if first else inner * count // 4, width, 0),
    )(*ins)


def spread(by_offset, squares, load, part):
    own0 = by_offset[0]
    a1 = send(by_offset[1], plane_pairs(1))
    a3 = send(by_offset[3], plane_pairs(3))
    row0 = send(own0, xor_pairs(2))
    core0 = send(own0, xor_pairs(1))
    diagonal0 = send(own0, xor_pairs(3))
    squares = squares + send(squares, xor_pairs(1))
    squares = squares + send(squares, xor_pairs(2))

    near = jnp.concatenate([a1, a3], axis=0)
    row0, core0, diagonal0, near, squares, far = lax.optimization_barrier(
        (row0, core0, diagonal0, near, squares, by_offset[2])
    )
    a2 = send(far, plane_pairs(2))
    row13 = send(near, xor_pairs(2))
    weight = load(squares)
    sums = part(0, weight, (own0, row0, core0, diagonal0), None, None)

    a2, row13, squares, sums = lax.optimization_barrier((a2, row13, squares, sums))
    row2 = send(a2, xor_pairs(2))
    core13 = send(jnp.concatenate([near, row13], axis=0), xor_pairs(1))
    squares = squares + send(squares, xor_pairs(4))
    squares = squares + send(squares, xor_pairs(8))
    sums = part(1, weight, (near, row13, core13), sums, None)

    row2, squares, sums = lax.optimization_barrier((row2, squares, sums))
    core2 = send(jnp.concatenate([a2, row2], axis=0), xor_pairs(1))
    return part(2, weight, (a2, row2, core2), sums, squares)


def live_part(
    x,
    norm_gain,
    final_gain,
    w_gate,
    w_up,
    w_down,
    lm_head,
    target_ids,
    slot_rows,
    gate_row,
    in_squares,
    where,
    down_at,
    first_id,
    live_rows,
    slots,
):
    cols = x.shape[1]
    *picked_rows, x_live = dispatch(slot_rows, x, norm_gain, slots, live_rows)
    packed = slot_rows[4]
    live_at = packed[None, :] == jnp.arange(live_rows, dtype=jnp.int32)[:, None]
    slot_live = jnp.stack(
        [
            jnp.sum(jnp.where(live_at, slot_rows[(4 - k) % 4][None, :] + 1, 0), axis=1) - 1
            for k in range(4)
        ],
        axis=1,
    )
    local_ids = (
        jnp.sum(jnp.where(live_at, target_ids[None, :], 0), axis=1, keepdims=True) - first_id
    )

    def hidden_step(group, weight, blocks, sums, squares):
        rows_of = None if squares is None else [slot_rows, squares]
        return hidden_part(where[group], blocks, slots, weight, w_up, sums, rows_of)

    hidden = spread(
        picked_rows, in_squares, lambda ready: resident(w_gate, ready)[0], hidden_step
    )

    two = 2 * slots
    own_a, row_a, core_a, own_b, row_b, core_b = down_all(
        down_at, hidden, w_down, slot_rows, gate_row, cols
    )
    heard_a = send(core_a, xor_pairs(1))
    heard_b = send(core_b, xor_pairs(1))
    across_a = (row_a + heard_a[two:].astype(F32)).astype(BF)
    crossed_a = send(across_a, xor_pairs(2))
    head, token = resident(lm_head, across_a)
    crossed_a, token = lax.optimization_barrier((crossed_a, token))
    total_a = (own_a + heard_a[:two].astype(F32) + crossed_a.astype(F32)).astype(BF)
    part2 = send(total_a[:slots], plane_pairs(2))
    part1 = send(total_a[slots:], plane_pairs(1))
    across_b = (row_b + heard_b[two:].astype(F32)).astype(BF)
    crossed_b = send(after(across_b, crossed_a), xor_pairs(2))
    total_b = (own_b + heard_b[:two].astype(F32) + crossed_b.astype(F32)).astype(BF)
    part3 = send(total_b[:slots], plane_pairs(3))
    parts = (total_b[slots:], part2, part1, part3)

    scaled, squares = mix(slot_live, x_live, final_gain, parts)

    def vocab_step(group, weight, blocks, sums, squares):
        return vocab_part(where[group], blocks, live_rows, weight, sums, squares, local_ids)

    stats = spread([scaled] * 4, squares, lambda ready: head, vocab_step)
    spot = packed[:, None] == jnp.arange(live_rows, dtype=jnp.int32)[None, :]
    return jnp.stack(
        [jnp.sum(jnp.where(spot, stats[:, j][None, :], 0.0), axis=1) for j in range(3)]
    )


def fast_body(
    residual_in,
    norm_gain,
    final_gain,
    expert_ids,
    gate_values,
    w_gate,
    w_up,
    w_down,
    lm_head,
    target_ids,
    lengths,
):
    tokens = residual_in.shape[0]
    devices = lax.axis_size("tensor")
    me = lax.axis_index("tensor").astype(jnp.int32)
    plane, row, core = me >> 2, (me >> 1) & 1, me & 1
    slot_rows, gate_row, need = route(plane, lengths, expert_ids.T, gate_values.T)
    need = jnp.maximum(need, lax.ppermute(need, "groups", [(0, 1), (1, 0)]))

    at = [row * 2 + core, (1 - row) * 2 + core, row * 2 + 1 - core, (1 - row) * 2 + 1 - core]
    planes = [(plane + k) & 3 for k in range(4)]
    where = [jnp.stack(at + [planes[(4 - k) % 4] for k in group]) for group in CHUNKS]
    down_at = jnp.stack(at + [planes[k] for k in (2, 1, 3, 0)])
    stream = residual_in.astype(F32)
    in_squares = jnp.sum(stream * stream, axis=1)[None, :]

    stats = lax.switch(
        need[0, 0].astype(jnp.int32),
        [
            functools.partial(live_part, live_rows=rows, slots=slots)
            for rows, slots in TIERS + ((tokens, CAP),)
        ],
        residual_in,
        norm_gain[None, :],
        final_gain[None, :],
        w_gate,
        w_up,
        w_down,
        lm_head,
        target_ids,
        slot_rows,
        gate_row,
        in_squares,
        where,
        down_at,
        me * lm_head.shape[1],
    )
    rows_dev = tokens // devices
    stats = stats.reshape(3, devices, rows_dev).transpose(1, 0, 2)
    stats = lax.all_to_all(stats, "tensor", 0, 0, tiled=True)
    top = jnp.max(stats[:, 0], axis=0)
    total = jnp.sum(stats[:, 1] * jnp.exp(stats[:, 0] - top[None, :]), axis=0)
    logprob = jnp.sum(stats[:, 2], axis=0) - top - jnp.log(total)
    own_live = lax.dynamic_slice_in_dim(slot_rows[4], me * rows_dev, rows_dev) >= 0
    return jnp.where(own_live, logprob, 0.0)


def body(*args):
    if lax.axis_size("tensor") == 16 and lax.axis_size("groups") == 2:
        return fast_body(*args)
    return plain_body(*args)


def solution(mesh):
    return jax.shard_map(
        body,
        mesh=mesh,
        in_specs=(
            P("groups", "tensor"),
            P("tensor"),
            P("tensor"),
            P("groups", None),
            P("groups", None),
            P(None, "tensor"),
            P(None, "tensor"),
            P("tensor", None),
            P(None, "tensor"),
            P("groups"),
            P("groups"),
        ),
        out_specs=P(("groups", "tensor")),
        check_vma=False,
    )
```

```python
import functools
import jax
import jax.numpy as jnp
from jax import lax
from jax.experimental import pallas as pl
from jax.experimental.pallas import tpu as pltpu
from jax.sharding import PartitionSpec as P

D = 6144
EXPERTS = 4
EXP_FF = 8192
TOP = 2
SEQ = 64
CAP = 384


epsilon = 1e-05


def combined_all(array, axis, combine):
    everything = jax.tree.map(lambda part: lax.all_gather(part, axis), array)
    leading = jax.tree.map(lambda part: part[0], everything)

    def hop(k, so_far):
        return combine(so_far, jax.tree.map(lambda part: part[k], everything))

    return lax.fori_loop(1, lax.axis_size(axis), hop, leading)


def slots_of(expert_ids):
    flat_ids = expert_ids.reshape(-1)
    pairs = jnp.arange(flat_ids.shape[0], dtype=jnp.int32)
    before = (pairs[None, :] < pairs[:, None]) & (flat_ids[None, :] == flat_ids[:, None])
    return jnp.sum(before.astype(jnp.int32), axis=1).reshape(expert_ids.shape)


def slot_tokens(expert_ids, slot_index):
    slot_code = (expert_ids * CAP + slot_index).reshape(-1)
    owner = jnp.arange(slot_code.shape[0], dtype=jnp.int32) // TOP
    wanted = jnp.arange(EXPERTS * CAP, dtype=jnp.int32)
    matches = slot_code[None, :] == wanted[:, None]
    return jnp.sum(jnp.where(matches, owner[None, :] + 1, 0), axis=1) - 1


def normalize(values, squares_total, gain_vec):
    return (
        values / jnp.sqrt(squares_total[:, None] / D + epsilon) * gain_vec.astype(jnp.float32)
    ).astype(jnp.bfloat16)


def plain_body(
    residual_in,
    norm_gain,
    final_gain,
    expert_ids,
    gate_values,
    w_gate,
    w_up,
    w_down,
    lm_head,
    target_ids,
    lengths,
):
    tokens, feature_cols = residual_in.shape
    hidden_dev = w_gate.shape[1]
    per_expert = EXP_FF // hidden_dev
    expert_now = lax.axis_index("tensor") // per_expert
    stream = residual_in.astype(jnp.float32)
    in_total = lax.psum(jnp.sum(stream * stream, axis=1), "tensor")
    normed = normalize(stream, in_total, norm_gain)
    slot_index = slots_of(expert_ids)
    token_of = slot_tokens(expert_ids, slot_index)
    zero_bf = jnp.zeros((), jnp.bfloat16)
    own_slots = lax.dynamic_slice_in_dim(token_of, expert_now * CAP, CAP)
    occupied = own_slots >= 0
    safe_index = jnp.maximum(own_slots, 0)
    slot_rows = jnp.where(
        occupied[:, None], lax.all_gather(normed, "tensor", axis=1, tiled=True)[safe_index], zero_bf
    )
    gate_out = jnp.dot(slot_rows, w_gate, preferred_element_type=jnp.float32)
    up_out = jnp.dot(slot_rows, w_up, preferred_element_type=jnp.float32)
    hidden = (jax.nn.silu(gate_out) * up_out).astype(jnp.bfloat16)
    partial_value = jnp.dot(hidden, w_down, preferred_element_type=jnp.float32)
    weight_own = jnp.where(expert_ids == expert_now, gate_values, jnp.zeros_like(gate_values))
    weighted = (
        weight_own[:, 0:1] * partial_value[slot_index[:, 0]]
        + weight_own[:, 1:2] * partial_value[slot_index[:, 1]]
    )
    moe_cols = lax.psum_scatter(weighted, "tensor", scatter_dimension=1, tiled=True)
    mixture = stream + moe_cols
    out_total = lax.psum(jnp.sum(mixture * mixture, axis=1), "tensor")
    normed_out = normalize(mixture, out_total, final_gain)
    vocab_dev = lm_head.shape[1]
    logits = jnp.dot(
        lax.all_gather(normed_out, "tensor", axis=1, tiled=True),
        lm_head,
        preferred_element_type=jnp.float32,
    )
    row_max = jnp.max(logits, axis=1)
    row_total = jnp.sum(jnp.exp(logits - row_max[:, None]), axis=1)
    local_ids = target_ids - lax.axis_index("tensor") * vocab_dev
    vocab_cols = jnp.arange(vocab_dev, dtype=jnp.int32)
    picked = jnp.sum(jnp.where(vocab_cols[None, :] == local_ids[:, None], logits, 0.0), axis=1)

    def joined(earlier, later):
        merged_max = jnp.maximum(earlier[0], later[0])
        merged_total = earlier[1] * jnp.exp(earlier[0] - merged_max) + later[1] * jnp.exp(
            later[0] - merged_max
        )
        return (merged_max, merged_total, earlier[2] + later[2])

    merged_max, merged_total, target_logit = combined_all(
        (row_max, row_total, picked), "tensor", joined
    )
    logprob = target_logit - merged_max - jnp.log(merged_total)
    rows_dev = tokens // lax.axis_size("tensor")
    first_row = lax.axis_index("tensor") * rows_dev
    own_rows = lax.dynamic_slice_in_dim(logprob, first_row, rows_dev)
    position = first_row + jnp.arange(rows_dev, dtype=jnp.int32)
    in_length = position % SEQ < lengths[position // SEQ]
    return jnp.where(in_length, own_rows, jnp.zeros_like(own_rows)).astype(jnp.float32)

TIERS = ((288, 224), (352, 272))
CHUNKS = ((0,), (1, 3), (2,))
VMEM = pl.BlockSpec(memory_space=pltpu.VMEM)
BF = jnp.bfloat16
F32 = jnp.float32


def send(array, pairs):
    return lax.ppermute(array, "tensor", pairs)


def xor_pairs(mask):
    return [(i, i ^ mask) for i in range(16)]


def plane_pairs(k):
    return [(i, ((i >> 2) + k) % 4 * 4 + (i & 3)) for i in range(16)]


def after(value, *others):
    return lax.optimization_barrier((value, *others))[0]


def params(mebibytes):
    return pltpu.CompilerParams(vmem_limit_bytes=mebibytes * 1024 * 1024)


def load_kernel(w_ref, after_ref, out_ref, token_ref, sem):
    copy = pltpu.make_async_copy(w_ref, out_ref, sem)
    copy.start()
    copy.wait()
    token_ref[...] = jnp.zeros_like(token_ref)


def resident(weight, ready):
    weight = pltpu.with_memory_space_constraint(weight, pltpu.HBM)
    return pl.pallas_call(
        load_kernel,
        in_specs=[pl.BlockSpec(memory_space=pltpu.HBM), pl.BlockSpec(memory_space=pl.ANY)],
        out_specs=[VMEM, VMEM],
        out_shape=[
            pltpu.VMEM(weight.shape, weight.dtype),
            jax.ShapeDtypeStruct((8, 128), F32),
        ],
        scratch_shapes=[pltpu.SemaphoreType.DMA],
        compiler_params=params(1),
        cost_estimate=pl.CostEstimate(
            flops=0, transcendentals=0, bytes_accessed=4 * weight.size
        ),
    )(weight, ready)


def cost(rows, inner, cols, other_bytes):
    return pl.CostEstimate(
        flops=2 * rows * inner * cols,
        transcendentals=0,
        bytes_accessed=2 * inner * cols + other_bytes,
    )


def route_kernel(where_ref, lengths_ref, ids_ref, gates_ref, slots_ref, gate_ref, need_ref, used_ref):
    tokens = ids_ref.shape[1]
    spot = lax.broadcasted_iota(jnp.int32, (1, tokens), 1)
    cand = lax.shift_right_logical(spot, SEQ.bit_length() - 1)
    size = jnp.zeros_like(spot)
    start = jnp.zeros_like(spot)
    alive = jnp.int32(0)
    for c in range(lengths_ref.shape[0]):
        size = jnp.where(cand == c, lengths_ref[c], size)
        start = jnp.where(cand == c, alive, start)
        alive = alive + lengths_ref[c]
    step = spot - cand * SEQ
    live = step < size
    used_ref[...] = jnp.zeros_like(used_ref)
    for k in range(EXPERTS):
        expert = lax.rem(where_ref[0] + k, EXPERTS)
        first = (ids_ref[0:1, :] == expert) & live
        second = (ids_ref[1:2, :] == expert) & live
        used_ref[k : k + 1, :] = jnp.where(first | second, 1.0, 0.0)
        if k == 0:
            gate_ref[...] = jnp.where(first, gates_ref[0:1, :], 0.0) + jnp.where(
                second, gates_ref[1:2, :], 0.0
            )
    used = used_ref[...]
    source = lax.broadcasted_iota(jnp.int32, (tokens, tokens), 0)
    target = lax.broadcasted_iota(jnp.int32, (tokens, tokens), 1)
    earlier = jnp.where(source < target, 1.0, 0.0).astype(BF)
    rank = jnp.dot(used.astype(BF), earlier, preferred_element_type=F32)
    slots_ref[...] = jnp.where(used > 0.0, rank.astype(jnp.int32), -1)
    slots_ref[4:5, :] = jnp.where(live, start + step, -1)
    fullest = jnp.max(jnp.sum(used, axis=1, keepdims=True))
    need = jnp.float32(0.0)
    for rows, slots in TIERS:
        over = (alive > rows) | (fullest > float(slots))
        need = need + jnp.where(over, 1.0, 0.0)
    need_ref[...] = jnp.full(need_ref.shape, need, F32)


def route(plane, lengths, ids, gates):
    tokens = ids.shape[1]
    smem = pl.BlockSpec(memory_space=pltpu.SMEM)
    vmem = pl.BlockSpec(memory_space=pltpu.VMEM)
    return pl.pallas_call(
        route_kernel,
        in_specs=[smem, smem, vmem, vmem],
        out_specs=[vmem] * 3,
        out_shape=[
            jax.ShapeDtypeStruct((8, tokens), jnp.int32),
            jax.ShapeDtypeStruct((1, tokens), F32),
            jax.ShapeDtypeStruct((8, 128), F32),
        ],
        scratch_shapes=[pltpu.VMEM((8, tokens), F32)],
        compiler_params=params(16),
    )(plane.reshape(1), lengths, ids, gates)


def dispatch_kernel(slot_ref, x_ref, gain_ref, s0, s1, s2, s3, xc_ref):
    x = x_ref[...]
    scaled = (x.astype(F32) * gain_ref[...].astype(F32)).astype(BF)
    tokens = x.shape[0]
    for k, out in enumerate((s0, s1, s2, s3)):
        rows = out.shape[0]
        spots = lax.broadcasted_iota(jnp.int32, (rows, tokens), 0)
        chosen = jnp.where(slot_ref[k : k + 1, :] == spots, 1.0, 0.0).astype(BF)
        out[...] = jnp.dot(chosen, scaled, preferred_element_type=F32).astype(BF)
    rows = xc_ref.shape[0]
    spots = lax.broadcasted_iota(jnp.int32, (rows, tokens), 0)
    chosen = jnp.where(slot_ref[4:5, :] == spots, 1.0, 0.0).astype(BF)
    xc_ref[...] = jnp.dot(chosen, x, preferred_element_type=F32).astype(BF)


def dispatch(slot_rows, x, gain, slots, live_rows):
    cols = x.shape[1]
    block = jax.ShapeDtypeStruct((slots, cols), BF)
    return pl.pallas_call(
        dispatch_kernel,
        out_shape=[block] * 4 + [jax.ShapeDtypeStruct((live_rows, cols), BF)],
        compiler_params=params(16),
    )(slot_rows, x, gain)


def place(where_ref, blocks, wide_ref):
    own, across, *core = blocks
    rows, cols = wide_ref.shape[0], own.shape[1]
    count = own.shape[0] // rows
    for g in range(count):
        pieces = ((own, g), (across, g), (core[0], g), (core[-1], g if len(core) == 2 else count + g))
        for quarter, (block, piece) in enumerate(pieces):
            at = pl.multiple_of((g * 4 + where_ref[quarter]) * cols, 128)
            wide_ref[:, pl.ds(at, cols)] = block[piece * rows : (piece + 1) * rows, :]


def whole_specs(arrays):
    return [pl.BlockSpec(array.shape, lambda n, w: (0, 0)) for array in arrays]


def product(wide, weights):
    depth = weights[0].shape[0]
    value = None
    for j, w in enumerate(weights):
        part = jnp.dot(
            wide[:, j * depth : (j + 1) * depth], w[...], preferred_element_type=F32
        )
        value = part if value is None else value + part
    return value


def resident_product(where_ref, wide, weight, n, tile):
    depth = weight.shape[0] // 4
    value = None
    for j in range(wide.shape[1] // depth):
        first = pl.multiple_of(where_ref[4 + j] * depth, 128)
        part = jnp.dot(
            wide[:, j * depth : (j + 1) * depth],
            weight[pl.ds(first, depth), pl.ds(pl.multiple_of(n * tile, 128), tile)],
            preferred_element_type=F32,
        )
        value = part if value is None else value + part
    return value


def weight_specs(count, depth, tile):
    return [
        pl.BlockSpec((depth, tile), functools.partial(lambda j, n, w: (w[4 + j], n), j))
        for j in range(count)
    ]


def by_slot(slot_ref, values, slots):
    spots = lax.broadcasted_iota(jnp.int32, (slots, slot_ref.shape[1]), 0)
    chosen = jnp.where(slot_ref[0:1, :] == spots, values, 0.0)
    return jnp.sum(chosen, axis=1, keepdims=True)


def hidden_kernel(given, count, first, last, where_ref, *refs):
    blocks, refs = refs[:given], refs[given:]
    wg, wu, refs = refs[0], refs[1 : 1 + count], refs[1 + count :]
    if not first:
        g_in, u_in, refs = refs[0], refs[1], refs[2:]
    if last:
        slot_ref, squares_ref, h_out, wide, inv = refs
    else:
        g_out, u_out, wide = refs
    n = pl.program_id(0)
    tile = wu[0].shape[1]

    @pl.when(n == 0)
    def _():
        place(where_ref, blocks, wide)
        if last:
            scale = 1.0 / jnp.sqrt(squares_ref[...] / D + epsilon)
            inv[...] = by_slot(slot_ref, scale, inv.shape[0])

    g = resident_product(where_ref, wide, wg, n, tile)
    u = product(wide, wu)
    at = pl.ds(pl.multiple_of(n * tile, 128), tile)
    if not first:
        g = g + g_in[:, at]
        u = u + u_in[:, at]
    if last:
        g = g * inv[...]
        u = u * inv[...]
        h_out[...] = (g / (1.0 + jnp.exp(-g)) * u).astype(BF)
    else:
        g_out[:, at] = g
        u_out[:, at] = u


def hidden_part(where, blocks, slots, w_gate, w_up, sums, rows_of):
    cols = blocks[0].shape[1]
    count = blocks[0].shape[0] // slots
    inner, width = w_up.shape
    tile, depth = 512 if slots > 272 else 1024, inner // 4
    first, last = sums is None, rows_of is not None
    w_gate = pltpu.with_memory_space_constraint(w_gate, pltpu.VMEM)
    w_up = pltpu.with_memory_space_constraint(w_up, pltpu.HBM)
    ins = [where, *blocks, w_gate] + [w_up] * count
    specs = whole_specs(blocks) + [VMEM] + weight_specs(count, depth, tile)
    aliases = {}
    if not first:
        if not last:
            aliases = {len(ins): 0, len(ins) + 1: 1}
        ins += [pltpu.with_memory_space_constraint(part, pltpu.VMEM) for part in sums]
        specs += [VMEM] * 2
    if last:
        ins += rows_of
        specs += whole_specs(rows_of)
        outs = jax.ShapeDtypeStruct((slots, width), BF)
        out_specs = pl.BlockSpec((slots, tile), lambda n, w: (0, n))
    else:
        outs, out_specs = [pltpu.VMEM((slots, width), F32)] * 2, [VMEM] * 2
    return pl.pallas_call(
        functools.partial(hidden_kernel, len(blocks), count, first, last),
        out_shape=outs,
        grid_spec=pltpu.PrefetchScalarGridSpec(
            num_scalar_prefetch=1,
            grid=(width // tile,),
            in_specs=specs,
            out_specs=out_specs,
            scratch_shapes=[pltpu.VMEM((slots, 4 * count * cols), BF)]
            + [pltpu.VMEM((slots, 1), F32)] * last,
        ),
        input_output_aliases=aliases,
        compiler_params=params(30),
        cost_estimate=cost(slots, 8 if first else count * depth, 2 * width, 0),
    )(*ins)


def down_kernel(where_ref, h_ref, w_ref, slot_ref, row_ref, *refs):
    *outs, total, gate_ref = refs
    rows = h_ref.shape[0]
    step = pl.program_id(0)

    @pl.when(step == 0)
    def _():
        gate_ref[...] = by_slot(slot_ref, row_ref[...], rows)

    value = jnp.dot(h_ref[...], w_ref[...], preferred_element_type=F32) * gate_ref[...]
    total[...] = value
    for c in range(4):
        own, across, core = outs[3 * (c // 2) : 3 * (c // 2) + 3]
        g = c % 2

        @pl.when(step == c)
        def _():
            cols = own.shape[1]
            for b in range(4):
                part = total[:, pl.ds(pl.multiple_of(where_ref[b] * cols, 128), cols)]
                if b < 2:
                    (own, across)[b][g * rows : (g + 1) * rows, :] = part
                else:
                    first = ((b - 2) * 2 + g) * rows
                    core[first : first + rows, :] = part.astype(BF)


def down_all(where, hidden, w_down, slot_rows, gate_row, cols):
    rows, inner = hidden.shape
    sizes = ((2 * rows, F32), (2 * rows, F32), (4 * rows, BF)) * 2
    return pl.pallas_call(
        down_kernel,
        out_shape=[jax.ShapeDtypeStruct((count, cols), kind) for count, kind in sizes],
        grid_spec=pltpu.PrefetchScalarGridSpec(
            num_scalar_prefetch=1,
            grid=(4,),
            in_specs=[
                pl.BlockSpec((rows, inner), lambda j, w: (0, 0)),
                pl.BlockSpec((inner, 4 * cols), lambda j, w: (0, w[4 + j])),
                *whole_specs([slot_rows, gate_row]),
            ],
            out_specs=[pl.BlockSpec((count, cols), lambda j, w: (0, 0)) for count, _ in sizes],
            scratch_shapes=[pltpu.VMEM((rows, 4 * cols), F32), pltpu.VMEM((rows, 1), F32)],
        ),
        compiler_params=params(40),
        cost_estimate=cost(rows, inner, 16 * cols, 64 * rows * cols),
    )(where, hidden, w_down, slot_rows, gate_row)


def mix_kernel(slot_ref, x_ref, gain_ref, e0, e2, e1, e3, out_ref, squares_ref):
    rows = x_ref.shape[0]
    mixture = x_ref[...].astype(F32)
    moe = jnp.zeros_like(mixture)
    for j, part in enumerate((e0, e1, e2, e3)):
        slots = part.shape[0]
        spots = lax.broadcasted_iota(jnp.int32, (rows, slots), 1)
        chosen = jnp.where(slot_ref[:, j : j + 1] == spots, 1.0, 0.0).astype(BF)
        moe = moe + jnp.dot(chosen, part[...], preferred_element_type=F32)
    mixture = mixture + moe
    out_ref[...] = (mixture * gain_ref[...].astype(F32)).astype(BF)
    squares_ref[...] = jnp.sum(mixture * mixture, axis=1, keepdims=True)


def mix(slot_cols, x, gain, parts):
    rows, cols = x.shape
    return pl.pallas_call(
        mix_kernel,
        out_shape=[
            jax.ShapeDtypeStruct((rows, cols), BF),
            jax.ShapeDtypeStruct((rows, 1), F32),
        ],
        compiler_params=params(16),
    )(slot_cols, x, gain, *parts)


def vocab_kernel(given, count, first, last, tile, where_ref, *refs):
    blocks, refs = refs[:given], refs[given:]
    weight, refs = refs[0], refs[1:]
    if not first:
        sum_in, refs = refs[0], refs[1:]
    if last:
        inv, local_ids, out, wide, top, total, picked = refs
    else:
        out, wide = refs
    n = pl.program_id(0)

    @pl.when(n == 0)
    def _():
        place(where_ref, blocks, wide)

    value = resident_product(where_ref, wide, weight, n, tile)
    at = pl.ds(pl.multiple_of(n * tile, 128), tile)
    if not first:
        value = value + sum_in[:, at]
    if not last:
        out[:, at] = value
        return
    logits = value * (1.0 / jnp.sqrt(inv[...] / D + epsilon))
    column = n * tile + lax.broadcasted_iota(jnp.int32, logits.shape, 1)
    tile_pick = jnp.sum(jnp.where(column == local_ids[...], logits, 0.0), axis=1, keepdims=True)
    tile_top = jnp.max(logits, axis=1, keepdims=True)

    @pl.when(n == 0)
    def _():
        top[...] = tile_top
        total[...] = jnp.sum(jnp.exp(logits - tile_top), axis=1, keepdims=True)
        picked[...] = tile_pick

    @pl.when(n > 0)
    def _():
        new_top = jnp.maximum(top[...], tile_top)
        total[...] = total[...] * jnp.exp(top[...] - new_top) + jnp.sum(
            jnp.exp(logits - new_top), axis=1, keepdims=True
        )
        top[...] = new_top
        picked[...] = picked[...] + tile_pick

    @pl.when(n == pl.num_programs(0) - 1)
    def _():
        lane = lax.broadcasted_iota(jnp.int32, out.shape, 1)
        out[...] = jnp.where(lane == 0, top[...], jnp.where(lane == 1, total[...], picked[...]))


def vocab_part(where, blocks, rows, lm_head, sums, inv, local_ids):
    cols = blocks[0].shape[1]
    count = blocks[0].shape[0] // rows
    inner, width = lm_head.shape
    tile = 512 if rows <= 352 else 256
    first, last = sums is None, inv is not None
    lm_head = pltpu.with_memory_space_constraint(lm_head, pltpu.VMEM)
    ins = [where, *blocks, lm_head]
    specs = whole_specs(blocks) + [VMEM]
    aliases = {}
    if not first:
        if not last:
            aliases = {len(ins): 0}
        ins.append(pltpu.with_memory_space_constraint(sums, pltpu.VMEM))
        specs.append(VMEM)
    scratch = [pltpu.VMEM((rows, 4 * count * cols), BF)]
    if last:
        ins += [inv, local_ids]
        specs += whole_specs([inv, local_ids])
        outs = jax.ShapeDtypeStruct((rows, 128), F32)
        out_specs = pl.BlockSpec((rows, 128), lambda n, w: (0, 0))
        scratch += [pltpu.VMEM((rows, 1), F32)] * 3
    else:
        outs, out_specs = pltpu.VMEM((rows, width), F32), VMEM
    return pl.pallas_call(
        functools.partial(vocab_kernel, len(blocks), count, first, last, tile),
        out_shape=outs,
        grid_spec=pltpu.PrefetchScalarGridSpec(
            num_scalar_prefetch=1,
            grid=(width // tile,),
            in_specs=specs,
            out_specs=out_specs,
            scratch_shapes=scratch,
        ),
        input_output_aliases=aliases,
        compiler_params=params(32),
        cost_estimate=cost(rows, 8 if first else inner * count // 4, width, 0),
    )(*ins)


def spread(by_offset, squares, load, part):
    own0 = by_offset[0]
    a1 = send(by_offset[1], plane_pairs(1))
    a3 = send(by_offset[3], plane_pairs(3))
    row0 = send(own0, xor_pairs(2))
    core0 = send(own0, xor_pairs(1))
    diagonal0 = send(own0, xor_pairs(3))
    weight, token = load(own0)

    near = jnp.concatenate([a1, a3], axis=0)
    row0, core0, diagonal0, near, squares, far, token = lax.optimization_barrier(
        (row0, core0, diagonal0, near, squares, by_offset[2], token)
    )
    a2 = send(far, plane_pairs(2))
    row13 = send(near, xor_pairs(2))
    sums = part(0, weight, (own0, row0, core0, diagonal0), None, None)
    squares = squares + token[:1, :1]
    squares = squares + send(squares, xor_pairs(1))
    squares = squares + send(squares, xor_pairs(2))
    squares = squares + send(squares, xor_pairs(4))

    a2, row13, squares, sums = lax.optimization_barrier((a2, row13, squares, sums))
    row2 = send(a2, xor_pairs(2))
    core13 = send(jnp.concatenate([near, row13], axis=0), xor_pairs(1))
    squares = squares + send(squares, xor_pairs(8))
    sums = part(1, weight, (near, row13, core13), sums, None)

    row2, squares, sums = lax.optimization_barrier((row2, squares, sums))
    core2 = send(jnp.concatenate([a2, row2], axis=0), xor_pairs(1))
    return part(2, weight, (a2, row2, core2), sums, squares)


def live_part(
    x,
    norm_gain,
    final_gain,
    w_gate,
    w_up,
    w_down,
    lm_head,
    target_ids,
    slot_rows,
    gate_row,
    in_squares,
    where,
    down_at,
    first_id,
    live_rows,
    slots,
):
    cols = x.shape[1]
    *picked_rows, x_live = dispatch(slot_rows, x, norm_gain, slots, live_rows)
    packed = slot_rows[4]
    live_at = packed[None, :] == jnp.arange(live_rows, dtype=jnp.int32)[:, None]
    slot_live = jnp.stack(
        [
            jnp.sum(jnp.where(live_at, slot_rows[(4 - k) % 4][None, :] + 1, 0), axis=1) - 1
            for k in range(4)
        ],
        axis=1,
    )
    local_ids = (
        jnp.sum(jnp.where(live_at, target_ids[None, :], 0), axis=1, keepdims=True) - first_id
    )

    def hidden_step(group, weight, blocks, sums, squares):
        rows_of = None if squares is None else [slot_rows, squares]
        return hidden_part(where[group], blocks, slots, weight, w_up, sums, rows_of)

    hidden = spread(
        picked_rows, in_squares, functools.partial(resident, w_gate), hidden_step
    )

    two = 2 * slots
    own_a, row_a, core_a, own_b, row_b, core_b = down_all(
        down_at, hidden, w_down, slot_rows, gate_row, cols
    )
    heard_a = send(core_a, xor_pairs(1))
    heard_b = send(core_b, xor_pairs(1))
    across_a = (row_a + heard_a[two:].astype(F32)).astype(BF)
    crossed_a = send(across_a, xor_pairs(2))
    total_a = (own_a + heard_a[:two].astype(F32) + crossed_a.astype(F32)).astype(BF)
    part2 = send(total_a[:slots], plane_pairs(2))
    part1 = send(total_a[slots:], plane_pairs(1))
    across_b = (row_b + heard_b[two:].astype(F32)).astype(BF)
    crossed_b = send(after(across_b, crossed_a), xor_pairs(2))
    total_b = (own_b + heard_b[:two].astype(F32) + crossed_b.astype(F32)).astype(BF)
    part3 = send(total_b[:slots], plane_pairs(3))
    parts = (total_b[slots:], part2, part1, part3)

    scaled, squares = mix(slot_live, x_live, final_gain, parts)

    def vocab_step(group, weight, blocks, sums, squares):
        return vocab_part(where[group], blocks, live_rows, weight, sums, squares, local_ids)

    stats = spread([scaled] * 4, squares, functools.partial(resident, lm_head), vocab_step)
    spot = packed[:, None] == jnp.arange(live_rows, dtype=jnp.int32)[None, :]
    return jnp.stack(
        [jnp.sum(jnp.where(spot, stats[:, j][None, :], 0.0), axis=1) for j in range(3)]
    )


def fast_body(
    residual_in,
    norm_gain,
    final_gain,
    expert_ids,
    gate_values,
    w_gate,
    w_up,
    w_down,
    lm_head,
    target_ids,
    lengths,
):
    tokens = residual_in.shape[0]
    devices = lax.axis_size("tensor")
    me = lax.axis_index("tensor").astype(jnp.int32)
    plane, row, core = me >> 2, (me >> 1) & 1, me & 1
    slot_rows, gate_row, need = route(plane, lengths, expert_ids.T, gate_values.T)
    need = jnp.maximum(need, lax.ppermute(need, "groups", [(0, 1), (1, 0)]))

    at = [row * 2 + core, (1 - row) * 2 + core, row * 2 + 1 - core, (1 - row) * 2 + 1 - core]
    planes = [(plane + k) & 3 for k in range(4)]
    where = [jnp.stack(at + [planes[(4 - k) % 4] for k in group]) for group in CHUNKS]
    down_at = jnp.stack(at + [planes[k] for k in (2, 1, 3, 0)])
    stream = residual_in.astype(F32)
    in_squares = jnp.sum(stream * stream, axis=1)[None, :]

    stats = lax.switch(
        need[0, 0].astype(jnp.int32),
        [
            functools.partial(live_part, live_rows=rows, slots=slots)
            for rows, slots in TIERS + ((tokens, CAP),)
        ],
        residual_in,
        norm_gain[None, :],
        final_gain[None, :],
        w_gate,
        w_up,
        w_down,
        lm_head,
        target_ids,
        slot_rows,
        gate_row,
        in_squares,
        where,
        down_at,
        me * lm_head.shape[1],
    )
    rows_dev = tokens // devices
    stats = stats.reshape(3, devices, rows_dev).transpose(1, 0, 2)
    stats = lax.all_to_all(stats, "tensor", 0, 0, tiled=True)
    top = jnp.max(stats[:, 0], axis=0)
    total = jnp.sum(stats[:, 1] * jnp.exp(stats[:, 0] - top[None, :]), axis=0)
    logprob = jnp.sum(stats[:, 2], axis=0) - top - jnp.log(total)
    own_live = lax.dynamic_slice_in_dim(slot_rows[4], me * rows_dev, rows_dev) >= 0
    return jnp.where(own_live, logprob, 0.0)


def body(*args):
    if lax.axis_size("tensor") == 16 and lax.axis_size("groups") == 2:
        return fast_body(*args)
    return plain_body(*args)


def solution(mesh):
    return jax.shard_map(
        body,
        mesh=mesh,
        in_specs=(
            P("groups", "tensor"),
            P("tensor"),
            P("tensor"),
            P("groups", None),
            P("groups", None),
            P(None, "tensor"),
            P(None, "tensor"),
            P("tensor", None),
            P(None, "tensor"),
            P("groups"),
            P("groups"),
        ),
        out_specs=P(("groups", "tensor")),
        check_vma=False,
    )
```

```python
import functools
import jax
import jax.numpy as jnp
from jax import lax
from jax.experimental import pallas as pl
from jax.experimental.pallas import tpu as pltpu
from jax.sharding import PartitionSpec as P

D = 6144
EXPERTS = 4
EXP_FF = 8192
TOP = 2
SEQ = 64
CAP = 384


epsilon = 1e-05


def combined_all(array, axis, combine):
    everything = jax.tree.map(lambda part: lax.all_gather(part, axis), array)
    leading = jax.tree.map(lambda part: part[0], everything)

    def hop(k, so_far):
        return combine(so_far, jax.tree.map(lambda part: part[k], everything))

    return lax.fori_loop(1, lax.axis_size(axis), hop, leading)


def slots_of(expert_ids):
    flat_ids = expert_ids.reshape(-1)
    pairs = jnp.arange(flat_ids.shape[0], dtype=jnp.int32)
    before = (pairs[None, :] < pairs[:, None]) & (flat_ids[None, :] == flat_ids[:, None])
    return jnp.sum(before.astype(jnp.int32), axis=1).reshape(expert_ids.shape)


def slot_tokens(expert_ids, slot_index):
    slot_code = (expert_ids * CAP + slot_index).reshape(-1)
    owner = jnp.arange(slot_code.shape[0], dtype=jnp.int32) // TOP
    wanted = jnp.arange(EXPERTS * CAP, dtype=jnp.int32)
    matches = slot_code[None, :] == wanted[:, None]
    return jnp.sum(jnp.where(matches, owner[None, :] + 1, 0), axis=1) - 1


def normalize(values, squares_total, gain_vec):
    return (
        values / jnp.sqrt(squares_total[:, None] / D + epsilon) * gain_vec.astype(jnp.float32)
    ).astype(jnp.bfloat16)


def plain_body(
    residual_in,
    norm_gain,
    final_gain,
    expert_ids,
    gate_values,
    w_gate,
    w_up,
    w_down,
    lm_head,
    target_ids,
    lengths,
):
    tokens, feature_cols = residual_in.shape
    hidden_dev = w_gate.shape[1]
    per_expert = EXP_FF // hidden_dev
    expert_now = lax.axis_index("tensor") // per_expert
    stream = residual_in.astype(jnp.float32)
    in_total = lax.psum(jnp.sum(stream * stream, axis=1), "tensor")
    normed = normalize(stream, in_total, norm_gain)
    slot_index = slots_of(expert_ids)
    token_of = slot_tokens(expert_ids, slot_index)
    zero_bf = jnp.zeros((), jnp.bfloat16)
    own_slots = lax.dynamic_slice_in_dim(token_of, expert_now * CAP, CAP)
    occupied = own_slots >= 0
    safe_index = jnp.maximum(own_slots, 0)
    slot_rows = jnp.where(
        occupied[:, None], lax.all_gather(normed, "tensor", axis=1, tiled=True)[safe_index], zero_bf
    )
    gate_out = jnp.dot(slot_rows, w_gate, preferred_element_type=jnp.float32)
    up_out = jnp.dot(slot_rows, w_up, preferred_element_type=jnp.float32)
    hidden = (jax.nn.silu(gate_out) * up_out).astype(jnp.bfloat16)
    partial_value = jnp.dot(hidden, w_down, preferred_element_type=jnp.float32)
    weight_own = jnp.where(expert_ids == expert_now, gate_values, jnp.zeros_like(gate_values))
    weighted = (
        weight_own[:, 0:1] * partial_value[slot_index[:, 0]]
        + weight_own[:, 1:2] * partial_value[slot_index[:, 1]]
    )
    moe_cols = lax.psum_scatter(weighted, "tensor", scatter_dimension=1, tiled=True)
    mixture = stream + moe_cols
    out_total = lax.psum(jnp.sum(mixture * mixture, axis=1), "tensor")
    normed_out = normalize(mixture, out_total, final_gain)
    vocab_dev = lm_head.shape[1]
    logits = jnp.dot(
        lax.all_gather(normed_out, "tensor", axis=1, tiled=True),
        lm_head,
        preferred_element_type=jnp.float32,
    )
    row_max = jnp.max(logits, axis=1)
    row_total = jnp.sum(jnp.exp(logits - row_max[:, None]), axis=1)
    local_ids = target_ids - lax.axis_index("tensor") * vocab_dev
    vocab_cols = jnp.arange(vocab_dev, dtype=jnp.int32)
    picked = jnp.sum(jnp.where(vocab_cols[None, :] == local_ids[:, None], logits, 0.0), axis=1)

    def joined(earlier, later):
        merged_max = jnp.maximum(earlier[0], later[0])
        merged_total = earlier[1] * jnp.exp(earlier[0] - merged_max) + later[1] * jnp.exp(
            later[0] - merged_max
        )
        return (merged_max, merged_total, earlier[2] + later[2])

    merged_max, merged_total, target_logit = combined_all(
        (row_max, row_total, picked), "tensor", joined
    )
    logprob = target_logit - merged_max - jnp.log(merged_total)
    rows_dev = tokens // lax.axis_size("tensor")
    first_row = lax.axis_index("tensor") * rows_dev
    own_rows = lax.dynamic_slice_in_dim(logprob, first_row, rows_dev)
    position = first_row + jnp.arange(rows_dev, dtype=jnp.int32)
    in_length = position % SEQ < lengths[position // SEQ]
    return jnp.where(in_length, own_rows, jnp.zeros_like(own_rows)).astype(jnp.float32)

TIERS = ((288, 224), (352, 272))
CHUNKS = ((0,), (1, 3), (2,))
VMEM = pl.BlockSpec(memory_space=pltpu.VMEM)
BF = jnp.bfloat16
F32 = jnp.float32


def send(array, pairs):
    return lax.ppermute(array, "tensor", pairs)


def xor_pairs(mask):
    return [(i, i ^ mask) for i in range(16)]


def plane_pairs(k):
    return [(i, ((i >> 2) + k) % 4 * 4 + (i & 3)) for i in range(16)]


def after(value, *others):
    return lax.optimization_barrier((value, *others))[0]


def params(mebibytes):
    return pltpu.CompilerParams(vmem_limit_bytes=mebibytes * 1024 * 1024)


def load_kernel(w_ref, after_ref, out_ref, token_ref, sem):
    copy = pltpu.make_async_copy(w_ref, out_ref, sem)
    copy.start()
    copy.wait()
    token_ref[...] = jnp.zeros_like(token_ref)


def resident(weight, ready):
    weight = pltpu.with_memory_space_constraint(weight, pltpu.HBM)
    return pl.pallas_call(
        load_kernel,
        in_specs=[pl.BlockSpec(memory_space=pltpu.HBM), pl.BlockSpec(memory_space=pl.ANY)],
        out_specs=[VMEM, VMEM],
        out_shape=[
            pltpu.VMEM(weight.shape, weight.dtype),
            jax.ShapeDtypeStruct((8, 128), F32),
        ],
        scratch_shapes=[pltpu.SemaphoreType.DMA],
        compiler_params=params(1),
        cost_estimate=pl.CostEstimate(
            flops=0, transcendentals=0, bytes_accessed=4 * weight.size
        ),
    )(weight, ready)


def cost(rows, inner, cols, other_bytes):
    return pl.CostEstimate(
        flops=2 * rows * inner * cols,
        transcendentals=0,
        bytes_accessed=2 * inner * cols + other_bytes,
    )


def route_kernel(where_ref, lengths_ref, ids_ref, gates_ref, slots_ref, gate_ref, need_ref, used_ref):
    tokens = ids_ref.shape[1]
    spot = lax.broadcasted_iota(jnp.int32, (1, tokens), 1)
    cand = lax.shift_right_logical(spot, SEQ.bit_length() - 1)
    size = jnp.zeros_like(spot)
    start = jnp.zeros_like(spot)
    alive = jnp.int32(0)
    for c in range(lengths_ref.shape[0]):
        size = jnp.where(cand == c, lengths_ref[c], size)
        start = jnp.where(cand == c, alive, start)
        alive = alive + lengths_ref[c]
    step = spot - cand * SEQ
    live = step < size
    used_ref[...] = jnp.zeros_like(used_ref)
    for k in range(EXPERTS):
        expert = lax.rem(where_ref[0] + k, EXPERTS)
        first = (ids_ref[0:1, :] == expert) & live
        second = (ids_ref[1:2, :] == expert) & live
        used_ref[k : k + 1, :] = jnp.where(first | second, 1.0, 0.0)
        if k == 0:
            gate_ref[...] = jnp.where(first, gates_ref[0:1, :], 0.0) + jnp.where(
                second, gates_ref[1:2, :], 0.0
            )
    used = used_ref[...]
    source = lax.broadcasted_iota(jnp.int32, (tokens, tokens), 0)
    target = lax.broadcasted_iota(jnp.int32, (tokens, tokens), 1)
    earlier = jnp.where(source < target, 1.0, 0.0).astype(BF)
    rank = jnp.dot(used.astype(BF), earlier, preferred_element_type=F32)
    slots_ref[...] = jnp.where(used > 0.0, rank.astype(jnp.int32), -1)
    slots_ref[4:5, :] = jnp.where(live, start + step, -1)
    fullest = jnp.max(jnp.sum(used, axis=1, keepdims=True))
    need = jnp.float32(0.0)
    for rows, slots in TIERS:
        over = (alive > rows) | (fullest > float(slots))
        need = need + jnp.where(over, 1.0, 0.0)
    need_ref[...] = jnp.full(need_ref.shape, need, F32)


def route(plane, lengths, ids, gates):
    tokens = ids.shape[1]
    smem = pl.BlockSpec(memory_space=pltpu.SMEM)
    vmem = pl.BlockSpec(memory_space=pltpu.VMEM)
    return pl.pallas_call(
        route_kernel,
        in_specs=[smem, smem, vmem, vmem],
        out_specs=[vmem] * 3,
        out_shape=[
            jax.ShapeDtypeStruct((8, tokens), jnp.int32),
            jax.ShapeDtypeStruct((1, tokens), F32),
            jax.ShapeDtypeStruct((8, 128), F32),
        ],
        scratch_shapes=[pltpu.VMEM((8, tokens), F32)],
        compiler_params=params(16),
    )(plane.reshape(1), lengths, ids, gates)


def dispatch_kernel(slot_ref, x_ref, gain_ref, s0, s1, s2, s3, xc_ref):
    x = x_ref[...]
    scaled = (x.astype(F32) * gain_ref[...].astype(F32)).astype(BF)
    tokens = x.shape[0]
    for k, out in enumerate((s0, s1, s2, s3)):
        rows = out.shape[0]
        spots = lax.broadcasted_iota(jnp.int32, (rows, tokens), 0)
        chosen = jnp.where(slot_ref[k : k + 1, :] == spots, 1.0, 0.0).astype(BF)
        out[...] = jnp.dot(chosen, scaled, preferred_element_type=F32).astype(BF)
    rows = xc_ref.shape[0]
    spots = lax.broadcasted_iota(jnp.int32, (rows, tokens), 0)
    chosen = jnp.where(slot_ref[4:5, :] == spots, 1.0, 0.0).astype(BF)
    xc_ref[...] = jnp.dot(chosen, x, preferred_element_type=F32).astype(BF)


def dispatch(slot_rows, x, gain, slots, live_rows):
    cols = x.shape[1]
    block = jax.ShapeDtypeStruct((slots, cols), BF)
    return pl.pallas_call(
        dispatch_kernel,
        out_shape=[block] * 4 + [jax.ShapeDtypeStruct((live_rows, cols), BF)],
        compiler_params=params(16),
    )(slot_rows, x, gain)


def place(where_ref, blocks, wide_ref):
    own, across, *core = blocks
    rows, cols = wide_ref.shape[0], own.shape[1]
    count = own.shape[0] // rows
    for g in range(count):
        pieces = ((own, g), (across, g), (core[0], g), (core[-1], g if len(core) == 2 else count + g))
        for quarter, (block, piece) in enumerate(pieces):
            at = pl.multiple_of((g * 4 + where_ref[quarter]) * cols, 128)
            wide_ref[:, pl.ds(at, cols)] = block[piece * rows : (piece + 1) * rows, :]


def whole_specs(arrays):
    return [pl.BlockSpec(array.shape, lambda n, w: (0, 0)) for array in arrays]


def product(wide, weights):
    depth = weights[0].shape[0]
    value = None
    for j, w in enumerate(weights):
        part = jnp.dot(
            wide[:, j * depth : (j + 1) * depth], w[...], preferred_element_type=F32
        )
        value = part if value is None else value + part
    return value


def resident_product(where_ref, wide, weight, n, tile):
    depth = weight.shape[0] // 4
    value = None
    for j in range(wide.shape[1] // depth):
        first = pl.multiple_of(where_ref[4 + j] * depth, 128)
        part = jnp.dot(
            wide[:, j * depth : (j + 1) * depth],
            weight[pl.ds(first, depth), pl.ds(pl.multiple_of(n * tile, 128), tile)],
            preferred_element_type=F32,
        )
        value = part if value is None else value + part
    return value


def weight_specs(count, depth, tile):
    return [
        pl.BlockSpec((depth, tile), functools.partial(lambda j, n, w: (w[4 + j], n), j))
        for j in range(count)
    ]


def by_slot(slot_ref, values, slots):
    spots = lax.broadcasted_iota(jnp.int32, (slots, slot_ref.shape[1]), 0)
    chosen = jnp.where(slot_ref[0:1, :] == spots, values, 0.0)
    return jnp.sum(chosen, axis=1, keepdims=True)


def hidden_kernel(given, count, first, last, where_ref, *refs):
    blocks, refs = refs[:given], refs[given:]
    wg, wu, refs = refs[0], refs[1 : 1 + count], refs[1 + count :]
    if not first:
        g_in, u_in, refs = refs[0], refs[1], refs[2:]
    if last:
        slot_ref, squares_ref, h_out, wide, inv = refs
    else:
        g_out, u_out, wide = refs
    n = pl.program_id(0)
    tile = wu[0].shape[1]

    @pl.when(n == 0)
    def _():
        place(where_ref, blocks, wide)
        if last:
            scale = 1.0 / jnp.sqrt(squares_ref[...] / D + epsilon)
            inv[...] = by_slot(slot_ref, scale, inv.shape[0])

    g = resident_product(where_ref, wide, wg, n, tile)
    u = product(wide, wu)
    at = pl.ds(pl.multiple_of(n * tile, 128), tile)
    if not first:
        g = g + g_in[:, at]
        u = u + u_in[:, at]
    if last:
        g = g * inv[...]
        u = u * inv[...]
        h_out[:, at] = (g / (1.0 + jnp.exp(-g)) * u).astype(BF)
    else:
        g_out[:, at] = g
        u_out[:, at] = u


def hidden_part(where, blocks, slots, w_gate, w_up, sums, rows_of):
    cols = blocks[0].shape[1]
    count = blocks[0].shape[0] // slots
    inner, width = w_up.shape
    tile, depth = 512 if slots > 272 else 1024, inner // 4
    first, last = sums is None, rows_of is not None
    w_gate = pltpu.with_memory_space_constraint(w_gate, pltpu.VMEM)
    w_up = pltpu.with_memory_space_constraint(w_up, pltpu.HBM)
    ins = [where, *blocks, w_gate] + [w_up] * count
    specs = whole_specs(blocks) + [VMEM] + weight_specs(count, depth, tile)
    aliases = {}
    if not first:
        if not last:
            aliases = {len(ins): 0, len(ins) + 1: 1}
        ins += [pltpu.with_memory_space_constraint(part, pltpu.VMEM) for part in sums]
        specs += [VMEM] * 2
    if last:
        ins += rows_of
        specs += whole_specs(rows_of)
        outs, out_specs = pltpu.VMEM((slots, width), BF), VMEM
    else:
        outs, out_specs = [pltpu.VMEM((slots, width), F32)] * 2, [VMEM] * 2
    return pl.pallas_call(
        functools.partial(hidden_kernel, len(blocks), count, first, last),
        out_shape=outs,
        grid_spec=pltpu.PrefetchScalarGridSpec(
            num_scalar_prefetch=1,
            grid=(width // tile,),
            in_specs=specs,
            out_specs=out_specs,
            scratch_shapes=[pltpu.VMEM((slots, 4 * count * cols), BF)]
            + [pltpu.VMEM((slots, 1), F32)] * last,
        ),
        input_output_aliases=aliases,
        compiler_params=params(30),
        cost_estimate=cost(slots, 8 if first else count * depth, 2 * width, 0),
    )(*ins)


def down_kernel(where_ref, h_ref, w_ref, slot_ref, row_ref, *refs):
    *outs, total, gate_ref = refs
    rows = h_ref.shape[0]
    step = pl.program_id(0)

    @pl.when(step == 0)
    def _():
        gate_ref[...] = by_slot(slot_ref, row_ref[...], rows)

    value = jnp.dot(h_ref[...], w_ref[...], preferred_element_type=F32) * gate_ref[...]
    total[...] = value
    for c in range(4):
        own, across, core = outs[3 * (c // 2) : 3 * (c // 2) + 3]
        g = c % 2

        @pl.when(step == c)
        def _():
            cols = own.shape[1]
            for b in range(4):
                part = total[:, pl.ds(pl.multiple_of(where_ref[b] * cols, 128), cols)]
                if b < 2:
                    (own, across)[b][g * rows : (g + 1) * rows, :] = part
                else:
                    first = ((b - 2) * 2 + g) * rows
                    core[first : first + rows, :] = part.astype(BF)


def down_all(where, hidden, w_down, slot_rows, gate_row, cols):
    rows, inner = hidden.shape
    hidden = pltpu.with_memory_space_constraint(hidden, pltpu.VMEM)
    sizes = ((2 * rows, F32), (2 * rows, F32), (4 * rows, BF)) * 2
    return pl.pallas_call(
        down_kernel,
        out_shape=[jax.ShapeDtypeStruct((count, cols), kind) for count, kind in sizes],
        grid_spec=pltpu.PrefetchScalarGridSpec(
            num_scalar_prefetch=1,
            grid=(4,),
            in_specs=[
                VMEM,
                pl.BlockSpec((inner, 4 * cols), lambda j, w: (0, w[4 + j])),
                *whole_specs([slot_rows, gate_row]),
            ],
            out_specs=[pl.BlockSpec((count, cols), lambda j, w: (0, 0)) for count, _ in sizes],
            scratch_shapes=[pltpu.VMEM((rows, 4 * cols), F32), pltpu.VMEM((rows, 1), F32)],
        ),
        compiler_params=params(40),
        cost_estimate=cost(rows, inner, 16 * cols, 64 * rows * cols),
    )(where, hidden, w_down, slot_rows, gate_row)


def mix_kernel(slot_ref, x_ref, gain_ref, e0, e2, e1, e3, out_ref, squares_ref):
    rows = x_ref.shape[0]
    mixture = x_ref[...].astype(F32)
    moe = jnp.zeros_like(mixture)
    for j, part in enumerate((e0, e1, e2, e3)):
        slots = part.shape[0]
        spots = lax.broadcasted_iota(jnp.int32, (rows, slots), 1)
        chosen = jnp.where(slot_ref[:, j : j + 1] == spots, 1.0, 0.0).astype(BF)
        moe = moe + jnp.dot(chosen, part[...], preferred_element_type=F32)
    mixture = mixture + moe
    out_ref[...] = (mixture * gain_ref[...].astype(F32)).astype(BF)
    squares_ref[...] = jnp.sum(mixture * mixture, axis=1, keepdims=True)


def mix(slot_cols, x, gain, parts):
    rows, cols = x.shape
    return pl.pallas_call(
        mix_kernel,
        out_shape=[
            jax.ShapeDtypeStruct((rows, cols), BF),
            jax.ShapeDtypeStruct((rows, 1), F32),
        ],
        compiler_params=params(16),
    )(slot_cols, x, gain, *parts)


def vocab_kernel(given, count, first, last, tile, where_ref, *refs):
    blocks, refs = refs[:given], refs[given:]
    weight, refs = refs[0], refs[1:]
    if not first:
        sum_in, refs = refs[0], refs[1:]
    if last:
        inv, local_ids, out, wide, top, total, picked = refs
    else:
        out, wide = refs
    n = pl.program_id(0)

    @pl.when(n == 0)
    def _():
        place(where_ref, blocks, wide)

    value = resident_product(where_ref, wide, weight, n, tile)
    at = pl.ds(pl.multiple_of(n * tile, 128), tile)
    if not first:
        value = value + sum_in[:, at]
    if not last:
        out[:, at] = value
        return
    logits = value * (1.0 / jnp.sqrt(inv[...] / D + epsilon))
    column = n * tile + lax.broadcasted_iota(jnp.int32, logits.shape, 1)
    tile_pick = jnp.sum(jnp.where(column == local_ids[...], logits, 0.0), axis=1, keepdims=True)
    tile_top = jnp.max(logits, axis=1, keepdims=True)

    @pl.when(n == 0)
    def _():
        top[...] = tile_top
        total[...] = jnp.sum(jnp.exp(logits - tile_top), axis=1, keepdims=True)
        picked[...] = tile_pick

    @pl.when(n > 0)
    def _():
        new_top = jnp.maximum(top[...], tile_top)
        total[...] = total[...] * jnp.exp(top[...] - new_top) + jnp.sum(
            jnp.exp(logits - new_top), axis=1, keepdims=True
        )
        top[...] = new_top
        picked[...] = picked[...] + tile_pick

    @pl.when(n == pl.num_programs(0) - 1)
    def _():
        lane = lax.broadcasted_iota(jnp.int32, out.shape, 1)
        out[...] = jnp.where(lane == 0, top[...], jnp.where(lane == 1, total[...], picked[...]))


def vocab_part(where, blocks, rows, lm_head, sums, inv, local_ids):
    cols = blocks[0].shape[1]
    count = blocks[0].shape[0] // rows
    inner, width = lm_head.shape
    tile = 512 if rows <= 352 else 256
    first, last = sums is None, inv is not None
    lm_head = pltpu.with_memory_space_constraint(lm_head, pltpu.VMEM)
    ins = [where, *blocks, lm_head]
    specs = whole_specs(blocks) + [VMEM]
    aliases = {}
    if not first:
        if not last:
            aliases = {len(ins): 0}
        ins.append(pltpu.with_memory_space_constraint(sums, pltpu.VMEM))
        specs.append(VMEM)
    scratch = [pltpu.VMEM((rows, 4 * count * cols), BF)]
    if last:
        ins += [inv, local_ids]
        specs += whole_specs([inv, local_ids])
        outs = jax.ShapeDtypeStruct((rows, 128), F32)
        out_specs = pl.BlockSpec((rows, 128), lambda n, w: (0, 0))
        scratch += [pltpu.VMEM((rows, 1), F32)] * 3
    else:
        outs, out_specs = pltpu.VMEM((rows, width), F32), VMEM
    return pl.pallas_call(
        functools.partial(vocab_kernel, len(blocks), count, first, last, tile),
        out_shape=outs,
        grid_spec=pltpu.PrefetchScalarGridSpec(
            num_scalar_prefetch=1,
            grid=(width // tile,),
            in_specs=specs,
            out_specs=out_specs,
            scratch_shapes=scratch,
        ),
        input_output_aliases=aliases,
        compiler_params=params(32),
        cost_estimate=cost(rows, 8 if first else inner * count // 4, width, 0),
    )(*ins)


def spread(by_offset, squares, load, part):
    own0 = by_offset[0]
    a1 = send(by_offset[1], plane_pairs(1))
    a3 = send(by_offset[3], plane_pairs(3))
    row0 = send(own0, xor_pairs(2))
    core0 = send(own0, xor_pairs(1))
    diagonal0 = send(own0, xor_pairs(3))
    weight, token = load(own0)

    near = jnp.concatenate([a1, a3], axis=0)
    row0, core0, diagonal0, near, squares, far, token = lax.optimization_barrier(
        (row0, core0, diagonal0, near, squares, by_offset[2], token)
    )
    a2 = send(far, plane_pairs(2))
    row13 = send(near, xor_pairs(2))
    squares = squares + token[:1, :1]
    more = [send(squares, xor_pairs(mask)) for mask in (1, 2, 3)]
    sums = part(0, weight, (own0, row0, core0, diagonal0), None, None)

    a2, row13, squares, more, sums = lax.optimization_barrier((a2, row13, squares, more, sums))
    row2 = send(a2, xor_pairs(2))
    core13 = send(jnp.concatenate([near, row13], axis=0), xor_pairs(1))
    squares = squares + more[0] + (more[1] + more[2])
    more = [send(squares, plane_pairs(k)) for k in (1, 2, 3)]
    sums = part(1, weight, (near, row13, core13), sums, None)

    row2, squares, more, sums = lax.optimization_barrier((row2, squares, more, sums))
    squares = squares + more[0] + (more[1] + more[2])
    core2 = send(jnp.concatenate([a2, row2], axis=0), xor_pairs(1))
    return part(2, weight, (a2, row2, core2), sums, squares)


def live_part(
    x,
    norm_gain,
    final_gain,
    w_gate,
    w_up,
    w_down,
    lm_head,
    target_ids,
    slot_rows,
    gate_row,
    in_squares,
    where,
    down_at,
    first_id,
    live_rows,
    slots,
):
    cols = x.shape[1]
    *picked_rows, x_live = dispatch(slot_rows, x, norm_gain, slots, live_rows)
    packed = slot_rows[4]
    live_at = packed[None, :] == jnp.arange(live_rows, dtype=jnp.int32)[:, None]
    slot_live = jnp.stack(
        [
            jnp.sum(jnp.where(live_at, slot_rows[(4 - k) % 4][None, :] + 1, 0), axis=1) - 1
            for k in range(4)
        ],
        axis=1,
    )
    local_ids = (
        jnp.sum(jnp.where(live_at, target_ids[None, :], 0), axis=1, keepdims=True) - first_id
    )

    def hidden_step(group, weight, blocks, sums, squares):
        rows_of = None if squares is None else [slot_rows, squares]
        return hidden_part(where[group], blocks, slots, weight, w_up, sums, rows_of)

    hidden = spread(
        picked_rows, in_squares, functools.partial(resident, w_gate), hidden_step
    )

    two = 2 * slots
    own_a, row_a, core_a, own_b, row_b, core_b = down_all(
        down_at, hidden, w_down, slot_rows, gate_row, cols
    )
    heard_a = send(core_a, xor_pairs(1))
    heard_b = send(core_b, xor_pairs(1))
    across_a = (row_a + heard_a[two:].astype(F32)).astype(BF)
    crossed_a = send(across_a, xor_pairs(2))
    total_a = (own_a + heard_a[:two].astype(F32) + crossed_a.astype(F32)).astype(BF)
    part2 = send(total_a[:slots], plane_pairs(2))
    part1 = send(total_a[slots:], plane_pairs(1))
    across_b = (row_b + heard_b[two:].astype(F32)).astype(BF)
    crossed_b = send(after(across_b, crossed_a), xor_pairs(2))
    total_b = (own_b + heard_b[:two].astype(F32) + crossed_b.astype(F32)).astype(BF)
    part3 = send(total_b[:slots], plane_pairs(3))
    parts = (total_b[slots:], part2, part1, part3)

    scaled, squares = mix(slot_live, x_live, final_gain, parts)

    def vocab_step(group, weight, blocks, sums, squares):
        return vocab_part(where[group], blocks, live_rows, weight, sums, squares, local_ids)

    stats = spread([scaled] * 4, squares, functools.partial(resident, lm_head), vocab_step)
    spot = packed[:, None] == jnp.arange(live_rows, dtype=jnp.int32)[None, :]
    return jnp.stack(
        [jnp.sum(jnp.where(spot, stats[:, j][None, :], 0.0), axis=1) for j in range(3)]
    )


def fast_body(
    residual_in,
    norm_gain,
    final_gain,
    expert_ids,
    gate_values,
    w_gate,
    w_up,
    w_down,
    lm_head,
    target_ids,
    lengths,
):
    tokens = residual_in.shape[0]
    devices = lax.axis_size("tensor")
    me = lax.axis_index("tensor").astype(jnp.int32)
    plane, row, core = me >> 2, (me >> 1) & 1, me & 1
    slot_rows, gate_row, need = route(plane, lengths, expert_ids.T, gate_values.T)
    need = jnp.maximum(need, lax.ppermute(need, "groups", [(0, 1), (1, 0)]))

    at = [row * 2 + core, (1 - row) * 2 + core, row * 2 + 1 - core, (1 - row) * 2 + 1 - core]
    planes = [(plane + k) & 3 for k in range(4)]
    where = [jnp.stack(at + [planes[(4 - k) % 4] for k in group]) for group in CHUNKS]
    down_at = jnp.stack(at + [planes[k] for k in (2, 1, 3, 0)])
    stream = residual_in.astype(F32)
    in_squares = jnp.sum(stream * stream, axis=1)[None, :]

    stats = lax.switch(
        need[0, 0].astype(jnp.int32),
        [
            functools.partial(live_part, live_rows=rows, slots=slots)
            for rows, slots in TIERS + ((tokens, CAP),)
        ],
        residual_in,
        norm_gain[None, :],
        final_gain[None, :],
        w_gate,
        w_up,
        w_down,
        lm_head,
        target_ids,
        slot_rows,
        gate_row,
        in_squares,
        where,
        down_at,
        me * lm_head.shape[1],
    )
    rows_dev = tokens // devices
    stats = stats.reshape(3, devices, rows_dev).transpose(1, 0, 2)
    stats = lax.all_to_all(stats, "tensor", 0, 0, tiled=True)
    top = jnp.max(stats[:, 0], axis=0)
    total = jnp.sum(stats[:, 1] * jnp.exp(stats[:, 0] - top[None, :]), axis=0)
    logprob = jnp.sum(stats[:, 2], axis=0) - top - jnp.log(total)
    own_live = lax.dynamic_slice_in_dim(slot_rows[4], me * rows_dev, rows_dev) >= 0
    return jnp.where(own_live, logprob, 0.0)


def body(*args):
    if lax.axis_size("tensor") == 16 and lax.axis_size("groups") == 2:
        return fast_body(*args)
    return plain_body(*args)


def solution(mesh):
    return jax.shard_map(
        body,
        mesh=mesh,
        in_specs=(
            P("groups", "tensor"),
            P("tensor"),
            P("tensor"),
            P("groups", None),
            P("groups", None),
            P(None, "tensor"),
            P(None, "tensor"),
            P("tensor", None),
            P(None, "tensor"),
            P("groups"),
            P("groups"),
        ),
        out_specs=P(("groups", "tensor")),
        check_vma=False,
    )
```

```python
import functools
import jax
import jax.numpy as jnp
from jax import lax
from jax.experimental import pallas as pl
from jax.experimental.pallas import tpu as pltpu
from jax.sharding import PartitionSpec as P

D = 6144
EXPERTS = 4
EXP_FF = 8192
TOP = 2
SEQ = 64
CAP = 384


epsilon = 1e-05


def combined_all(array, axis, combine):
    everything = jax.tree.map(lambda part: lax.all_gather(part, axis), array)
    leading = jax.tree.map(lambda part: part[0], everything)

    def hop(k, so_far):
        return combine(so_far, jax.tree.map(lambda part: part[k], everything))

    return lax.fori_loop(1, lax.axis_size(axis), hop, leading)


def slots_of(expert_ids):
    flat_ids = expert_ids.reshape(-1)
    pairs = jnp.arange(flat_ids.shape[0], dtype=jnp.int32)
    before = (pairs[None, :] < pairs[:, None]) & (flat_ids[None, :] == flat_ids[:, None])
    return jnp.sum(before.astype(jnp.int32), axis=1).reshape(expert_ids.shape)


def slot_tokens(expert_ids, slot_index):
    slot_code = (expert_ids * CAP + slot_index).reshape(-1)
    owner = jnp.arange(slot_code.shape[0], dtype=jnp.int32) // TOP
    wanted = jnp.arange(EXPERTS * CAP, dtype=jnp.int32)
    matches = slot_code[None, :] == wanted[:, None]
    return jnp.sum(jnp.where(matches, owner[None, :] + 1, 0), axis=1) - 1


def normalize(values, squares_total, gain_vec):
    return (
        values / jnp.sqrt(squares_total[:, None] / D + epsilon) * gain_vec.astype(jnp.float32)
    ).astype(jnp.bfloat16)


def plain_body(
    residual_in,
    norm_gain,
    final_gain,
    expert_ids,
    gate_values,
    w_gate,
    w_up,
    w_down,
    lm_head,
    target_ids,
    lengths,
):
    tokens, feature_cols = residual_in.shape
    hidden_dev = w_gate.shape[1]
    per_expert = EXP_FF // hidden_dev
    expert_now = lax.axis_index("tensor") // per_expert
    stream = residual_in.astype(jnp.float32)
    in_total = lax.psum(jnp.sum(stream * stream, axis=1), "tensor")
    normed = normalize(stream, in_total, norm_gain)
    slot_index = slots_of(expert_ids)
    token_of = slot_tokens(expert_ids, slot_index)
    zero_bf = jnp.zeros((), jnp.bfloat16)
    own_slots = lax.dynamic_slice_in_dim(token_of, expert_now * CAP, CAP)
    occupied = own_slots >= 0
    safe_index = jnp.maximum(own_slots, 0)
    slot_rows = jnp.where(
        occupied[:, None], lax.all_gather(normed, "tensor", axis=1, tiled=True)[safe_index], zero_bf
    )
    gate_out = jnp.dot(slot_rows, w_gate, preferred_element_type=jnp.float32)
    up_out = jnp.dot(slot_rows, w_up, preferred_element_type=jnp.float32)
    hidden = (jax.nn.silu(gate_out) * up_out).astype(jnp.bfloat16)
    partial_value = jnp.dot(hidden, w_down, preferred_element_type=jnp.float32)
    weight_own = jnp.where(expert_ids == expert_now, gate_values, jnp.zeros_like(gate_values))
    weighted = (
        weight_own[:, 0:1] * partial_value[slot_index[:, 0]]
        + weight_own[:, 1:2] * partial_value[slot_index[:, 1]]
    )
    moe_cols = lax.psum_scatter(weighted, "tensor", scatter_dimension=1, tiled=True)
    mixture = stream + moe_cols
    out_total = lax.psum(jnp.sum(mixture * mixture, axis=1), "tensor")
    normed_out = normalize(mixture, out_total, final_gain)
    vocab_dev = lm_head.shape[1]
    logits = jnp.dot(
        lax.all_gather(normed_out, "tensor", axis=1, tiled=True),
        lm_head,
        preferred_element_type=jnp.float32,
    )
    row_max = jnp.max(logits, axis=1)
    row_total = jnp.sum(jnp.exp(logits - row_max[:, None]), axis=1)
    local_ids = target_ids - lax.axis_index("tensor") * vocab_dev
    vocab_cols = jnp.arange(vocab_dev, dtype=jnp.int32)
    picked = jnp.sum(jnp.where(vocab_cols[None, :] == local_ids[:, None], logits, 0.0), axis=1)

    def joined(earlier, later):
        merged_max = jnp.maximum(earlier[0], later[0])
        merged_total = earlier[1] * jnp.exp(earlier[0] - merged_max) + later[1] * jnp.exp(
            later[0] - merged_max
        )
        return (merged_max, merged_total, earlier[2] + later[2])

    merged_max, merged_total, target_logit = combined_all(
        (row_max, row_total, picked), "tensor", joined
    )
    logprob = target_logit - merged_max - jnp.log(merged_total)
    rows_dev = tokens // lax.axis_size("tensor")
    first_row = lax.axis_index("tensor") * rows_dev
    own_rows = lax.dynamic_slice_in_dim(logprob, first_row, rows_dev)
    position = first_row + jnp.arange(rows_dev, dtype=jnp.int32)
    in_length = position % SEQ < lengths[position // SEQ]
    return jnp.where(in_length, own_rows, jnp.zeros_like(own_rows)).astype(jnp.float32)

TIERS = ((304, 240), (352, 272))
CHUNKS = ((0,), (1, 3), (2,))
VMEM = pl.BlockSpec(memory_space=pltpu.VMEM)
BF = jnp.bfloat16
F32 = jnp.float32


def send(array, pairs):
    return lax.ppermute(array, "tensor", pairs)


def xor_pairs(mask):
    return [(i, i ^ mask) for i in range(16)]


def plane_pairs(k):
    return [(i, ((i >> 2) + k) % 4 * 4 + (i & 3)) for i in range(16)]


def after(value, *others):
    return lax.optimization_barrier((value, *others))[0]


def params(mebibytes):
    return pltpu.CompilerParams(vmem_limit_bytes=mebibytes * 1024 * 1024)


def load_kernel(w_ref, after_ref, out_ref, token_ref, sem):
    copy = pltpu.make_async_copy(w_ref, out_ref, sem)
    copy.start()
    copy.wait()
    token_ref[...] = jnp.zeros_like(token_ref)


def resident(weight, ready):
    weight = pltpu.with_memory_space_constraint(weight, pltpu.HBM)
    return pl.pallas_call(
        load_kernel,
        in_specs=[pl.BlockSpec(memory_space=pltpu.HBM), pl.BlockSpec(memory_space=pl.ANY)],
        out_specs=[VMEM, VMEM],
        out_shape=[
            pltpu.VMEM(weight.shape, weight.dtype),
            jax.ShapeDtypeStruct((8, 128), F32),
        ],
        scratch_shapes=[pltpu.SemaphoreType.DMA],
        compiler_params=params(1),
        cost_estimate=pl.CostEstimate(
            flops=0, transcendentals=0, bytes_accessed=4 * weight.size
        ),
    )(weight, ready)


def cost(rows, inner, cols, other_bytes):
    return pl.CostEstimate(
        flops=2 * rows * inner * cols,
        transcendentals=0,
        bytes_accessed=2 * inner * cols + other_bytes,
    )


def route_kernel(where_ref, lengths_ref, ids_ref, gates_ref, slots_ref, gate_ref, need_ref, used_ref):
    tokens = ids_ref.shape[1]
    spot = lax.broadcasted_iota(jnp.int32, (1, tokens), 1)
    cand = lax.shift_right_logical(spot, SEQ.bit_length() - 1)
    size = jnp.zeros_like(spot)
    start = jnp.zeros_like(spot)
    alive = jnp.int32(0)
    for c in range(lengths_ref.shape[0]):
        size = jnp.where(cand == c, lengths_ref[c], size)
        start = jnp.where(cand == c, alive, start)
        alive = alive + lengths_ref[c]
    step = spot - cand * SEQ
    live = step < size
    used_ref[...] = jnp.zeros_like(used_ref)
    for k in range(EXPERTS):
        expert = lax.rem(where_ref[0] + k, EXPERTS)
        first = (ids_ref[0:1, :] == expert) & live
        second = (ids_ref[1:2, :] == expert) & live
        used_ref[k : k + 1, :] = jnp.where(first | second, 1.0, 0.0)
        if k == 0:
            gate_ref[...] = jnp.where(first, gates_ref[0:1, :], 0.0) + jnp.where(
                second, gates_ref[1:2, :], 0.0
            )
    used = used_ref[...]
    source = lax.broadcasted_iota(jnp.int32, (tokens, tokens), 0)
    target = lax.broadcasted_iota(jnp.int32, (tokens, tokens), 1)
    earlier = jnp.where(source < target, 1.0, 0.0).astype(BF)
    rank = jnp.dot(used.astype(BF), earlier, preferred_element_type=F32)
    slots_ref[...] = jnp.where(used > 0.0, rank.astype(jnp.int32), -1)
    slots_ref[4:5, :] = jnp.where(live, start + step, -1)
    fullest = jnp.max(jnp.sum(used, axis=1, keepdims=True))
    need = jnp.float32(0.0)
    for rows, slots in TIERS:
        over = (alive > rows) | (fullest > float(slots))
        need = need + jnp.where(over, 1.0, 0.0)
    need_ref[...] = jnp.full(need_ref.shape, need, F32)


def route(plane, lengths, ids, gates):
    tokens = ids.shape[1]
    smem = pl.BlockSpec(memory_space=pltpu.SMEM)
    vmem = pl.BlockSpec(memory_space=pltpu.VMEM)
    return pl.pallas_call(
        route_kernel,
        in_specs=[smem, smem, vmem, vmem],
        out_specs=[vmem] * 3,
        out_shape=[
            jax.ShapeDtypeStruct((8, tokens), jnp.int32),
            jax.ShapeDtypeStruct((1, tokens), F32),
            jax.ShapeDtypeStruct((8, 128), F32),
        ],
        scratch_shapes=[pltpu.VMEM((8, tokens), F32)],
        compiler_params=params(16),
    )(plane.reshape(1), lengths, ids, gates)


def dispatch_kernel(slot_ref, x_ref, gain_ref, s0, s1, s2, s3, xc_ref):
    x = x_ref[...]
    scaled = (x.astype(F32) * gain_ref[...].astype(F32)).astype(BF)
    tokens = x.shape[0]
    for k, out in enumerate((s0, s1, s2, s3)):
        rows = out.shape[0]
        spots = lax.broadcasted_iota(jnp.int32, (rows, tokens), 0)
        chosen = jnp.where(slot_ref[k : k + 1, :] == spots, 1.0, 0.0).astype(BF)
        out[...] = jnp.dot(chosen, scaled, preferred_element_type=F32).astype(BF)
    rows = xc_ref.shape[0]
    spots = lax.broadcasted_iota(jnp.int32, (rows, tokens), 0)
    chosen = jnp.where(slot_ref[4:5, :] == spots, 1.0, 0.0).astype(BF)
    xc_ref[...] = jnp.dot(chosen, x, preferred_element_type=F32).astype(BF)


def dispatch(slot_rows, x, gain, slots, live_rows):
    cols = x.shape[1]
    block = jax.ShapeDtypeStruct((slots, cols), BF)
    return pl.pallas_call(
        dispatch_kernel,
        out_shape=[block] * 4 + [jax.ShapeDtypeStruct((live_rows, cols), BF)],
        compiler_params=params(16),
    )(slot_rows, x, gain)


def place(where_ref, blocks, wide_ref):
    own, across, *core = blocks
    rows, cols = wide_ref.shape[0], own.shape[1]
    count = own.shape[0] // rows
    for g in range(count):
        pieces = ((own, g), (across, g), (core[0], g), (core[-1], g if len(core) == 2 else count + g))
        for quarter, (block, piece) in enumerate(pieces):
            at = pl.multiple_of((g * 4 + where_ref[quarter]) * cols, 128)
            wide_ref[:, pl.ds(at, cols)] = block[piece * rows : (piece + 1) * rows, :]


def whole_specs(arrays):
    return [pl.BlockSpec(array.shape, lambda n, w: (0, 0)) for array in arrays]


def product(wide, weights):
    depth = weights[0].shape[0]
    value = None
    for j, w in enumerate(weights):
        part = jnp.dot(
            wide[:, j * depth : (j + 1) * depth], w[...], preferred_element_type=F32
        )
        value = part if value is None else value + part
    return value


def resident_product(where_ref, wide, weight, n, tile):
    depth = weight.shape[0] // 4
    value = None
    for j in range(wide.shape[1] // depth):
        first = pl.multiple_of(where_ref[4 + j] * depth, 128)
        part = jnp.dot(
            wide[:, j * depth : (j + 1) * depth],
            weight[pl.ds(first, depth), pl.ds(pl.multiple_of(n * tile, 128), tile)],
            preferred_element_type=F32,
        )
        value = part if value is None else value + part
    return value


def weight_specs(count, depth, tile):
    return [
        pl.BlockSpec((depth, tile), functools.partial(lambda j, n, w: (w[4 + j], n), j))
        for j in range(count)
    ]


def by_slot(slot_ref, values, slots):
    spots = lax.broadcasted_iota(jnp.int32, (slots, slot_ref.shape[1]), 0)
    chosen = jnp.where(slot_ref[0:1, :] == spots, values, 0.0)
    return jnp.sum(chosen, axis=1, keepdims=True)


def hidden_kernel(given, count, first, last, where_ref, *refs):
    blocks, refs = refs[:given], refs[given:]
    wg, wu, refs = refs[0], refs[1 : 1 + count], refs[1 + count :]
    if not first:
        g_in, u_in, refs = refs[0], refs[1], refs[2:]
    if last:
        slot_ref, squares_ref, h_out, wide, inv = refs
    else:
        g_out, u_out, wide = refs
    n = pl.program_id(0)
    tile = wu[0].shape[1]

    @pl.when(n == 0)
    def _():
        place(where_ref, blocks, wide)
        if last:
            scale = 1.0 / jnp.sqrt(squares_ref[...] / D + epsilon)
            inv[...] = by_slot(slot_ref, scale, inv.shape[0])

    g = resident_product(where_ref, wide, wg, n, tile)
    u = product(wide, wu)
    at = pl.ds(pl.multiple_of(n * tile, 128), tile)
    if not first:
        g = g + g_in[:, at]
        u = u + u_in[:, at]
    if last:
        g = g * inv[...]
        u = u * inv[...]
        h_out[:, at] = (g / (1.0 + jnp.exp(-g)) * u).astype(BF)
    else:
        g_out[:, at] = g
        u_out[:, at] = u


def hidden_part(where, blocks, slots, w_gate, w_up, sums, rows_of):
    cols = blocks[0].shape[1]
    count = blocks[0].shape[0] // slots
    inner, width = w_up.shape
    tile, depth = 512 if slots > 272 else 1024, inner // 4
    first, last = sums is None, rows_of is not None
    w_gate = pltpu.with_memory_space_constraint(w_gate, pltpu.VMEM)
    w_up = pltpu.with_memory_space_constraint(w_up, pltpu.HBM)
    ins = [where, *blocks, w_gate] + [w_up] * count
    specs = whole_specs(blocks) + [VMEM] + weight_specs(count, depth, tile)
    aliases = {}
    if not first:
        if not last:
            aliases = {len(ins): 0, len(ins) + 1: 1}
        ins += [pltpu.with_memory_space_constraint(part, pltpu.VMEM) for part in sums]
        specs += [VMEM] * 2
    if last:
        ins += rows_of
        specs += whole_specs(rows_of)
        outs, out_specs = pltpu.VMEM((slots, width), BF), VMEM
    else:
        outs, out_specs = [pltpu.VMEM((slots, width), F32)] * 2, [VMEM] * 2
    return pl.pallas_call(
        functools.partial(hidden_kernel, len(blocks), count, first, last),
        out_shape=outs,
        grid_spec=pltpu.PrefetchScalarGridSpec(
            num_scalar_prefetch=1,
            grid=(width // tile,),
            in_specs=specs,
            out_specs=out_specs,
            scratch_shapes=[pltpu.VMEM((slots, 4 * count * cols), BF)]
            + [pltpu.VMEM((slots, 1), F32)] * last,
        ),
        input_output_aliases=aliases,
        compiler_params=params(30),
        cost_estimate=cost(slots, 8 if first else count * depth, 2 * width, 0),
    )(*ins)


def down_kernel(where_ref, h_ref, w_ref, slot_ref, row_ref, *refs):
    *outs, total, gate_ref = refs
    rows = h_ref.shape[0]
    step = pl.program_id(0)

    @pl.when(step == 0)
    def _():
        gate_ref[...] = by_slot(slot_ref, row_ref[...], rows)

    value = jnp.dot(h_ref[...], w_ref[...], preferred_element_type=F32) * gate_ref[...]
    total[...] = value
    for c in range(4):
        own, across, core = outs[3 * (c // 2) : 3 * (c // 2) + 3]
        g = c % 2

        @pl.when(step == c)
        def _():
            cols = own.shape[1]
            for b in range(4):
                part = total[:, pl.ds(pl.multiple_of(where_ref[b] * cols, 128), cols)]
                if b < 2:
                    (own, across)[b][g * rows : (g + 1) * rows, :] = part
                else:
                    first = ((b - 2) * 2 + g) * rows
                    core[first : first + rows, :] = part.astype(BF)


def down_all(where, hidden, w_down, slot_rows, gate_row, cols):
    rows, inner = hidden.shape
    hidden = pltpu.with_memory_space_constraint(hidden, pltpu.VMEM)
    sizes = ((2 * rows, F32), (2 * rows, F32), (4 * rows, BF)) * 2
    return pl.pallas_call(
        down_kernel,
        out_shape=[jax.ShapeDtypeStruct((count, cols), kind) for count, kind in sizes],
        grid_spec=pltpu.PrefetchScalarGridSpec(
            num_scalar_prefetch=1,
            grid=(4,),
            in_specs=[
                VMEM,
                pl.BlockSpec((inner, 4 * cols), lambda j, w: (0, w[4 + j])),
                *whole_specs([slot_rows, gate_row]),
            ],
            out_specs=[pl.BlockSpec((count, cols), lambda j, w: (0, 0)) for count, _ in sizes],
            scratch_shapes=[pltpu.VMEM((rows, 4 * cols), F32), pltpu.VMEM((rows, 1), F32)],
        ),
        compiler_params=params(40),
        cost_estimate=cost(rows, inner, 16 * cols, 64 * rows * cols),
    )(where, hidden, w_down, slot_rows, gate_row)


def mix_kernel(slot_ref, x_ref, gain_ref, e0, e2, e1, e3, out_ref, squares_ref):
    rows = x_ref.shape[0]
    mixture = x_ref[...].astype(F32)
    moe = jnp.zeros_like(mixture)
    for j, part in enumerate((e0, e1, e2, e3)):
        slots = part.shape[0]
        spots = lax.broadcasted_iota(jnp.int32, (rows, slots), 1)
        chosen = jnp.where(slot_ref[:, j : j + 1] == spots, 1.0, 0.0).astype(BF)
        moe = moe + jnp.dot(chosen, part[...], preferred_element_type=F32)
    mixture = mixture + moe
    out_ref[...] = (mixture * gain_ref[...].astype(F32)).astype(BF)
    squares_ref[...] = jnp.sum(mixture * mixture, axis=1, keepdims=True)


def mix(slot_cols, x, gain, parts):
    rows, cols = x.shape
    return pl.pallas_call(
        mix_kernel,
        out_shape=[
            jax.ShapeDtypeStruct((rows, cols), BF),
            jax.ShapeDtypeStruct((rows, 1), F32),
        ],
        compiler_params=params(16),
    )(slot_cols, x, gain, *parts)


def vocab_kernel(given, count, first, last, tile, where_ref, *refs):
    blocks, refs = refs[:given], refs[given:]
    weight, refs = refs[0], refs[1:]
    if not first:
        sum_in, refs = refs[0], refs[1:]
    if last:
        inv, local_ids, out, wide, top, total, picked = refs
    else:
        out, wide = refs
    n = pl.program_id(0)

    @pl.when(n == 0)
    def _():
        place(where_ref, blocks, wide)

    value = resident_product(where_ref, wide, weight, n, tile)
    at = pl.ds(pl.multiple_of(n * tile, 128), tile)
    if not first:
        value = value + sum_in[:, at]
    if not last:
        out[:, at] = value
        return
    rows = value.shape[0]
    same = lax.broadcasted_iota(jnp.int32, (rows, rows), 0) == lax.broadcasted_iota(
        jnp.int32, (rows, rows), 1
    )
    squares = jnp.sum(jnp.where(same, inv[...], 0.0), axis=1, keepdims=True)
    logits = value * (1.0 / jnp.sqrt(squares / D + epsilon))
    column = n * tile + lax.broadcasted_iota(jnp.int32, logits.shape, 1)
    tile_pick = jnp.sum(jnp.where(column == local_ids[...], logits, 0.0), axis=1, keepdims=True)
    tile_top = jnp.max(logits, axis=1, keepdims=True)

    @pl.when(n == 0)
    def _():
        top[...] = tile_top
        total[...] = jnp.sum(jnp.exp(logits - tile_top), axis=1, keepdims=True)
        picked[...] = tile_pick

    @pl.when(n > 0)
    def _():
        new_top = jnp.maximum(top[...], tile_top)
        total[...] = total[...] * jnp.exp(top[...] - new_top) + jnp.sum(
            jnp.exp(logits - new_top), axis=1, keepdims=True
        )
        top[...] = new_top
        picked[...] = picked[...] + tile_pick

    @pl.when(n == pl.num_programs(0) - 1)
    def _():
        lane = lax.broadcasted_iota(jnp.int32, out.shape, 1)
        out[...] = jnp.where(lane == 0, top[...], jnp.where(lane == 1, total[...], picked[...]))


def vocab_part(where, blocks, rows, lm_head, sums, inv, local_ids):
    cols = blocks[0].shape[1]
    count = blocks[0].shape[0] // rows
    inner, width = lm_head.shape
    tile = 512 if rows <= 352 else 256
    first, last = sums is None, inv is not None
    lm_head = pltpu.with_memory_space_constraint(lm_head, pltpu.VMEM)
    ins = [where, *blocks, lm_head]
    specs = whole_specs(blocks) + [VMEM]
    aliases = {}
    if not first:
        if not last:
            aliases = {len(ins): 0}
        ins.append(pltpu.with_memory_space_constraint(sums, pltpu.VMEM))
        specs.append(VMEM)
    scratch = [pltpu.VMEM((rows, 4 * count * cols), BF)]
    if last:
        ins += [inv, local_ids]
        specs += whole_specs([inv, local_ids])
        outs = jax.ShapeDtypeStruct((rows, 128), F32)
        out_specs = pl.BlockSpec((rows, 128), lambda n, w: (0, 0))
        scratch += [pltpu.VMEM((rows, 1), F32)] * 3
    else:
        outs, out_specs = pltpu.VMEM((rows, width), F32), VMEM
    return pl.pallas_call(
        functools.partial(vocab_kernel, len(blocks), count, first, last, tile),
        out_shape=outs,
        grid_spec=pltpu.PrefetchScalarGridSpec(
            num_scalar_prefetch=1,
            grid=(width // tile,),
            in_specs=specs,
            out_specs=out_specs,
            scratch_shapes=scratch,
        ),
        input_output_aliases=aliases,
        compiler_params=params(32),
        cost_estimate=cost(rows, 8 if first else inner * count // 4, width, 0),
    )(*ins)


def spread(by_offset, squares, load, part):
    own0 = by_offset[0]
    a1 = send(by_offset[1], plane_pairs(1))
    a3 = send(by_offset[3], plane_pairs(3))
    row0 = send(own0, xor_pairs(2))
    core0 = send(own0, xor_pairs(1))
    diagonal0 = send(own0, xor_pairs(3))
    weight, token = load(own0)

    near = jnp.concatenate([a1, a3], axis=0)
    row0, core0, diagonal0, near, squares, far, token = lax.optimization_barrier(
        (row0, core0, diagonal0, near, squares, by_offset[2], token)
    )
    a2 = send(far, plane_pairs(2))
    row13 = send(near, xor_pairs(2))
    squares = squares + token[:1, :1]
    more = [send(squares, xor_pairs(mask)) for mask in (1, 2, 3)]
    sums = part(0, weight, (own0, row0, core0, diagonal0), None, None)

    a2, row13, squares, more, sums = lax.optimization_barrier((a2, row13, squares, more, sums))
    row2 = send(a2, xor_pairs(2))
    core13 = send(jnp.concatenate([near, row13], axis=0), xor_pairs(1))
    squares = squares + more[0] + (more[1] + more[2])
    more = [send(squares, plane_pairs(k)) for k in (1, 2, 3)]
    sums = part(1, weight, (near, row13, core13), sums, None)

    row2, squares, more, sums = lax.optimization_barrier((row2, squares, more, sums))
    squares = squares + more[0] + (more[1] + more[2])
    core2 = send(jnp.concatenate([a2, row2], axis=0), xor_pairs(1))
    return part(2, weight, (a2, row2, core2), sums, squares)


def live_part(
    x,
    norm_gain,
    final_gain,
    w_gate,
    w_up,
    w_down,
    lm_head,
    target_ids,
    slot_rows,
    gate_row,
    in_squares,
    where,
    down_at,
    first_id,
    live_rows,
    slots,
):
    cols = x.shape[1]
    *picked_rows, x_live = dispatch(slot_rows, x, norm_gain, slots, live_rows)
    packed = slot_rows[4]
    live_at = packed[None, :] == jnp.arange(live_rows, dtype=jnp.int32)[:, None]
    slot_live = jnp.stack(
        [
            jnp.sum(jnp.where(live_at, slot_rows[(4 - k) % 4][None, :] + 1, 0), axis=1) - 1
            for k in range(4)
        ],
        axis=1,
    )
    local_ids = (
        jnp.sum(jnp.where(live_at, target_ids[None, :], 0), axis=1, keepdims=True) - first_id
    )

    def hidden_step(group, weight, blocks, sums, squares):
        rows_of = None if squares is None else [slot_rows, squares]
        return hidden_part(where[group], blocks, slots, weight, w_up, sums, rows_of)

    hidden = spread(
        picked_rows, in_squares, functools.partial(resident, w_gate), hidden_step
    )

    two = 2 * slots
    own_a, row_a, core_a, own_b, row_b, core_b = down_all(
        down_at, hidden, w_down, slot_rows, gate_row, cols
    )
    heard_a = send(core_a, xor_pairs(1))
    heard_b = send(core_b, xor_pairs(1))
    across_a = (row_a + heard_a[two:].astype(F32)).astype(BF)
    crossed_a = send(across_a, xor_pairs(2))
    total_a = (own_a + heard_a[:two].astype(F32) + crossed_a.astype(F32)).astype(BF)
    part2 = send(total_a[:slots], plane_pairs(2))
    part1 = send(total_a[slots:], plane_pairs(1))
    across_b = (row_b + heard_b[two:].astype(F32)).astype(BF)
    crossed_b = send(after(across_b, crossed_a), xor_pairs(2))
    total_b = (own_b + heard_b[:two].astype(F32) + crossed_b.astype(F32)).astype(BF)
    part3 = send(total_b[:slots], plane_pairs(3))
    parts = (total_b[slots:], part2, part1, part3)

    scaled, squares = mix(slot_live, x_live, final_gain, parts)

    def vocab_step(group, weight, blocks, sums, squares):
        return vocab_part(where[group], blocks, live_rows, weight, sums, squares, local_ids)

    squares = squares.reshape(1, -1)
    stats = spread([scaled] * 4, squares, lambda own: resident(lm_head, squares), vocab_step)
    spot = packed[:, None] == jnp.arange(live_rows, dtype=jnp.int32)[None, :]
    return jnp.stack(
        [jnp.sum(jnp.where(spot, stats[:, j][None, :], 0.0), axis=1) for j in range(3)]
    )


def fast_body(
    residual_in,
    norm_gain,
    final_gain,
    expert_ids,
    gate_values,
    w_gate,
    w_up,
    w_down,
    lm_head,
    target_ids,
    lengths,
):
    tokens = residual_in.shape[0]
    devices = lax.axis_size("tensor")
    me = lax.axis_index("tensor").astype(jnp.int32)
    plane, row, core = me >> 2, (me >> 1) & 1, me & 1
    slot_rows, gate_row, need = route(plane, lengths, expert_ids.T, gate_values.T)
    need = jnp.maximum(need, lax.ppermute(need, "groups", [(0, 1), (1, 0)]))

    at = [row * 2 + core, (1 - row) * 2 + core, row * 2 + 1 - core, (1 - row) * 2 + 1 - core]
    planes = [(plane + k) & 3 for k in range(4)]
    where = [jnp.stack(at + [planes[(4 - k) % 4] for k in group]) for group in CHUNKS]
    down_at = jnp.stack(at + [planes[k] for k in (2, 1, 3, 0)])
    stream = residual_in.astype(F32)
    in_squares = jnp.sum(stream * stream, axis=1)[None, :]

    stats = lax.switch(
        need[0, 0].astype(jnp.int32),
        [
            functools.partial(live_part, live_rows=rows, slots=slots)
            for rows, slots in TIERS + ((tokens, CAP),)
        ],
        residual_in,
        norm_gain[None, :],
        final_gain[None, :],
        w_gate,
        w_up,
        w_down,
        lm_head,
        target_ids,
        slot_rows,
        gate_row,
        in_squares,
        where,
        down_at,
        me * lm_head.shape[1],
    )
    rows_dev = tokens // devices
    stats = stats.reshape(3, devices, rows_dev).transpose(1, 0, 2)
    stats = lax.all_to_all(stats, "tensor", 0, 0, tiled=True)
    top = jnp.max(stats[:, 0], axis=0)
    total = jnp.sum(stats[:, 1] * jnp.exp(stats[:, 0] - top[None, :]), axis=0)
    logprob = jnp.sum(stats[:, 2], axis=0) - top - jnp.log(total)
    own_live = lax.dynamic_slice_in_dim(slot_rows[4], me * rows_dev, rows_dev) >= 0
    return jnp.where(own_live, logprob, 0.0)


def body(*args):
    if lax.axis_size("tensor") == 16 and lax.axis_size("groups") == 2:
        return fast_body(*args)
    return plain_body(*args)


def solution(mesh):
    return jax.shard_map(
        body,
        mesh=mesh,
        in_specs=(
            P("groups", "tensor"),
            P("tensor"),
            P("tensor"),
            P("groups", None),
            P("groups", None),
            P(None, "tensor"),
            P(None, "tensor"),
            P("tensor", None),
            P(None, "tensor"),
            P("groups"),
            P("groups"),
        ),
        out_specs=P(("groups", "tensor")),
        check_vma=False,
    )
```

```python
import functools
import jax
import jax.numpy as jnp
from jax import lax
from jax.experimental import pallas as pl
from jax.experimental.pallas import tpu as pltpu
from jax.sharding import PartitionSpec as P

D = 6144
EXPERTS = 4
EXP_FF = 8192
TOP = 2
SEQ = 64
CAP = 384


epsilon = 1e-05


def combined_all(array, axis, combine):
    everything = jax.tree.map(lambda part: lax.all_gather(part, axis), array)
    leading = jax.tree.map(lambda part: part[0], everything)

    def hop(k, so_far):
        return combine(so_far, jax.tree.map(lambda part: part[k], everything))

    return lax.fori_loop(1, lax.axis_size(axis), hop, leading)


def slots_of(expert_ids):
    flat_ids = expert_ids.reshape(-1)
    pairs = jnp.arange(flat_ids.shape[0], dtype=jnp.int32)
    before = (pairs[None, :] < pairs[:, None]) & (flat_ids[None, :] == flat_ids[:, None])
    return jnp.sum(before.astype(jnp.int32), axis=1).reshape(expert_ids.shape)


def slot_tokens(expert_ids, slot_index):
    slot_code = (expert_ids * CAP + slot_index).reshape(-1)
    owner = jnp.arange(slot_code.shape[0], dtype=jnp.int32) // TOP
    wanted = jnp.arange(EXPERTS * CAP, dtype=jnp.int32)
    matches = slot_code[None, :] == wanted[:, None]
    return jnp.sum(jnp.where(matches, owner[None, :] + 1, 0), axis=1) - 1


def normalize(values, squares_total, gain_vec):
    return (
        values / jnp.sqrt(squares_total[:, None] / D + epsilon) * gain_vec.astype(jnp.float32)
    ).astype(jnp.bfloat16)


def plain_body(
    residual_in,
    norm_gain,
    final_gain,
    expert_ids,
    gate_values,
    w_gate,
    w_up,
    w_down,
    lm_head,
    target_ids,
    lengths,
):
    tokens, feature_cols = residual_in.shape
    hidden_dev = w_gate.shape[1]
    per_expert = EXP_FF // hidden_dev
    expert_now = lax.axis_index("tensor") // per_expert
    stream = residual_in.astype(jnp.float32)
    in_total = lax.psum(jnp.sum(stream * stream, axis=1), "tensor")
    normed = normalize(stream, in_total, norm_gain)
    slot_index = slots_of(expert_ids)
    token_of = slot_tokens(expert_ids, slot_index)
    zero_bf = jnp.zeros((), jnp.bfloat16)
    own_slots = lax.dynamic_slice_in_dim(token_of, expert_now * CAP, CAP)
    occupied = own_slots >= 0
    safe_index = jnp.maximum(own_slots, 0)
    slot_rows = jnp.where(
        occupied[:, None], lax.all_gather(normed, "tensor", axis=1, tiled=True)[safe_index], zero_bf
    )
    gate_out = jnp.dot(slot_rows, w_gate, preferred_element_type=jnp.float32)
    up_out = jnp.dot(slot_rows, w_up, preferred_element_type=jnp.float32)
    hidden = (jax.nn.silu(gate_out) * up_out).astype(jnp.bfloat16)
    partial_value = jnp.dot(hidden, w_down, preferred_element_type=jnp.float32)
    weight_own = jnp.where(expert_ids == expert_now, gate_values, jnp.zeros_like(gate_values))
    weighted = (
        weight_own[:, 0:1] * partial_value[slot_index[:, 0]]
        + weight_own[:, 1:2] * partial_value[slot_index[:, 1]]
    )
    moe_cols = lax.psum_scatter(weighted, "tensor", scatter_dimension=1, tiled=True)
    mixture = stream + moe_cols
    out_total = lax.psum(jnp.sum(mixture * mixture, axis=1), "tensor")
    normed_out = normalize(mixture, out_total, final_gain)
    vocab_dev = lm_head.shape[1]
    logits = jnp.dot(
        lax.all_gather(normed_out, "tensor", axis=1, tiled=True),
        lm_head,
        preferred_element_type=jnp.float32,
    )
    row_max = jnp.max(logits, axis=1)
    row_total = jnp.sum(jnp.exp(logits - row_max[:, None]), axis=1)
    local_ids = target_ids - lax.axis_index("tensor") * vocab_dev
    vocab_cols = jnp.arange(vocab_dev, dtype=jnp.int32)
    picked = jnp.sum(jnp.where(vocab_cols[None, :] == local_ids[:, None], logits, 0.0), axis=1)

    def joined(earlier, later):
        merged_max = jnp.maximum(earlier[0], later[0])
        merged_total = earlier[1] * jnp.exp(earlier[0] - merged_max) + later[1] * jnp.exp(
            later[0] - merged_max
        )
        return (merged_max, merged_total, earlier[2] + later[2])

    merged_max, merged_total, target_logit = combined_all(
        (row_max, row_total, picked), "tensor", joined
    )
    logprob = target_logit - merged_max - jnp.log(merged_total)
    rows_dev = tokens // lax.axis_size("tensor")
    first_row = lax.axis_index("tensor") * rows_dev
    own_rows = lax.dynamic_slice_in_dim(logprob, first_row, rows_dev)
    position = first_row + jnp.arange(rows_dev, dtype=jnp.int32)
    in_length = position % SEQ < lengths[position // SEQ]
    return jnp.where(in_length, own_rows, jnp.zeros_like(own_rows)).astype(jnp.float32)

TIERS = ((304, 240), (352, 272))
CHUNKS = ((0,), (1, 3), (2,))
VMEM = pl.BlockSpec(memory_space=pltpu.VMEM)
BF = jnp.bfloat16
F32 = jnp.float32


def send(array, pairs):
    return lax.ppermute(array, "tensor", pairs)


def xor_pairs(mask):
    return [(i, i ^ mask) for i in range(16)]


def plane_pairs(k):
    return [(i, ((i >> 2) + k) % 4 * 4 + (i & 3)) for i in range(16)]


def after(value, *others):
    return lax.optimization_barrier((value, *others))[0]


def params(mebibytes):
    return pltpu.CompilerParams(vmem_limit_bytes=mebibytes * 1024 * 1024)


def load_kernel(w_ref, after_ref, out_ref, token_ref, sem):
    copy = pltpu.make_async_copy(w_ref, out_ref, sem)
    copy.start()
    copy.wait()
    token_ref[...] = jnp.zeros_like(token_ref)


def resident(weight, ready):
    weight = pltpu.with_memory_space_constraint(weight, pltpu.HBM)
    return pl.pallas_call(
        load_kernel,
        in_specs=[pl.BlockSpec(memory_space=pltpu.HBM), pl.BlockSpec(memory_space=pl.ANY)],
        out_specs=[VMEM, VMEM],
        out_shape=[
            pltpu.VMEM(weight.shape, weight.dtype),
            jax.ShapeDtypeStruct((8, 128), F32),
        ],
        scratch_shapes=[pltpu.SemaphoreType.DMA],
        compiler_params=params(1),
        cost_estimate=pl.CostEstimate(
            flops=0, transcendentals=0, bytes_accessed=4 * weight.size
        ),
    )(weight, ready)


def cost(rows, inner, cols, other_bytes):
    return pl.CostEstimate(
        flops=2 * rows * inner * cols,
        transcendentals=0,
        bytes_accessed=2 * inner * cols + other_bytes,
    )


def route_kernel(where_ref, lengths_ref, ids_ref, gates_ref, slots_ref, gate_ref, need_ref, used_ref):
    tokens = ids_ref.shape[1]
    spot = lax.broadcasted_iota(jnp.int32, (1, tokens), 1)
    cand = lax.shift_right_logical(spot, SEQ.bit_length() - 1)
    size = jnp.zeros_like(spot)
    start = jnp.zeros_like(spot)
    alive = jnp.int32(0)
    for c in range(lengths_ref.shape[0]):
        size = jnp.where(cand == c, lengths_ref[c], size)
        start = jnp.where(cand == c, alive, start)
        alive = alive + lengths_ref[c]
    step = spot - cand * SEQ
    live = step < size
    used_ref[...] = jnp.zeros_like(used_ref)
    for k in range(EXPERTS):
        expert = lax.rem(where_ref[0] + k, EXPERTS)
        first = (ids_ref[0:1, :] == expert) & live
        second = (ids_ref[1:2, :] == expert) & live
        used_ref[k : k + 1, :] = jnp.where(first | second, 1.0, 0.0)
        if k == 0:
            gate_ref[...] = jnp.where(first, gates_ref[0:1, :], 0.0) + jnp.where(
                second, gates_ref[1:2, :], 0.0
            )
    used = used_ref[...]
    source = lax.broadcasted_iota(jnp.int32, (tokens, tokens), 0)
    target = lax.broadcasted_iota(jnp.int32, (tokens, tokens), 1)
    earlier = jnp.where(source < target, 1.0, 0.0).astype(BF)
    rank = jnp.dot(used.astype(BF), earlier, preferred_element_type=F32)
    slots_ref[...] = jnp.where(used > 0.0, rank.astype(jnp.int32), -1)
    slots_ref[4:5, :] = jnp.where(live, start + step, -1)
    fullest = jnp.max(jnp.sum(used, axis=1, keepdims=True))
    need = jnp.float32(0.0)
    for rows, slots in TIERS:
        over = (alive > rows) | (fullest > float(slots))
        need = need + jnp.where(over, 1.0, 0.0)
    need_ref[...] = jnp.full(need_ref.shape, need, F32)


def route(plane, lengths, ids, gates):
    tokens = ids.shape[1]
    smem = pl.BlockSpec(memory_space=pltpu.SMEM)
    vmem = pl.BlockSpec(memory_space=pltpu.VMEM)
    return pl.pallas_call(
        route_kernel,
        in_specs=[smem, smem, vmem, vmem],
        out_specs=[vmem] * 3,
        out_shape=[
            jax.ShapeDtypeStruct((8, tokens), jnp.int32),
            jax.ShapeDtypeStruct((1, tokens), F32),
            jax.ShapeDtypeStruct((8, 128), F32),
        ],
        scratch_shapes=[pltpu.VMEM((8, tokens), F32)],
        compiler_params=params(16),
    )(plane.reshape(1), lengths, ids, gates)


def dispatch_kernel(slot_ref, x_ref, gain_ref, s0, s1, s2, s3, xc_ref):
    x = x_ref[...]
    scaled = (x.astype(F32) * gain_ref[...].astype(F32)).astype(BF)
    tokens = x.shape[0]
    for k, out in enumerate((s0, s1, s2, s3)):
        rows = out.shape[0]
        spots = lax.broadcasted_iota(jnp.int32, (rows, tokens), 0)
        chosen = jnp.where(slot_ref[k : k + 1, :] == spots, 1.0, 0.0).astype(BF)
        out[...] = jnp.dot(chosen, scaled, preferred_element_type=F32).astype(BF)
    rows = xc_ref.shape[0]
    spots = lax.broadcasted_iota(jnp.int32, (rows, tokens), 0)
    chosen = jnp.where(slot_ref[4:5, :] == spots, 1.0, 0.0).astype(BF)
    xc_ref[...] = jnp.dot(chosen, x, preferred_element_type=F32).astype(BF)


def dispatch(slot_rows, x, gain, slots, live_rows):
    cols = x.shape[1]
    block = jax.ShapeDtypeStruct((slots, cols), BF)
    return pl.pallas_call(
        dispatch_kernel,
        out_shape=[block] * 4 + [jax.ShapeDtypeStruct((live_rows, cols), BF)],
        compiler_params=params(16),
    )(slot_rows, x, gain)


def place(where_ref, blocks, wide_ref):
    own, across, *core = blocks
    rows, cols = wide_ref.shape[0], own.shape[1]
    count = own.shape[0] // rows
    for g in range(count):
        pieces = ((own, g), (across, g), (core[0], g), (core[-1], g if len(core) == 2 else count + g))
        for quarter, (block, piece) in enumerate(pieces):
            at = pl.multiple_of((g * 4 + where_ref[quarter]) * cols, 128)
            wide_ref[:, pl.ds(at, cols)] = block[piece * rows : (piece + 1) * rows, :]


def whole_specs(arrays):
    return [pl.BlockSpec(array.shape, lambda n, w: (0, 0)) for array in arrays]


def product(wide, weights):
    depth = weights[0].shape[0]
    value = None
    for j, w in enumerate(weights):
        part = jnp.dot(
            wide[:, j * depth : (j + 1) * depth], w[...], preferred_element_type=F32
        )
        value = part if value is None else value + part
    return value


def resident_product(where_ref, wide, weight, n, tile):
    depth = weight.shape[0] // 4
    value = None
    for j in range(wide.shape[1] // depth):
        first = pl.multiple_of(where_ref[4 + j] * depth, 128)
        part = jnp.dot(
            wide[:, j * depth : (j + 1) * depth],
            weight[pl.ds(first, depth), pl.ds(pl.multiple_of(n * tile, 128), tile)],
            preferred_element_type=F32,
        )
        value = part if value is None else value + part
    return value


def weight_specs(count, depth, tile):
    return [
        pl.BlockSpec((depth, tile), functools.partial(lambda j, n, w: (w[4 + j], n), j))
        for j in range(count)
    ]


def by_slot(slot_ref, values, slots):
    spots = lax.broadcasted_iota(jnp.int32, (slots, slot_ref.shape[1]), 0)
    chosen = jnp.where(slot_ref[0:1, :] == spots, values, 0.0)
    return jnp.sum(chosen, axis=1, keepdims=True)


def hidden_kernel(given, count, first, last, where_ref, *refs):
    blocks, refs = refs[:given], refs[given:]
    wg, wu, refs = refs[0], refs[1 : 1 + count], refs[1 + count :]
    if not first:
        g_in, u_in, refs = refs[0], refs[1], refs[2:]
    if last:
        slot_ref, squares_ref, h_out, wide, inv = refs
    else:
        g_out, u_out, wide = refs
    n = pl.program_id(0)
    tile = wu[0].shape[1]

    @pl.when(n == 0)
    def _():
        place(where_ref, blocks, wide)
        if last:
            scale = 1.0 / jnp.sqrt(squares_ref[...] / D + epsilon)
            inv[...] = by_slot(slot_ref, scale, inv.shape[0])

    g = resident_product(where_ref, wide, wg, n, tile)
    u = product(wide, wu)
    at = pl.ds(pl.multiple_of(n * tile, 128), tile)
    if not first:
        g = g + g_in[:, at]
        u = u + u_in[:, at]
    if last:
        g = g * inv[...]
        u = u * inv[...]
        h_out[:, at] = (g / (1.0 + jnp.exp(-g)) * u).astype(BF)
    else:
        g_out[:, at] = g
        u_out[:, at] = u


def hidden_part(where, blocks, slots, w_gate, w_up, sums, rows_of):
    cols = blocks[0].shape[1]
    count = blocks[0].shape[0] // slots
    inner, width = w_up.shape
    tile, depth = 512 if slots > 272 else 1024, inner // 4
    first, last = sums is None, rows_of is not None
    w_gate = pltpu.with_memory_space_constraint(w_gate, pltpu.VMEM)
    w_up = pltpu.with_memory_space_constraint(w_up, pltpu.HBM)
    ins = [where, *blocks, w_gate] + [w_up] * count
    specs = whole_specs(blocks) + [VMEM] + weight_specs(count, depth, tile)
    aliases = {}
    if not first:
        if not last:
            aliases = {len(ins): 0, len(ins) + 1: 1}
        ins += [pltpu.with_memory_space_constraint(part, pltpu.VMEM) for part in sums]
        specs += [VMEM] * 2
    if last:
        ins += rows_of
        specs += whole_specs(rows_of)
        outs, out_specs = pltpu.VMEM((slots, width), BF), VMEM
    else:
        outs, out_specs = [pltpu.VMEM((slots, width), F32)] * 2, [VMEM] * 2
    return pl.pallas_call(
        functools.partial(hidden_kernel, len(blocks), count, first, last),
        out_shape=outs,
        grid_spec=pltpu.PrefetchScalarGridSpec(
            num_scalar_prefetch=1,
            grid=(width // tile,),
            in_specs=specs,
            out_specs=out_specs,
            scratch_shapes=[pltpu.VMEM((slots, 4 * count * cols), BF)]
            + [pltpu.VMEM((slots, 1), F32)] * last,
        ),
        input_output_aliases=aliases,
        compiler_params=params(30),
        cost_estimate=cost(slots, 8 if first else count * depth, 2 * width, 0),
    )(*ins)


def down_kernel(where_ref, h_ref, w_ref, slot_ref, row_ref, *refs):
    *outs, total, gate_ref = refs
    rows = h_ref.shape[0]
    step = pl.program_id(0)

    @pl.when(step == 0)
    def _():
        gate_ref[...] = by_slot(slot_ref, row_ref[...], rows)

    value = jnp.dot(h_ref[...], w_ref[...], preferred_element_type=F32) * gate_ref[...]
    total[...] = value
    for c, (group, g, count) in enumerate(((0, 0, 1), (1, 0, 2), (1, 1, 2), (2, 0, 1))):
        own, across, core = outs[3 * group : 3 * group + 3]

        @pl.when(step == c)
        def _():
            cols = own.shape[1]
            for b in range(4):
                part = total[:, pl.ds(pl.multiple_of(where_ref[b] * cols, 128), cols)]
                if b < 2:
                    (own, across)[b][g * rows : (g + 1) * rows, :] = part
                else:
                    first = ((b - 2) * count + g) * rows
                    core[first : first + rows, :] = part.astype(BF)


def down_all(where, hidden, w_down, slot_rows, gate_row, cols):
    rows, inner = hidden.shape
    hidden = pltpu.with_memory_space_constraint(hidden, pltpu.VMEM)
    sizes = []
    for chunks in (1, 2, 1):
        sizes += [(chunks * rows, F32), (chunks * rows, F32), (2 * chunks * rows, BF)]
    return pl.pallas_call(
        down_kernel,
        out_shape=[jax.ShapeDtypeStruct((count, cols), kind) for count, kind in sizes],
        grid_spec=pltpu.PrefetchScalarGridSpec(
            num_scalar_prefetch=1,
            grid=(4,),
            in_specs=[
                VMEM,
                pl.BlockSpec((inner, 4 * cols), lambda j, w: (0, w[4 + j])),
                *whole_specs([slot_rows, gate_row]),
            ],
            out_specs=[pl.BlockSpec((count, cols), lambda j, w: (0, 0)) for count, _ in sizes],
            scratch_shapes=[pltpu.VMEM((rows, 4 * cols), F32), pltpu.VMEM((rows, 1), F32)],
        ),
        compiler_params=params(40),
        cost_estimate=cost(rows, inner, 16 * cols, 64 * rows * cols),
    )(where, hidden, w_down, slot_rows, gate_row)


def mix_kernel(slot_ref, x_ref, gain_ref, e0, e2, e1, e3, out_ref, squares_ref):
    rows = x_ref.shape[0]
    mixture = x_ref[...].astype(F32)
    moe = jnp.zeros_like(mixture)
    for j, part in enumerate((e0, e1, e2, e3)):
        slots = part.shape[0]
        spots = lax.broadcasted_iota(jnp.int32, (rows, slots), 1)
        chosen = jnp.where(slot_ref[:, j : j + 1] == spots, 1.0, 0.0).astype(BF)
        moe = moe + jnp.dot(chosen, part[...], preferred_element_type=F32)
    mixture = mixture + moe
    out_ref[...] = (mixture * gain_ref[...].astype(F32)).astype(BF)
    squares_ref[...] = jnp.sum(mixture * mixture, axis=1, keepdims=True)


def mix(slot_cols, x, gain, parts):
    rows, cols = x.shape
    return pl.pallas_call(
        mix_kernel,
        out_shape=[
            jax.ShapeDtypeStruct((rows, cols), BF),
            jax.ShapeDtypeStruct((rows, 1), F32),
        ],
        compiler_params=params(16),
    )(slot_cols, x, gain, *parts)


def vocab_kernel(given, count, first, last, tile, where_ref, *refs):
    blocks, refs = refs[:given], refs[given:]
    weight, refs = refs[0], refs[1:]
    if not first:
        sum_in, refs = refs[0], refs[1:]
    if last:
        inv, local_ids, out, wide, top, total, picked = refs
    else:
        out, wide = refs
    n = pl.program_id(0)

    @pl.when(n == 0)
    def _():
        place(where_ref, blocks, wide)

    value = resident_product(where_ref, wide, weight, n, tile)
    at = pl.ds(pl.multiple_of(n * tile, 128), tile)
    if not first:
        value = value + sum_in[:, at]
    if not last:
        out[:, at] = value
        return
    rows = value.shape[0]
    same = lax.broadcasted_iota(jnp.int32, (rows, rows), 0) == lax.broadcasted_iota(
        jnp.int32, (rows, rows), 1
    )
    squares = jnp.sum(jnp.where(same, inv[...], 0.0), axis=1, keepdims=True)
    logits = value * (1.0 / jnp.sqrt(squares / D + epsilon))
    column = n * tile + lax.broadcasted_iota(jnp.int32, logits.shape, 1)
    tile_pick = jnp.sum(jnp.where(column == local_ids[...], logits, 0.0), axis=1, keepdims=True)
    tile_top = jnp.max(logits, axis=1, keepdims=True)

    @pl.when(n == 0)
    def _():
        top[...] = tile_top
        total[...] = jnp.sum(jnp.exp(logits - tile_top), axis=1, keepdims=True)
        picked[...] = tile_pick

    @pl.when(n > 0)
    def _():
        new_top = jnp.maximum(top[...], tile_top)
        total[...] = total[...] * jnp.exp(top[...] - new_top) + jnp.sum(
            jnp.exp(logits - new_top), axis=1, keepdims=True
        )
        top[...] = new_top
        picked[...] = picked[...] + tile_pick

    @pl.when(n == pl.num_programs(0) - 1)
    def _():
        lane = lax.broadcasted_iota(jnp.int32, out.shape, 1)
        out[...] = jnp.where(lane == 0, top[...], jnp.where(lane == 1, total[...], picked[...]))


def vocab_part(where, blocks, rows, lm_head, sums, inv, local_ids):
    cols = blocks[0].shape[1]
    count = blocks[0].shape[0] // rows
    inner, width = lm_head.shape
    tile = 512 if rows <= 352 else 256
    first, last = sums is None, inv is not None
    lm_head = pltpu.with_memory_space_constraint(lm_head, pltpu.VMEM)
    ins = [where, *blocks, lm_head]
    specs = whole_specs(blocks) + [VMEM]
    aliases = {}
    if not first:
        if not last:
            aliases = {len(ins): 0}
        ins.append(pltpu.with_memory_space_constraint(sums, pltpu.VMEM))
        specs.append(VMEM)
    scratch = [pltpu.VMEM((rows, 4 * count * cols), BF)]
    if last:
        ins += [inv, local_ids]
        specs += whole_specs([inv, local_ids])
        outs = jax.ShapeDtypeStruct((rows, 128), F32)
        out_specs = pl.BlockSpec((rows, 128), lambda n, w: (0, 0))
        scratch += [pltpu.VMEM((rows, 1), F32)] * 3
    else:
        outs, out_specs = pltpu.VMEM((rows, width), F32), VMEM
    return pl.pallas_call(
        functools.partial(vocab_kernel, len(blocks), count, first, last, tile),
        out_shape=outs,
        grid_spec=pltpu.PrefetchScalarGridSpec(
            num_scalar_prefetch=1,
            grid=(width // tile,),
            in_specs=specs,
            out_specs=out_specs,
            scratch_shapes=scratch,
        ),
        input_output_aliases=aliases,
        compiler_params=params(32),
        cost_estimate=cost(rows, 8 if first else inner * count // 4, width, 0),
    )(*ins)


def spread(by_offset, squares, load, part):
    own0 = by_offset[0]
    a1 = send(by_offset[1], plane_pairs(1))
    a3 = send(by_offset[3], plane_pairs(3))
    row0 = send(own0, xor_pairs(2))
    core0 = send(own0, xor_pairs(1))
    diagonal0 = send(own0, xor_pairs(3))
    weight, token = load(own0)

    near = jnp.concatenate([a1, a3], axis=0)
    row0, core0, diagonal0, near, squares, far, token = lax.optimization_barrier(
        (row0, core0, diagonal0, near, squares, by_offset[2], token)
    )
    a2 = send(far, plane_pairs(2))
    row13 = send(near, xor_pairs(2))
    squares = squares + token[:1, :1]
    more = [send(squares, xor_pairs(mask)) for mask in (1, 2, 3)]
    sums = part(0, weight, (own0, row0, core0, diagonal0), None, None)

    a2, row13, squares, more, sums = lax.optimization_barrier((a2, row13, squares, more, sums))
    row2 = send(a2, xor_pairs(2))
    core13 = send(jnp.concatenate([near, row13], axis=0), xor_pairs(1))
    squares = squares + more[0] + (more[1] + more[2])
    more = [send(squares, plane_pairs(k)) for k in (1, 2, 3)]
    sums = part(1, weight, (near, row13, core13), sums, None)

    row2, squares, more, sums = lax.optimization_barrier((row2, squares, more, sums))
    squares = squares + more[0] + (more[1] + more[2])
    core2 = send(jnp.concatenate([a2, row2], axis=0), xor_pairs(1))
    return part(2, weight, (a2, row2, core2), sums, squares)


def live_part(
    x,
    norm_gain,
    final_gain,
    w_gate,
    w_up,
    w_down,
    lm_head,
    target_ids,
    slot_rows,
    gate_row,
    in_squares,
    where,
    down_at,
    first_id,
    live_rows,
    slots,
):
    cols = x.shape[1]
    *picked_rows, x_live = dispatch(slot_rows, x, norm_gain, slots, live_rows)
    packed = slot_rows[4]
    live_at = packed[None, :] == jnp.arange(live_rows, dtype=jnp.int32)[:, None]
    slot_live = jnp.stack(
        [
            jnp.sum(jnp.where(live_at, slot_rows[(4 - k) % 4][None, :] + 1, 0), axis=1) - 1
            for k in range(4)
        ],
        axis=1,
    )
    local_ids = (
        jnp.sum(jnp.where(live_at, target_ids[None, :], 0), axis=1, keepdims=True) - first_id
    )

    def hidden_step(group, weight, blocks, sums, squares):
        rows_of = None if squares is None else [slot_rows, squares]
        return hidden_part(where[group], blocks, slots, weight, w_up, sums, rows_of)

    hidden = spread(
        picked_rows, in_squares, functools.partial(resident, w_gate), hidden_step
    )

    pieces = down_all(down_at, hidden, w_down, slot_rows, gate_row, cols)
    heard = [send(core, xor_pairs(1)) for core in pieces[2::3]]
    totals, crossed = [], None
    for own, across, both in zip(pieces[0::3], pieces[1::3], heard):
        rows = own.shape[0]
        across = (across + both[rows:].astype(F32)).astype(BF)
        if crossed is not None:
            across = after(across, crossed)
        crossed = send(across, xor_pairs(2))
        totals.append((own + both[:rows].astype(F32) + crossed.astype(F32)).astype(BF))
    part2 = send(totals[0], plane_pairs(2))
    part1 = send(totals[1][:slots], plane_pairs(1))
    part3 = send(totals[1][slots:], plane_pairs(3))
    parts = (totals[2], part2, part1, part3)

    scaled, squares = mix(slot_live, x_live, final_gain, parts)

    def vocab_step(group, weight, blocks, sums, squares):
        return vocab_part(where[group], blocks, live_rows, weight, sums, squares, local_ids)

    squares = squares.reshape(1, -1)
    stats = spread([scaled] * 4, squares, lambda own: resident(lm_head, squares), vocab_step)
    spot = packed[:, None] == jnp.arange(live_rows, dtype=jnp.int32)[None, :]
    return jnp.stack(
        [jnp.sum(jnp.where(spot, stats[:, j][None, :], 0.0), axis=1) for j in range(3)]
    )


def fast_body(
    residual_in,
    norm_gain,
    final_gain,
    expert_ids,
    gate_values,
    w_gate,
    w_up,
    w_down,
    lm_head,
    target_ids,
    lengths,
):
    tokens = residual_in.shape[0]
    devices = lax.axis_size("tensor")
    me = lax.axis_index("tensor").astype(jnp.int32)
    plane, row, core = me >> 2, (me >> 1) & 1, me & 1
    slot_rows, gate_row, need = route(plane, lengths, expert_ids.T, gate_values.T)
    need = jnp.maximum(need, lax.ppermute(need, "groups", [(0, 1), (1, 0)]))

    at = [row * 2 + core, (1 - row) * 2 + core, row * 2 + 1 - core, (1 - row) * 2 + 1 - core]
    planes = [(plane + k) & 3 for k in range(4)]
    where = [jnp.stack(at + [planes[(4 - k) % 4] for k in group]) for group in CHUNKS]
    down_at = jnp.stack(at + [planes[k] for k in (2, 1, 3, 0)])
    stream = residual_in.astype(F32)
    in_squares = jnp.sum(stream * stream, axis=1)[None, :]

    stats = lax.switch(
        need[0, 0].astype(jnp.int32),
        [
            functools.partial(live_part, live_rows=rows, slots=slots)
            for rows, slots in TIERS + ((tokens, CAP),)
        ],
        residual_in,
        norm_gain[None, :],
        final_gain[None, :],
        w_gate,
        w_up,
        w_down,
        lm_head,
        target_ids,
        slot_rows,
        gate_row,
        in_squares,
        where,
        down_at,
        me * lm_head.shape[1],
    )
    rows_dev = tokens // devices
    stats = stats.reshape(3, devices, rows_dev).transpose(1, 0, 2)
    stats = lax.all_to_all(stats, "tensor", 0, 0, tiled=True)
    top = jnp.max(stats[:, 0], axis=0)
    total = jnp.sum(stats[:, 1] * jnp.exp(stats[:, 0] - top[None, :]), axis=0)
    logprob = jnp.sum(stats[:, 2], axis=0) - top - jnp.log(total)
    own_live = lax.dynamic_slice_in_dim(slot_rows[4], me * rows_dev, rows_dev) >= 0
    return jnp.where(own_live, logprob, 0.0)


def body(*args):
    if lax.axis_size("tensor") == 16 and lax.axis_size("groups") == 2:
        return fast_body(*args)
    return plain_body(*args)


def solution(mesh):
    return jax.shard_map(
        body,
        mesh=mesh,
        in_specs=(
            P("groups", "tensor"),
            P("tensor"),
            P("tensor"),
            P("groups", None),
            P("groups", None),
            P(None, "tensor"),
            P(None, "tensor"),
            P("tensor", None),
            P(None, "tensor"),
            P("groups"),
            P("groups"),
        ),
        out_specs=P(("groups", "tensor")),
        check_vma=False,
    )
```
